256 devices in a mesh: seq: 32 (over y, x, core), tensor: 8 (over z).
Axes of the slice: x: 4, y: 4, z: 8, core: 2. Of those that a mesh axis runs over, the one named last changes fastest.
Arguments:
- hidden: bfloat16 [8192, 3072], P('seq'), may hold values from -6 to 6
- attention_norm_gain: bfloat16 [3072], replicated, may hold values from 0.099609375 to 1.8984375
- query_key_value_weight: bfloat16 [3, 3072, 3072], P(None, None, 'tensor'), may hold values from -0.109375 to 0.109375
- output_weight: bfloat16 [3072, 3072], P('tensor'), may hold values from -0.3125 to 0.3125
- adapter_down_weight: bfloat16 [3072, 16], P('tensor'), may hold values from -0.3125 to 0.3125
- adapter_up_weight: bfloat16 [16, 3072], replicated, may hold values from -1.5 to 1.5
- final_norm_gain: bfloat16 [3072], replicated, may hold values from 0.099609375 to 1.8984375
- head: bfloat16 [16384, 3072], P('tensor', 'seq')
- prompt_key_slots: bfloat16 [64, 128, 3072], P('seq', None, 'tensor')
- prompt_value_slots: bfloat16 [64, 128, 3072], P('seq', None, 'tensor'), may hold values from -6 to 6
- counts: int32 [8], replicated, may hold values from 1 to 8, as said below
- page_slot_index: int32 [64], replicated, may hold values from 0 to 63, each once
- owner: int32 [128], replicated, may hold values from 0 to 7, as said below
- targets: int32 [8192], P('seq'), may hold values from 0 to 16383
Outputs:
- logprob_policy: float32 [8192], P('seq')
- logprob_reference: float32 [8192], P('seq')
The draws below stay inside these ranges and needn't reach their ends.
Inputs may be any that keep to these rules, and one draw needn't show every extreme that they name: `counts`: every prompt fills 1 to 8 pages, and some prompt fills exactly 8. `page_slot_index`: slot s is held by index s // 2 of seq; every slot is named once. `owner`: every prompt owns exactly 16 rollouts, placed anywhere.
All inputs are finite; a program needn't handle non-finite values.
Results may differ from the reference program's by a relative error of at most 0.014.
The reference program's roundings to bfloat16 on the way count: a program that leaves them out, or rounds other values in their place, can miss the bound.
Values may be sent and summed in bfloat16 or wider, within the bound.
No kernel may reach another device: no remote copies, remote signals or barrier semaphores. Data moves between devices by JAX's collectives and lax.ppermute only.
A program may use at most 192 MiB of HBM per device.

```python
import math
import jax
import jax.numpy as jnp
import numpy as np
from jax import lax

MODEL_WIDTH = 3072
HEAD_COUNT = 32
HEAD_WIDTH = 96
V = 16384
ADAPTER_RANK = 16
LEN = 64
PAGE = 128
MAXP = 8
GROUP = 16
ROLLOUTS = 128
TOKENS = 8192
GROUPS = 8
SLOTS = 64


def draw_head(key, part):
    first = jax.random.fold_in(key, 0)
    scale = 3.0 / math.sqrt(MODEL_WIDTH)
    basic = jax.random.normal(first, (V, MODEL_WIDTH), jnp.float32)
    return (basic * scale).astype(jnp.bfloat16)


def draw_prompt_key_slots(key, part):
    first = jax.random.fold_in(key, 0)
    return jax.random.normal(first, (SLOTS, PAGE, HEAD_COUNT * HEAD_WIDTH), jnp.float32).astype(jnp.bfloat16)


def draw_counts(key, part):
    first, second = jax.random.split(key)
    basic = MAXP // jax.random.randint(first, (GROUPS,), 1, MAXP + 1)
    chosen = jax.random.randint(second, (), 0, GROUPS)
    return jnp.where(jnp.arange(GROUPS) == chosen, MAXP, basic).astype(jnp.int32)


def draw_owner(key, part):
    return (jax.random.permutation(key, ROLLOUTS) // GROUP).astype(jnp.int32)


def place_ends(result, stream_key, smallest, largest):
    dims = result.shape
    index_at = [jax.random.randint(jax.random.fold_in(stream_key, axis), (), 0, dims[axis]) for axis in range(len(dims))]
    result = result.at[tuple(index_at)].set(smallest)
    longest = dims.index(max(dims))
    index_at[longest] = (index_at[longest] + 1) % dims[longest]
    return result.at[tuple(index_at)].set(largest)


def shard_levels(rng, dims, cuts, least, largest):
    level, own = 1.0, jax.random.fold_in(rng, 6)
    for dim, parts in cuts:
        steps = jnp.exp(jax.random.uniform(jax.random.fold_in(own, dim), (parts,), jnp.float32, least / len(cuts), largest / len(cuts)))
        level = level * jnp.repeat(steps, dims[dim] // parts).reshape([-1 if axis == dim else 1 for axis in range(len(dims))])
    return level


def rank_bounds(number_of, skew):
    loads = [(1 << 20) // math.isqrt(grade ** skew) + 1 for grade in range(1, number_of + 1)]
    width = 1 + sum(loads) // (1 << 30)
    return np.cumsum(np.array([max(1, weight // width) for weight in loads]))


def skewed_ids(rng, shape, count, skew):
    grid = rank_bounds(count, skew)
    ticket = jax.random.randint(jax.random.fold_in(rng, 1), shape, 0, int(grid[count - 1]))
    standing = jnp.searchsorted(jnp.asarray(grid, jnp.int32), ticket, side="right")
    return jax.random.permutation(jax.random.fold_in(rng, 2), count)[standing].astype(jnp.int32)


def bell_draw(stream_key, extent, scale, most, shards=(), held_as=jnp.bfloat16):
    array = jax.random.normal(stream_key, extent, jnp.float32) * scale
    if len(shards) > 0:
        array = shard_levels(stream_key, extent, shards, -0.22, 0.18) * array
    return jnp.clip(array, min=-most, max=most).astype(held_as)


def setup_inputs(seed: int = 0) -> dict:
    key_list = jax.random.split(jax.random.key(seed), 15)
    return {
        "hidden": bell_draw(key_list[0], (TOKENS, MODEL_WIDTH), 1.0, 6.0, ((0, 32),)),
        "attention_norm_gain": jnp.clip(1.0 + 0.18 * jax.random.normal(key_list[1], (MODEL_WIDTH,), jnp.float32), 0.099609375, 1.8984375).astype(jnp.bfloat16),
        "query_key_value_weight": bell_draw(key_list[2], (3, MODEL_WIDTH, HEAD_COUNT * HEAD_WIDTH), MODEL_WIDTH ** -0.5, 0.109375, ((2, 8),)),
        "output_weight": bell_draw(key_list[3], (HEAD_COUNT * HEAD_WIDTH, MODEL_WIDTH), (HEAD_COUNT * HEAD_WIDTH // 8) ** -0.5, 0.3125, ((0, 8),)),
        "adapter_down_weight": bell_draw(key_list[4], (HEAD_COUNT * HEAD_WIDTH, ADAPTER_RANK), (HEAD_COUNT * HEAD_WIDTH // 8) ** -0.5, 0.3125, ((0, 8),)),
        "adapter_up_weight": bell_draw(key_list[5], (ADAPTER_RANK, MODEL_WIDTH), ADAPTER_RANK ** -0.5, 1.5),
        "final_norm_gain": jnp.clip(1.0 + 0.18 * jax.random.normal(key_list[6], (MODEL_WIDTH,), jnp.float32), 0.099609375, 1.8984375).astype(jnp.bfloat16),
        "head": draw_head(jax.random.fold_in(key_list[14], 71), 0),
        "prompt_key_slots": draw_prompt_key_slots(jax.random.fold_in(key_list[14], 71), 0),
        "prompt_value_slots": bell_draw(key_list[9], (SLOTS, PAGE, HEAD_COUNT * HEAD_WIDTH), 1.0, 6.0, ((0, 32), (2, 8))),
        "counts": draw_counts(jax.random.fold_in(key_list[14], 71), 0),
        "page_slot_index": jax.random.permutation(key_list[11], SLOTS).astype(jnp.int32),
        "owner": draw_owner(jax.random.fold_in(key_list[14], 71), 0),
        "targets": place_ends(skewed_ids(key_list[13], (TOKENS,), V, 2), jax.random.fold_in(key_list[13], 3), 0, V - 1).astype(jnp.int32),
    }


EPSILON = 1e-05
NEGATIVE = -1e+30

def rms_norm(values, gain):
    mean_sq = lax.optimization_barrier(jnp.mean(values * values, axis=-1, keepdims=True))
    return (values * lax.rsqrt(mean_sq + EPSILON) * gain.astype(jnp.float32)).astype(jnp.bfloat16)

def rotate(values, positions):
    half_width = values.shape[-1] // 2
    frequency = 10000.0 ** (-jnp.arange(half_width, dtype=jnp.float32) * 2.0 / values.shape[-1])
    angles = positions.astype(jnp.float32)[:, None] * frequency[None, :]
    cosine = jnp.cos(angles)[:, None, :]
    sinus = jnp.sin(angles)[:, None, :]
    first = values[..., :half_width]
    second = values[..., half_width:]
    return jnp.concatenate([first * cosine - second * sinus, second * cosine + first * sinus], axis=-1)

def reference(hidden, attention_norm_gain, query_key_value_weight, output_weight, adapter_down_weight, adapter_up_weight, final_norm_gain, head, prompt_key_slots, prompt_value_slots, counts, page_slot_index, owner, targets):
    stream = hidden.astype(jnp.float32)
    normed = rms_norm(stream, attention_norm_gain)
    token_ids = jnp.arange(TOKENS, dtype=jnp.int32)
    group_of = owner[token_ids // LEN]
    positions = counts[group_of] * PAGE + token_ids % LEN
    queries = rotate(jnp.dot(normed, query_key_value_weight[0], preferred_element_type=jnp.float32).reshape(TOKENS, HEAD_COUNT, HEAD_WIDTH), positions).astype(jnp.bfloat16)
    keys_new = rotate(jnp.dot(normed, query_key_value_weight[1], preferred_element_type=jnp.float32).reshape(TOKENS, HEAD_COUNT, HEAD_WIDTH), positions).astype(jnp.bfloat16)
    values_new = jnp.dot(normed, query_key_value_weight[2], preferred_element_type=jnp.float32).astype(jnp.bfloat16).reshape(TOKENS, HEAD_COUNT, HEAD_WIDTH)
    score_scale = 1.0 / math.sqrt(HEAD_WIDTH)
    keys_cached = prompt_key_slots.reshape(SLOTS, PAGE, HEAD_COUNT, HEAD_WIDTH)
    values_cached = prompt_value_slots.reshape(SLOTS, PAGE, HEAD_COUNT, HEAD_WIDTH)

    def attend(rollout):
        group_id = owner[rollout]
        rollout_query = lax.dynamic_slice_in_dim(queries, rollout * LEN, LEN, 0)
        rollout_key = lax.dynamic_slice_in_dim(keys_new, rollout * LEN, LEN, 0)
        rollout_value = lax.dynamic_slice_in_dim(values_new, rollout * LEN, LEN, 0)
        slot_ids = lax.dynamic_slice_in_dim(page_slot_index, group_id * MAXP, MAXP, 0)
        cache_k = keys_cached[slot_ids].reshape(MAXP * PAGE, HEAD_COUNT, HEAD_WIDTH)
        cache_v = values_cached[slot_ids].reshape(MAXP * PAGE, HEAD_COUNT, HEAD_WIDTH)
        every_key = jnp.concatenate([cache_k, rollout_key], axis=0)
        every_value = jnp.concatenate([cache_v, rollout_value], axis=0)
        is_live = jnp.arange(MAXP * PAGE, dtype=jnp.int32) // PAGE < counts[group_id]
        causal = jnp.arange(LEN, dtype=jnp.int32)[None, :] <= jnp.arange(LEN, dtype=jnp.int32)[:, None]
        visible = jnp.concatenate([jnp.broadcast_to(is_live[None, :], (LEN, MAXP * PAGE)), causal], axis=1)
        scores = jnp.einsum('thd,khd->htk', rollout_query.astype(jnp.float32), every_key.astype(jnp.float32)) * score_scale
        maxima = lax.optimization_barrier(jnp.max(jnp.where(visible[None], scores, NEGATIVE), axis=-1, keepdims=True))
        weights = jnp.where(visible[None], jnp.exp(scores - maxima), 0.0)
        totals = lax.optimization_barrier(jnp.sum(weights, axis=-1))
        rounded = lax.optimization_barrier(weights.astype(jnp.bfloat16)).astype(jnp.float32)
        mixture = jnp.einsum('htk,khd->thd', rounded, every_value.astype(jnp.float32))
        return (mixture / totals.T[:, :, None]).astype(jnp.bfloat16).reshape(LEN, HEAD_COUNT * HEAD_WIDTH)
    attention_output = lax.map(attend, jnp.arange(ROLLOUTS, dtype=jnp.int32)).reshape(TOKENS, HEAD_COUNT * HEAD_WIDTH)
    branch = jnp.dot(attention_output, output_weight, preferred_element_type=jnp.float32)
    adapter_delta = jnp.dot(attention_output, adapter_down_weight, preferred_element_type=jnp.float32)
    reference_hidden = stream + branch
    policy_hidden = reference_hidden + jnp.dot(adapter_delta, adapter_up_weight.astype(jnp.float32), precision=lax.Precision.HIGHEST)
    normed_ref = rms_norm(reference_hidden, final_norm_gain)
    normed_pol = rms_norm(policy_hidden, final_norm_gain)
    block_size = math.gcd(TOKENS, 512)

    def score_block(block_id):
        block_ids = lax.dynamic_slice_in_dim(targets, block_id * block_size, block_size, 0)
        results = []
        for normed_rows in (normed_pol, normed_ref):
            block_rows = lax.dynamic_slice_in_dim(normed_rows, block_id * block_size, block_size, 0)
            logits = jnp.dot(block_rows, head.T, preferred_element_type=jnp.float32)
            maxima = lax.optimization_barrier(jnp.max(logits, axis=1))
            log_total = maxima + jnp.log(lax.optimization_barrier(jnp.sum(jnp.exp(logits - maxima[:, None]), axis=1)))
            picked = jnp.take_along_axis(logits, block_ids[:, None], axis=1)[:, 0]
            results.append(picked - log_total)
        return jnp.stack(results)
    scored = lax.map(score_block, jnp.arange(TOKENS // block_size, dtype=jnp.int32))
    scored = jnp.transpose(scored, (1, 0, 2)).reshape(2, TOKENS)
    return (scored[0], scored[1])
```

```python
import math

import jax
import jax.numpy as jnp
from jax import lax
from jax.experimental import pallas as pl
from jax.experimental.pallas import tpu as pltpu
from jax.sharding import PartitionSpec as P

HEAD_WIDTH = 96
LEN = 64
PAGE = 128
MAXP = 8


EPSILON = 1e-05
NEGATIVE = -1e30
PAD = 128
VMEM_LIMIT = 56 * 1024 * 1024
F32 = jnp.float32
BF16 = jnp.bfloat16


def rms_norm(values, gain):
    mean_sq = jnp.mean(values * values, axis=-1, keepdims=True)
    return (values * lax.rsqrt(mean_sq + EPSILON) * gain.astype(F32)).astype(BF16)


def project_kernel(hidden_ref, gain_ref, weight_ref, cos_ref, sin_ref, out_ref, normed):
    part = pl.program_id(0)

    @pl.when(part == 0)
    def _():
        normed[...] = rms_norm(hidden_ref[...].astype(F32), gain_ref[...])

    product = jnp.dot(normed[...], weight_ref[0], preferred_element_type=F32)

    @pl.when(part < 2)
    def _():
        width = product.shape[1]
        half = HEAD_WIDTH // 2
        lane = lax.broadcasted_iota(jnp.int32, product.shape, 1) % HEAD_WIDTH
        partner = jnp.where(
            lane < half, -pltpu.roll(product, width - half, 1), pltpu.roll(product, half, 1)
        )
        out_ref[0] = (product * cos_ref[...] + partner * sin_ref[...]).astype(BF16)

    @pl.when(part == 2)
    def _():
        out_ref[0] = product.astype(BF16)


def project(hidden, gain, weight, cosine, sinus):
    rows, width = hidden.shape
    parts, _, cols = weight.shape
    whole = lambda i: (0, 0)
    return pl.pallas_call(
        project_kernel,
        grid=(parts,),
        in_specs=[
            pl.BlockSpec((rows, width), whole),
            pl.BlockSpec((1, width), whole),
            pl.BlockSpec((1, width, cols), lambda i: (i, 0, 0)),
            pl.BlockSpec((rows, cols), whole),
            pl.BlockSpec((rows, cols), whole),
        ],
        out_specs=pl.BlockSpec((1, rows, cols), lambda i: (i, 0, 0)),
        out_shape=jax.ShapeDtypeStruct((parts, rows, cols), BF16),
        scratch_shapes=[pltpu.VMEM((rows, width), BF16)],
        compiler_params=pltpu.CompilerParams(vmem_limit_bytes=VMEM_LIMIT),
        name="project",
    )(hidden, gain, weight, cosine, sinus)


def dot_nt(left, right):
    return lax.dot_general(left, right, (((1,), (1,)), ((), ())), preferred_element_type=F32)


def attend_kernel(
    first_ref,
    counts_ref,
    index_ref,
    owner_ref,
    qkv_ref,
    cache_ref,
    out_weight_ref,
    down_ref,
    out_ref,
    keys,
    values,
    attended,
    sems,
):
    rollouts = keys.shape[0]
    width = qkv_ref.shape[2]
    heads = width // HEAD_WIDTH
    scale = 1.0 / math.sqrt(HEAD_WIDTH)

    def copies(r, j):
        group = owner_ref[first_ref[0] + r]
        slot = index_ref[group * MAXP + j]
        rows = pl.ds(j * PAGE, PAGE)
        source = cache_ref.at[slot // 2]
        return (
            pltpu.make_async_copy(source.at[slot % 2], keys.at[r, rows], sems.at[r, 0, j]),
            pltpu.make_async_copy(source.at[2 + slot % 2], values.at[r, rows], sems.at[r, 1, j]),
        )

    for r in range(rollouts):
        for j in range(MAXP):
            for copy in copies(r, j):
                copy.start()
    lane_head = lax.broadcasted_iota(jnp.int32, (LEN, width), 1) // HEAD_WIDTH
    own_row = lax.broadcasted_iota(jnp.int32, (heads * LEN, LEN), 0) % LEN
    own_col = lax.broadcasted_iota(jnp.int32, (heads * LEN, LEN), 1)
    page_of = lax.broadcasted_iota(jnp.int32, (heads * LEN, MAXP * PAGE), 1) // PAGE
    for r in range(rollouts):
        rows = slice(r * LEN, (r + 1) * LEN)
        query = qkv_ref[0, rows, :].astype(F32)
        stacked = jnp.concatenate(
            [jnp.where(lane_head == h, query, 0.0) for h in range(heads)], axis=0
        ).astype(BF16)
        own = dot_nt(stacked, qkv_ref[1, rows, :]) * scale
        own = jnp.where(own_col <= own_row, own, NEGATIVE)
        for j in range(MAXP):
            for copy in copies(r, j):
                copy.wait()
        live = counts_ref[owner_ref[first_ref[0] + r]]
        cached = dot_nt(stacked, keys[r]) * scale
        cached = jnp.where(page_of < live, cached, NEGATIVE)
        largest = jnp.maximum(
            jnp.max(own, axis=1, keepdims=True), jnp.max(cached, axis=1, keepdims=True)
        )
        own = jnp.exp(own - largest)
        cached = jnp.exp(cached - largest)
        total = jnp.sum(own, axis=1, keepdims=True) + jnp.sum(cached, axis=1, keepdims=True)
        mixed = jnp.dot(cached.astype(BF16), values[r], preferred_element_type=F32) + jnp.dot(
            own.astype(BF16), qkv_ref[2, rows, :], preferred_element_type=F32
        )
        mixed = mixed / total
        picked = jnp.zeros((LEN, width), F32)
        for h in range(heads):
            picked = jnp.where(lane_head == h, mixed[h * LEN : (h + 1) * LEN], picked)
        attended[rows, :] = picked.astype(BF16)
    model = out_weight_ref.shape[1]
    out_ref[:, :model] = jnp.dot(
        attended[...], out_weight_ref[...], preferred_element_type=F32
    ).astype(BF16)
    out_ref[:, model:] = jnp.dot(
        attended[...], down_ref[...], preferred_element_type=F32
    ).astype(BF16)


def attend(first, counts, index, owner, qkv, cache, out_weight, down):
    _, rows, width = qkv.shape
    rollouts = rows // LEN
    model = out_weight.shape[1]
    vmem = pl.BlockSpec(memory_space=pltpu.VMEM)
    return pl.pallas_call(
        attend_kernel,
        grid_spec=pltpu.PrefetchScalarGridSpec(
            num_scalar_prefetch=4,
            grid=(),
            in_specs=[vmem, pl.BlockSpec(memory_space=pl.ANY), vmem, vmem],
            out_specs=vmem,
            scratch_shapes=[
                pltpu.VMEM((rollouts, MAXP * PAGE, width), BF16),
                pltpu.VMEM((rollouts, MAXP * PAGE, width), BF16),
                pltpu.VMEM((rows, width), BF16),
                pltpu.SemaphoreType.DMA((rollouts, 2, MAXP)),
            ],
        ),
        out_shape=jax.ShapeDtypeStruct((rows, model + PAD), BF16),
        compiler_params=pltpu.CompilerParams(vmem_limit_bytes=VMEM_LIMIT),
        name="attend",
    )(first, counts, index, owner, qkv, cache, out_weight, down)


def score_kernel(*refs):
    place_ref, hidden_ref, up_ref, gain_ref, target_ref, head_ref = refs[:6]
    out_ref, normed, largest, total, picked = refs[-5:]
    blocks = refs[6:-5]
    step = pl.program_id(0)
    ranks = len(blocks)
    model = hidden_ref.shape[1]
    rows = hidden_ref.shape[0]
    size = rows // ranks

    @pl.when(step == 0)
    def _():
        for k, block in enumerate(blocks):
            at = pl.ds(pl.multiple_of(place_ref[1 + k] * size, size), size)
            reference = hidden_ref[at, :].astype(F32) + block[:, :model].astype(F32)
            policy = reference + jnp.dot(
                block[:, model:], up_ref[...], preferred_element_type=F32
            )
            normed[0, at, :] = rms_norm(policy, gain_ref[...])
            normed[1, at, :] = rms_norm(reference, gain_ref[...])
        largest[...] = jnp.full_like(largest, NEGATIVE)
        total[...] = jnp.zeros_like(total)
        picked[...] = jnp.zeros_like(picked)

    logits = jnp.dot(
        normed[...].reshape(2 * rows, model), head_ref[...], preferred_element_type=F32
    )
    columns = lax.broadcasted_iota(jnp.int32, logits.shape, 1)
    wanted = target_ref[...] - (place_ref[0] * pl.num_programs(0) + step) * logits.shape[1]
    picked[...] += jnp.sum(jnp.where(columns == wanted, logits, 0.0), axis=1, keepdims=True)
    before = largest[...]
    after = jnp.maximum(before, jnp.max(logits, axis=1, keepdims=True))
    total[...] = total[...] * jnp.exp(before - after) + jnp.sum(
        jnp.exp(logits - after), axis=1, keepdims=True
    )
    largest[...] = after

    @pl.when(step == pl.num_programs(0) - 1)
    def _():
        lane = lax.broadcasted_iota(jnp.int32, (2 * rows, 128), 1)
        packed = jnp.where(
            lane == 0, largest[...], jnp.where(lane == 1, total[...], picked[...])
        )
        out_ref[...] = jnp.transpose(packed)[:8, :]


def score(place, hidden, up, gain, targets, head, blocks):
    rows, model = hidden.shape
    vocab = head.shape[1]
    tile = 512
    whole = lambda i, p: (0, 0)
    return pl.pallas_call(
        score_kernel,
        grid_spec=pltpu.PrefetchScalarGridSpec(
            num_scalar_prefetch=1,
            grid=(vocab // tile,),
            in_specs=[
                pl.BlockSpec(hidden.shape, whole),
                pl.BlockSpec(up.shape, whole),
                pl.BlockSpec(gain.shape, whole),
                pl.BlockSpec(targets.shape, whole),
                pl.BlockSpec((model, tile), lambda i, p: (0, i)),
            ]
            + [pl.BlockSpec(block.shape, whole) for block in blocks],
            out_specs=pl.BlockSpec((8, 2 * rows), whole),
            scratch_shapes=[
                pltpu.VMEM((2, rows, model), BF16),
                pltpu.VMEM((2 * rows, 1), F32),
                pltpu.VMEM((2 * rows, 1), F32),
                pltpu.VMEM((2 * rows, 1), F32),
            ],
        ),
        out_shape=jax.ShapeDtypeStruct((8, 2 * rows), F32),
        compiler_params=pltpu.CompilerParams(vmem_limit_bytes=VMEM_LIMIT),
        name="score",
    )(place, hidden, up, gain, targets, head, *blocks)


def shifted(value, ranks, step):
    return lax.ppermute(value, "tensor", [(i, (i + step) % ranks) for i in range(ranks)])


def ring_sum(branch, ranks):
    me = lax.axis_index("tensor")
    size = branch.shape[0] // ranks

    def mine(rank):
        return lax.dynamic_slice_in_dim(branch, (rank % ranks) * size, size, 0)

    half = ranks // 2
    left = mine(me + ranks - half)
    right = None
    for step in range(1, half + 1):
        arrived_left = shifted(left, ranks, -1)
        arrived_right = None if right is None else shifted(right, ranks, 1)
        if step == half:
            total = (
                mine(me).astype(F32) + arrived_left.astype(F32) + arrived_right.astype(F32)
            )
            return total.astype(BF16)
        left = (mine(me + ranks - half + step).astype(F32) + arrived_left.astype(F32)).astype(BF16)
        own = mine(me + half - step).astype(F32)
        if arrived_right is not None:
            own = own + arrived_right.astype(F32)
        right = own.astype(BF16)


def ring_gather(block, ranks):
    me = lax.axis_index("tensor")
    blocks, places = [block], [me]
    from_right = from_left = block
    for step in range(1, ranks // 2 + 1):
        from_right = shifted(from_right, ranks, -1)
        blocks.append(from_right)
        places.append((me + step) % ranks)
        if step < ranks // 2:
            from_left = shifted(from_left, ranks, 1)
            blocks.append(from_left)
            places.append((me + ranks - step) % ranks)
    return blocks, places


def local(
    hidden,
    attention_norm_gain,
    query_key_value_weight,
    output_weight,
    adapter_down_weight,
    adapter_up_weight,
    final_norm_gain,
    head,
    prompt_key_slots,
    prompt_value_slots,
    counts,
    page_slot_index,
    owner,
    targets,
):
    tok_rows, model = hidden.shape
    rollouts_here = tok_rows // LEN
    width_here = output_weight.shape[0]
    heads_here = width_here // HEAD_WIDTH
    ranks = lax.axis_size("tensor")
    first = lax.axis_index("seq") * rollouts_here
    cache = lax.all_gather(
        jnp.concatenate([prompt_key_slots, prompt_value_slots], axis=0)[None],
        "seq",
        axis=0,
        tiled=True,
    )
    head_columns = lax.all_gather(head.T, "seq", axis=0, tiled=True)

    groups_iota = jnp.arange(counts.shape[0], dtype=jnp.int32)
    my_groups = lax.dynamic_slice_in_dim(owner, first, rollouts_here, 0)
    my_pages = jnp.sum(
        jnp.where(my_groups[:, None] == groups_iota[None, :], counts[None, :], 0), axis=1
    )
    positions = jnp.repeat(my_pages, LEN) * PAGE + jnp.arange(tok_rows, dtype=jnp.int32) % LEN
    half = HEAD_WIDTH // 2
    place_in_head = jnp.arange(width_here, dtype=jnp.int32) % half
    frequency = 10000.0 ** (-place_in_head.astype(F32) * 2.0 / HEAD_WIDTH)
    angles = positions.astype(F32)[:, None] * frequency[None, :]
    qkv = project(
        hidden,
        attention_norm_gain[None, :],
        query_key_value_weight,
        jnp.cos(angles),
        jnp.sin(angles),
    )
    rank_pad = PAD - adapter_down_weight.shape[1]
    branch = attend(
        first[None].astype(jnp.int32),
        counts,
        page_slot_index,
        owner,
        qkv,
        cache,
        output_weight,
        jnp.pad(adapter_down_weight, ((0, 0), (0, rank_pad))),
    )
    blocks, places = ring_gather(ring_sum(branch, ranks), ranks)
    place = jnp.stack([lax.axis_index("tensor")] + places).astype(jnp.int32)
    stats = score(
        place,
        hidden,
        jnp.pad(adapter_up_weight, ((0, rank_pad), (0, 0))),
        final_norm_gain[None, :],
        jnp.concatenate([targets, targets])[:, None],
        head_columns,
        blocks,
    )
    every = jnp.stack([stats] + [shifted(stats, ranks, k) for k in range(1, ranks)])
    maxima, totals, picked = every[:, 0], every[:, 1], every[:, 2]
    largest = jnp.max(maxima, axis=0)
    total = jnp.sum(totals * jnp.exp(maxima - largest[None]), axis=0)
    log_probs = jnp.sum(picked, axis=0) - largest - jnp.log(total)
    return (log_probs[:tok_rows], log_probs[tok_rows:])


def solution(mesh):
    return jax.shard_map(
        local,
        mesh=mesh,
        in_specs=(
            P("seq", None),
            P(),
            P(None, None, "tensor"),
            P("tensor", None),
            P("tensor", None),
            P(),
            P(),
            P("tensor", "seq"),
            P("seq", None, "tensor"),
            P("seq", None, "tensor"),
            P(),
            P(),
            P(),
            P("seq"),
        ),
        out_specs=(P("seq"), P("seq")),
        check_vma=False,
    )
```

```python
import math

import jax
import jax.numpy as jnp
from jax import lax
from jax.experimental import pallas as pl
from jax.experimental.pallas import tpu as pltpu
from jax.sharding import PartitionSpec as P

HEAD_WIDTH = 96
LEN = 64
PAGE = 128
MAXP = 8


EPSILON = 1e-05
NEGATIVE = -1e30
PAD = 128
VMEM_LIMIT = 28 * 1024 * 1024
F32 = jnp.float32
BF16 = jnp.bfloat16


def rms_norm(values, gain):
    mean_sq = jnp.mean(values * values, axis=-1, keepdims=True)
    return (values * lax.rsqrt(mean_sq + EPSILON) * gain.astype(F32)).astype(BF16)


def project_kernel(hidden_ref, gain_ref, weight_ref, cos_ref, sin_ref, out_ref, normed):
    part = pl.program_id(0)

    @pl.when(part == 0)
    def _():
        normed[...] = rms_norm(hidden_ref[...].astype(F32), gain_ref[...])

    product = jnp.dot(normed[...], weight_ref[0], preferred_element_type=F32)

    @pl.when(part < 2)
    def _():
        width = product.shape[1]
        half = HEAD_WIDTH // 2
        lane = lax.broadcasted_iota(jnp.int32, product.shape, 1) % HEAD_WIDTH
        partner = jnp.where(
            lane < half, -pltpu.roll(product, width - half, 1), pltpu.roll(product, half, 1)
        )
        out_ref[0] = (product * cos_ref[...] + partner * sin_ref[...]).astype(BF16)

    @pl.when(part == 2)
    def _():
        out_ref[0] = product.astype(BF16)


def project(hidden, gain, weight, cosine, sinus):
    rows, width = hidden.shape
    parts, _, cols = weight.shape
    whole = lambda i: (0, 0)
    return pl.pallas_call(
        project_kernel,
        grid=(parts,),
        in_specs=[
            pl.BlockSpec((rows, width), whole),
            pl.BlockSpec((1, width), whole),
            pl.BlockSpec((1, width, cols), lambda i: (i, 0, 0)),
            pl.BlockSpec((rows, cols), whole),
            pl.BlockSpec((rows, cols), whole),
        ],
        out_specs=pl.BlockSpec((1, rows, cols), lambda i: (i, 0, 0)),
        out_shape=jax.ShapeDtypeStruct((parts, rows, cols), BF16),
        scratch_shapes=[pltpu.VMEM((rows, width), BF16)],
        compiler_params=pltpu.CompilerParams(vmem_limit_bytes=VMEM_LIMIT),
        name="project",
    )(hidden, gain, weight, cosine, sinus)


def dot_nt(left, right):
    return lax.dot_general(left, right, (((1,), (1,)), ((), ())), preferred_element_type=F32)


def attend_kernel(*refs):
    first_ref, counts_ref, index_ref, owner_ref = refs[:4]
    qkv_ref, out_weight_ref, down_ref = refs[4:7]
    out_ref, keys, values, attended, sems = refs[-5:]
    pieces = refs[7:-5]
    key_pieces, value_pieces = pieces[: len(pieces) // 2], pieces[len(pieces) // 2 :]
    rollouts = keys.shape[0]
    width = qkv_ref.shape[2]
    heads = width // HEAD_WIDTH
    scale = 1.0 / math.sqrt(HEAD_WIDTH)
    first = first_ref[0]
    my_y, my_x, my_core = first_ref[1], first_ref[2], first_ref[3]

    def start_copies(r, j):
        slot = index_ref[owner_ref[first + r] * MAXP + j]
        device = slot // 2
        down_y = (device // 8 - my_y + 4) % 4
        down_x = (device // 2 % 4 - my_x + 4) % 4
        other = (device % 2 != my_core).astype(jnp.int32)
        rows = pl.ds(pl.multiple_of(j * PAGE, PAGE), PAGE)
        for which, (refs_here, buffer, far, near) in enumerate(
            ((key_pieces, keys, down_y, down_x), (value_pieces, values, down_x, down_y))
        ):
            at = near * 2 + slot % 2
            high = ((far == 2) & (at >= 4)).astype(jnp.int32)
            piece = far + high + (far == 3).astype(jnp.int32) + 5 * other
            at = at - 4 * high
            for p, ref in enumerate(refs_here):

                @pl.when(piece == p)
                def _():
                    row = jnp.minimum(at, ref.shape[0] - 1)
                    pltpu.make_async_copy(
                        ref.at[row], buffer.at[r, rows], sems.at[r, which, j]
                    ).start()

    lax.fori_loop(
        0, rollouts * MAXP, lambda n, _: (start_copies(n // MAXP, n % MAXP), 0)[1], 0
    )
    lane_head = lax.broadcasted_iota(jnp.int32, (LEN, width), 1) // HEAD_WIDTH
    own_row = lax.broadcasted_iota(jnp.int32, (heads * LEN, LEN), 0) % LEN
    own_col = lax.broadcasted_iota(jnp.int32, (heads * LEN, LEN), 1)
    page_of = lax.broadcasted_iota(jnp.int32, (heads * LEN, MAXP * PAGE), 1) // PAGE
    for r in range(rollouts):
        rows = slice(r * LEN, (r + 1) * LEN)
        query = qkv_ref[0, rows, :].astype(F32)
        stacked = jnp.concatenate(
            [jnp.where(lane_head == h, query, 0.0) for h in range(heads)], axis=0
        ).astype(BF16)
        own = dot_nt(stacked, qkv_ref[1, rows, :]) * scale
        own = jnp.where(own_col <= own_row, own, NEGATIVE)
        for j in range(MAXP):
            for which, (refs_here, buffer) in enumerate(
                ((key_pieces, keys), (value_pieces, values))
            ):
                pltpu.make_async_copy(
                    refs_here[0].at[0],
                    buffer.at[r, pl.ds(j * PAGE, PAGE)],
                    sems.at[r, which, j],
                ).wait()
        live = counts_ref[owner_ref[first + r]]
        cached = dot_nt(stacked, keys[r]) * scale
        cached = jnp.where(page_of < live, cached, NEGATIVE)
        largest = jnp.maximum(
            jnp.max(own, axis=1, keepdims=True), jnp.max(cached, axis=1, keepdims=True)
        )
        own = jnp.exp(own - largest)
        cached = jnp.exp(cached - largest)
        total = jnp.sum(own, axis=1, keepdims=True) + jnp.sum(cached, axis=1, keepdims=True)
        mixed = jnp.dot(cached.astype(BF16), values[r], preferred_element_type=F32) + jnp.dot(
            own.astype(BF16), qkv_ref[2, rows, :], preferred_element_type=F32
        )
        mixed = mixed / total
        picked = jnp.zeros((LEN, width), F32)
        for h in range(heads):
            picked = jnp.where(lane_head == h, mixed[h * LEN : (h + 1) * LEN], picked)
        attended[rows, :] = picked.astype(BF16)
    model = out_weight_ref.shape[1]
    out_ref[:, :model] = jnp.dot(
        attended[...], out_weight_ref[...], preferred_element_type=F32
    ).astype(BF16)
    out_ref[:, model:] = jnp.dot(
        attended[...], down_ref[...], preferred_element_type=F32
    ).astype(BF16)


def attend(first, counts, index, owner, qkv, key_pieces, value_pieces, out_weight, down):
    _, rows, width = qkv.shape
    rollouts = rows // LEN
    model = out_weight.shape[1]
    vmem = pl.BlockSpec(memory_space=pltpu.VMEM)
    pieces = list(key_pieces) + list(value_pieces)
    return pl.pallas_call(
        attend_kernel,
        grid_spec=pltpu.PrefetchScalarGridSpec(
            num_scalar_prefetch=4,
            grid=(),
            in_specs=[vmem, vmem, vmem] + [pl.BlockSpec(memory_space=pl.ANY)] * len(pieces),
            out_specs=vmem,
            scratch_shapes=[
                pltpu.VMEM((rollouts, MAXP * PAGE, width), BF16),
                pltpu.VMEM((rollouts, MAXP * PAGE, width), BF16),
                pltpu.VMEM((rows, width), BF16),
                pltpu.SemaphoreType.DMA((rollouts, 2, MAXP)),
            ],
        ),
        out_shape=jax.ShapeDtypeStruct((rows, model + PAD), BF16),
        compiler_params=pltpu.CompilerParams(vmem_limit_bytes=VMEM_LIMIT),
        name="attend",
    )(first, counts, index, owner, qkv, out_weight, down, *pieces)


def score_kernel(*refs):
    place_ref, up_ref, gain_ref, head_ref = refs[:4]
    out_ref, normed, wanted, largest, total, picked = refs[-6:]
    inputs = refs[4:-6]
    count = len(inputs) // 3
    step = pl.program_id(0)
    size, model = inputs[0].shape
    rows = count * size

    @pl.when(step == 0)
    def _():
        for k in range(count):
            hidden_ref, target_ref, block = inputs[3 * k : 3 * k + 3]
            at = pl.ds(k * size, size)
            reference = hidden_ref[...].astype(F32) + block[:, :model].astype(F32)
            policy = reference + jnp.dot(
                block[:, model:], up_ref[...], preferred_element_type=F32
            )
            normed[0, at, :] = rms_norm(policy, gain_ref[...])
            normed[1, at, :] = rms_norm(reference, gain_ref[...])
            wanted[pl.ds(k * size, size), :] = target_ref[...]
            wanted[pl.ds(rows + k * size, size), :] = target_ref[...]
        largest[...] = jnp.full_like(largest, NEGATIVE)
        total[...] = jnp.zeros_like(total)
        picked[...] = jnp.zeros_like(picked)

    logits = jnp.dot(
        normed[...].reshape(2 * rows, model), head_ref[...], preferred_element_type=F32
    )
    columns = lax.broadcasted_iota(jnp.int32, logits.shape, 1)
    column = wanted[...] - (place_ref[0] * pl.num_programs(0) + step) * logits.shape[1]
    picked[...] += jnp.sum(jnp.where(columns == column, logits, 0.0), axis=1, keepdims=True)
    before = largest[...]
    after = jnp.maximum(before, jnp.max(logits, axis=1, keepdims=True))
    total[...] = total[...] * jnp.exp(before - after) + jnp.sum(
        jnp.exp(logits - after), axis=1, keepdims=True
    )
    largest[...] = after

    @pl.when(step == pl.num_programs(0) - 1)
    def _():
        lane = lax.broadcasted_iota(jnp.int32, (2 * rows, 128), 1)
        packed = jnp.where(
            lane == 0, largest[...], jnp.where(lane == 1, total[...], picked[...])
        )
        out_ref[...] = jnp.transpose(packed)[:8, :]


def score(place, hidden, up, gain, targets, head, blocks):
    model = hidden.shape[1]
    vocab = head.shape[1]
    size = blocks[0].shape[0]
    rows = len(blocks) * size
    tile = 512
    whole = lambda i, p: (0, 0)
    per_block, operands = [], []
    for k, block in enumerate(blocks):
        here = lambda i, p, k=k: (p[1 + k], 0)
        per_block += [
            pl.BlockSpec((size, model), here),
            pl.BlockSpec((size, 1), here),
            pl.BlockSpec(block.shape, whole),
        ]
        operands += [hidden, targets, block]
    return pl.pallas_call(
        score_kernel,
        grid_spec=pltpu.PrefetchScalarGridSpec(
            num_scalar_prefetch=1,
            grid=(vocab // tile,),
            in_specs=[
                pl.BlockSpec(up.shape, whole),
                pl.BlockSpec(gain.shape, whole),
                pl.BlockSpec((model, tile), lambda i, p: (0, i)),
            ]
            + per_block,
            out_specs=pl.BlockSpec((8, 2 * rows), whole),
            scratch_shapes=[
                pltpu.VMEM((2, rows, model), BF16),
                pltpu.VMEM((2 * rows, 1), jnp.int32),
                pltpu.VMEM((2 * rows, 1), F32),
                pltpu.VMEM((2 * rows, 1), F32),
                pltpu.VMEM((2 * rows, 1), F32),
            ],
        ),
        out_shape=jax.ShapeDtypeStruct((8, 2 * rows), F32),
        compiler_params=pltpu.CompilerParams(vmem_limit_bytes=VMEM_LIMIT),
        cost_estimate=pl.CostEstimate(
            flops=4 * rows * model * vocab,
            transcendentals=2 * rows * vocab,
            bytes_accessed=2 * model * vocab,
        ),
        name="score",
    )(place, up, gain, head, *operands)


def shifted(value, ranks, step):
    return lax.ppermute(value, "tensor", [(i, (i + step) % ranks) for i in range(ranks)])


def ring_sum(branch, ranks):
    me = lax.axis_index("tensor")
    size = branch.shape[0] // ranks

    def mine(rank):
        return lax.dynamic_slice_in_dim(branch, (rank % ranks) * size, size, 0)

    half = ranks // 2
    left = mine(me + ranks - half)
    right = None
    for step in range(1, half + 1):
        arrived_left = shifted(left, ranks, -1)
        arrived_right = None if right is None else shifted(right, ranks, 1)
        if step == half:
            total = (
                mine(me).astype(F32) + arrived_left.astype(F32) + arrived_right.astype(F32)
            )
            return total.astype(BF16)
        left = (mine(me + ranks - half + step).astype(F32) + arrived_left.astype(F32)).astype(BF16)
        own = mine(me + half - step).astype(F32)
        if arrived_right is not None:
            own = own + arrived_right.astype(F32)
        right = own.astype(BF16)


def ring_gather(block, ranks):
    me = lax.axis_index("tensor")
    blocks, places = [block], [me]
    from_right = from_left = block
    for step in range(1, ranks // 2 + 1):
        from_right = shifted(from_right, ranks, -1)
        blocks.append(from_right)
        places.append((me + step) % ranks)
        if step < ranks // 2:
            from_left = shifted(from_left, ranks, 1)
            blocks.append(from_left)
            places.append((me + ranks - step) % ranks)
    return blocks, places


def along(value, axis, step):
    def target(i):
        y, x, core = i // 8, i // 2 % 4, i % 2
        if axis == "y":
            y = (y + step) % 4
        elif axis == "x":
            x = (x + step) % 4
        else:
            core = 1 - core
        return y * 8 + x * 2 + core

    return lax.ppermute(value, "seq", [(i, target(i)) for i in range(32)])


def gather_pages(keys, values):
    lines = []
    for value, axis in ((keys, "x"), (values, "y")):
        lines.append([value] + [along(value, axis, step) for step in (3, 2, 1)])
    lines = lax.optimization_barrier(lines)
    lines = lax.optimization_barrier([jnp.concatenate(line) for line in lines])
    ahead = [(along(line, axis, 3), along(line, axis, 1)) for line, axis in zip(lines, "yx")]
    near = [along(line, "core", 1) for line in lines]
    ahead, near = lax.optimization_barrier((ahead, near))
    halves = [
        (along(behind[:4], axis, 1), along(front[4:], axis, 3))
        for (front, behind), axis in zip(ahead, "yx")
    ]
    crossed = [(along(front, "core", 1), along(behind, "core", 1)) for front, behind in ahead]
    halves, crossed = lax.optimization_barrier((halves, crossed))
    result = []
    for line, near_line, (front, behind), (low, high), (far_front, far_behind) in zip(
        lines, near, ahead, halves, crossed
    ):
        far_low, far_high = along(low, "core", 1), along(high, "core", 1)
        result.append(
            [line, front, low, high, behind]
            + [near_line, far_front, far_low, far_high, far_behind]
        )
    return result[0], result[1], lines


def local(
    hidden,
    attention_norm_gain,
    query_key_value_weight,
    output_weight,
    adapter_down_weight,
    adapter_up_weight,
    final_norm_gain,
    head,
    prompt_key_slots,
    prompt_value_slots,
    counts,
    page_slot_index,
    owner,
    targets,
):
    tok_rows, model = hidden.shape
    rollouts_here = tok_rows // LEN
    width_here = output_weight.shape[0]
    heads_here = width_here // HEAD_WIDTH
    ranks = lax.axis_size("tensor")
    first = lax.axis_index("seq") * rollouts_here
    me = lax.axis_index("seq")
    key_pieces, value_pieces, stage = gather_pages(prompt_key_slots, prompt_value_slots)
    head_rows, _ = lax.optimization_barrier((head.T, stage))
    head_columns = lax.all_gather(head_rows, "seq", axis=0, tiled=True)

    groups_iota = jnp.arange(counts.shape[0], dtype=jnp.int32)
    my_groups = lax.dynamic_slice_in_dim(owner, first, rollouts_here, 0)
    my_pages = jnp.sum(
        jnp.where(my_groups[:, None] == groups_iota[None, :], counts[None, :], 0), axis=1
    )
    positions = jnp.repeat(my_pages, LEN) * PAGE + jnp.arange(tok_rows, dtype=jnp.int32) % LEN
    half = HEAD_WIDTH // 2
    place_in_head = jnp.arange(width_here, dtype=jnp.int32) % half
    frequency = 10000.0 ** (-place_in_head.astype(F32) * 2.0 / HEAD_WIDTH)
    angles = positions.astype(F32)[:, None] * frequency[None, :]
    qkv = project(
        hidden,
        attention_norm_gain[None, :],
        query_key_value_weight,
        jnp.cos(angles),
        jnp.sin(angles),
    )
    rank_pad = PAD - adapter_down_weight.shape[1]
    branch = attend(
        jnp.stack([first, me // 8, me // 2 % 4, me % 2]).astype(jnp.int32),
        counts,
        page_slot_index,
        owner,
        qkv,
        key_pieces,
        value_pieces,
        output_weight,
        jnp.pad(adapter_down_weight, ((0, 0), (0, rank_pad))),
    )
    blocks, places = ring_gather(ring_sum(branch, ranks), ranks)
    up = jnp.pad(adapter_up_weight, ((0, rank_pad), (0, 0)))
    size = tok_rows // ranks
    stats = []
    for chosen in ((0, 1, 2), (3, 4), (5, 6), (7,)):
        part = score(
            jnp.stack([lax.axis_index("tensor")] + [places[k] for k in chosen]).astype(jnp.int32),
            hidden,
            up,
            final_norm_gain[None, :],
            targets[:, None],
            head_columns,
            [blocks[k] for k in chosen],
        ).reshape(8, 2, len(chosen), size)
        stats += [(places[k], part[:, :, n]) for n, k in enumerate(chosen)]
    ordered = sorted(range(ranks), key=lambda k: (0, 1, 3, 5, 7, 6, 4, 2).index(k))
    line = jnp.stack([stats[k][1] for k in ordered] * 2, axis=2)
    turned = lax.dynamic_slice_in_dim(line, ranks - lax.axis_index("tensor"), ranks, 2)
    turned = turned.reshape(8, 2 * tok_rows)
    every = lax.all_to_all(
        jnp.broadcast_to(turned[None], (ranks, 8, 2 * tok_rows)), "tensor", 0, 0, tiled=True
    )
    maxima, totals, picked = every[:, 0], every[:, 1], every[:, 2]
    largest = jnp.max(maxima, axis=0)
    total = jnp.sum(totals * jnp.exp(maxima - largest[None]), axis=0)
    log_probs = jnp.sum(picked, axis=0) - largest - jnp.log(total)
    return (log_probs[:tok_rows], log_probs[tok_rows:])


def solution(mesh):
    return jax.shard_map(
        local,
        mesh=mesh,
        in_specs=(
            P("seq", None),
            P(),
            P(None, None, "tensor"),
            P("tensor", None),
            P("tensor", None),
            P(),
            P(),
            P("tensor", "seq"),
            P("seq", None, "tensor"),
            P("seq", None, "tensor"),
            P(),
            P(),
            P(),
            P("seq"),
        ),
        out_specs=(P("seq"), P("seq")),
        check_vma=False,
    )
```

```python
import math

import jax
import jax.numpy as jnp
from jax import lax
from jax.experimental import pallas as pl
from jax.experimental.pallas import tpu as pltpu
from jax.sharding import PartitionSpec as P

HEAD_WIDTH = 96
LEN = 64
PAGE = 128
MAXP = 8


EPSILON = 1e-05
NEGATIVE = -1e30
PAD = 128
VMEM_LIMIT = 28 * 1024 * 1024
F32 = jnp.float32
BF16 = jnp.bfloat16


def rms_norm(values, gain):
    mean_sq = jnp.mean(values * values, axis=-1, keepdims=True)
    return (values * lax.rsqrt(mean_sq + EPSILON) * gain.astype(F32)).astype(BF16)


def project_kernel(hidden_ref, gain_ref, weight_ref, cos_ref, sin_ref, out_ref, normed):
    part = pl.program_id(0)

    @pl.when(part == 0)
    def _():
        normed[...] = rms_norm(hidden_ref[...].astype(F32), gain_ref[...])

    product = jnp.dot(normed[...], weight_ref[0], preferred_element_type=F32)

    @pl.when(part < 2)
    def _():
        width = product.shape[1]
        half = HEAD_WIDTH // 2
        lane = lax.broadcasted_iota(jnp.int32, product.shape, 1) % HEAD_WIDTH
        partner = jnp.where(
            lane < half, -pltpu.roll(product, width - half, 1), pltpu.roll(product, half, 1)
        )
        out_ref[0] = (product * cos_ref[...] + partner * sin_ref[...]).astype(BF16)

    @pl.when(part == 2)
    def _():
        out_ref[0] = product.astype(BF16)


def project(hidden, gain, weight, cosine, sinus):
    rows, width = hidden.shape
    parts, _, cols = weight.shape
    whole = lambda i: (0, 0)
    return pl.pallas_call(
        project_kernel,
        grid=(parts,),
        in_specs=[
            pl.BlockSpec((rows, width), whole),
            pl.BlockSpec((1, width), whole),
            pl.BlockSpec((1, width, cols), lambda i: (i, 0, 0)),
            pl.BlockSpec((rows, cols), whole),
            pl.BlockSpec((rows, cols), whole),
        ],
        out_specs=pl.BlockSpec((1, rows, cols), lambda i: (i, 0, 0)),
        out_shape=jax.ShapeDtypeStruct((parts, rows, cols), BF16),
        scratch_shapes=[pltpu.VMEM((rows, width), BF16)],
        compiler_params=pltpu.CompilerParams(vmem_limit_bytes=VMEM_LIMIT),
        name="project",
    )(hidden, gain, weight, cosine, sinus)


def dot_nt(left, right):
    return lax.dot_general(left, right, (((1,), (1,)), ((), ())), preferred_element_type=F32)


def attend_kernel(*refs):
    first_ref, counts_ref, index_ref, owner_ref = refs[:4]
    qkv_ref, out_weight_ref, down_ref = refs[4:7]
    out_ref, keys, values, attended, sems = refs[-5:]
    pieces = refs[7:-5]
    key_pieces, value_pieces = pieces[: len(pieces) // 2], pieces[len(pieces) // 2 :]
    rollouts = keys.shape[0]
    width = qkv_ref.shape[2]
    heads = width // HEAD_WIDTH
    scale = 1.0 / math.sqrt(HEAD_WIDTH)
    first = first_ref[0]
    my_y, my_x, my_core = first_ref[1], first_ref[2], first_ref[3]

    def start_copies(r, j):
        slot = index_ref[owner_ref[first + r] * MAXP + j]
        device = slot // 2
        down_y = (device // 8 - my_y + 4) % 4
        down_x = (device // 2 % 4 - my_x + 4) % 4
        other = (device % 2 != my_core).astype(jnp.int32)
        rows = pl.ds(pl.multiple_of(j * PAGE, PAGE), PAGE)
        for which, (refs_here, buffer, far, near) in enumerate(
            ((key_pieces, keys, down_y, down_x), (value_pieces, values, down_x, down_y))
        ):
            at = near * 2 + slot % 2
            high = ((far == 2) & (at >= 4)).astype(jnp.int32)
            piece = far + high + (far == 3).astype(jnp.int32) + 5 * other
            at = at - 4 * high
            for p, ref in enumerate(refs_here):

                @pl.when(piece == p)
                def _():
                    row = jnp.minimum(at, ref.shape[0] - 1)
                    pltpu.make_async_copy(
                        ref.at[row], buffer.at[r, rows], sems.at[r, which, j]
                    ).start()

        return 0

    def live_pages(r):
        return counts_ref[owner_ref[first + r]]

    def covering(live):
        return jnp.where(live <= 1, 1, jnp.where(live <= 2, 2, jnp.where(live <= 4, 4, MAXP)))

    def start_rollout(r, _):
        return lax.fori_loop(0, covering(live_pages(r)), lambda j, _: start_copies(r, j), 0)

    lax.fori_loop(0, rollouts, start_rollout, 0)
    lane_head = lax.broadcasted_iota(jnp.int32, (LEN, width), 1) // HEAD_WIDTH
    own_row = lax.broadcasted_iota(jnp.int32, (heads * LEN, LEN), 0) % LEN
    own_col = lax.broadcasted_iota(jnp.int32, (heads * LEN, LEN), 1)

    def mix_rollout(r, _):
        live = live_pages(r)
        rows = pl.ds(pl.multiple_of(r * LEN, LEN), LEN)

        def mix(pages):
            query = qkv_ref[0, rows, :].astype(F32)
            stacked = jnp.concatenate(
                [jnp.where(lane_head == h, query, 0.0) for h in range(heads)], axis=0
            ).astype(BF16)
            own = dot_nt(stacked, qkv_ref[1, rows, :]) * scale
            own = jnp.where(own_col <= own_row, own, NEGATIVE)
            for j in range(pages):
                for which, (refs_here, buffer) in enumerate(
                    ((key_pieces, keys), (value_pieces, values))
                ):
                    pltpu.make_async_copy(
                        refs_here[0].at[0],
                        buffer.at[r, pl.ds(j * PAGE, PAGE)],
                        sems.at[r, which, j],
                    ).wait()
            span = pl.ds(0, pages * PAGE)
            cached = dot_nt(stacked, keys[r, span]) * scale
            page_of = lax.broadcasted_iota(jnp.int32, cached.shape, 1) // PAGE
            cached = jnp.where(page_of < live, cached, NEGATIVE)
            largest = jnp.maximum(
                jnp.max(own, axis=1, keepdims=True), jnp.max(cached, axis=1, keepdims=True)
            )
            own = jnp.exp(own - largest)
            cached = jnp.exp(cached - largest)
            total = jnp.sum(own, axis=1, keepdims=True) + jnp.sum(cached, axis=1, keepdims=True)
            mixed = jnp.dot(
                cached.astype(BF16), values[r, span], preferred_element_type=F32
            ) + jnp.dot(own.astype(BF16), qkv_ref[2, rows, :], preferred_element_type=F32)
            mixed = mixed / total
            picked = jnp.zeros((LEN, width), F32)
            for h in range(heads):
                picked = jnp.where(lane_head == h, mixed[h * LEN : (h + 1) * LEN], picked)
            attended[rows, :] = picked.astype(BF16)

        for pages in (1, 2, 4, MAXP):
            pl.when(covering(live) == pages)(lambda pages=pages: mix(pages))
        return 0

    lax.fori_loop(0, rollouts, mix_rollout, 0)
    model = out_weight_ref.shape[1]
    out_ref[:, :model] = jnp.dot(
        attended[...], out_weight_ref[...], preferred_element_type=F32
    ).astype(BF16)
    out_ref[:, model:] = jnp.dot(
        attended[...], down_ref[...], preferred_element_type=F32
    ).astype(BF16)


def attend(first, counts, index, owner, qkv, key_pieces, value_pieces, out_weight, down):
    _, rows, width = qkv.shape
    rollouts = rows // LEN
    model = out_weight.shape[1]
    vmem = pl.BlockSpec(memory_space=pltpu.VMEM)
    pieces = [
        pltpu.with_memory_space_constraint(piece, pltpu.HBM)
        for piece in list(key_pieces) + list(value_pieces)
    ]
    return pl.pallas_call(
        attend_kernel,
        grid_spec=pltpu.PrefetchScalarGridSpec(
            num_scalar_prefetch=4,
            grid=(),
            in_specs=[vmem, vmem, vmem] + [pl.BlockSpec(memory_space=pltpu.HBM)] * len(pieces),
            out_specs=vmem,
            scratch_shapes=[
                pltpu.VMEM((rollouts, MAXP * PAGE, width), BF16),
                pltpu.VMEM((rollouts, MAXP * PAGE, width), BF16),
                pltpu.VMEM((rows, width), BF16),
                pltpu.SemaphoreType.DMA((rollouts, 2, MAXP)),
            ],
        ),
        out_shape=jax.ShapeDtypeStruct((rows, model + PAD), BF16),
        compiler_params=pltpu.CompilerParams(vmem_limit_bytes=VMEM_LIMIT),
        name="attend",
    )(first, counts, index, owner, qkv, out_weight, down, *pieces)


def score_kernel(*refs):
    place_ref, up_ref, gain_ref, head_ref = refs[:4]
    out_ref, normed, wanted, largest, total, picked = refs[-6:]
    inputs = refs[4:-6]
    count = len(inputs) // 3
    step = pl.program_id(0)
    size, model = inputs[0].shape
    rows = count * size

    @pl.when(step == 0)
    def _():
        for k in range(count):
            hidden_ref, target_ref, block = inputs[3 * k : 3 * k + 3]
            at = pl.ds(k * size, size)
            reference = hidden_ref[...].astype(F32) + block[:, :model].astype(F32)
            policy = reference + jnp.dot(
                block[:, model:], up_ref[...], preferred_element_type=F32
            )
            normed[0, at, :] = rms_norm(policy, gain_ref[...])
            normed[1, at, :] = rms_norm(reference, gain_ref[...])
            wanted[pl.ds(k * size, size), :] = target_ref[...]
            wanted[pl.ds(rows + k * size, size), :] = target_ref[...]
        largest[...] = jnp.full_like(largest, NEGATIVE)
        total[...] = jnp.zeros_like(total)
        picked[...] = jnp.zeros_like(picked)

    logits = jnp.dot(
        normed[...].reshape(2 * rows, model), head_ref[...], preferred_element_type=F32
    )
    columns = lax.broadcasted_iota(jnp.int32, logits.shape, 1)
    column = wanted[...] - (place_ref[0] * pl.num_programs(0) + step) * logits.shape[1]
    picked[...] += jnp.sum(jnp.where(columns == column, logits, 0.0), axis=1, keepdims=True)
    before = largest[...]
    after = jnp.maximum(before, jnp.max(logits, axis=1, keepdims=True))
    total[...] = total[...] * jnp.exp(before - after) + jnp.sum(
        jnp.exp(logits - after), axis=1, keepdims=True
    )
    largest[...] = after

    @pl.when(step == pl.num_programs(0) - 1)
    def _():
        lane = lax.broadcasted_iota(jnp.int32, (2 * rows, 128), 1)
        packed = jnp.where(
            lane == 0, largest[...], jnp.where(lane == 1, total[...], picked[...])
        )
        out_ref[...] = jnp.transpose(packed)[:8, :]


def score(place, hidden, up, gain, targets, head, blocks):
    model = hidden.shape[1]
    vocab = head.shape[1]
    size = blocks[0].shape[0]
    rows = len(blocks) * size
    tile = 512
    whole = lambda i, p: (0, 0)
    per_block, operands = [], []
    for k, block in enumerate(blocks):
        here = lambda i, p, k=k: (p[1 + k], 0)
        per_block += [
            pl.BlockSpec((size, model), here),
            pl.BlockSpec((size, 1), here),
            pl.BlockSpec(block.shape, whole),
        ]
        operands += [hidden, targets, block]
    return pl.pallas_call(
        score_kernel,
        grid_spec=pltpu.PrefetchScalarGridSpec(
            num_scalar_prefetch=1,
            grid=(vocab // tile,),
            in_specs=[
                pl.BlockSpec(up.shape, whole),
                pl.BlockSpec(gain.shape, whole),
                pl.BlockSpec((model, tile), lambda i, p: (0, i)),
            ]
            + per_block,
            out_specs=pl.BlockSpec((8, 2 * rows), whole),
            scratch_shapes=[
                pltpu.VMEM((2, rows, model), BF16),
                pltpu.VMEM((2 * rows, 1), jnp.int32),
                pltpu.VMEM((2 * rows, 1), F32),
                pltpu.VMEM((2 * rows, 1), F32),
                pltpu.VMEM((2 * rows, 1), F32),
            ],
        ),
        out_shape=jax.ShapeDtypeStruct((8, 2 * rows), F32),
        compiler_params=pltpu.CompilerParams(vmem_limit_bytes=VMEM_LIMIT),
        cost_estimate=pl.CostEstimate(
            flops=4 * rows * model * vocab,
            transcendentals=2 * rows * vocab,
            bytes_accessed=2 * model * vocab,
        ),
        name="score",
    )(place, up, gain, head, *operands)


def shifted(value, ranks, step):
    return lax.ppermute(value, "tensor", [(i, (i + step) % ranks) for i in range(ranks)])


def reduce_rows(branch, ranks):
    me = lax.axis_index("tensor")
    size = branch.shape[0] // ranks
    half = size // 2

    def mine(offset, start=0, rows=size):
        return lax.dynamic_slice_in_dim(branch, (me + offset) % ranks * size + start, rows, 0)

    far = (
        shifted(mine(5), ranks, -1),
        shifted(mine(3), ranks, 1),
        shifted(mine(4, 0, half), ranks, -2),
        shifted(mine(4, half, half), ranks, 2),
    )
    behind, ahead, low, high = (value.astype(F32) for value in lax.optimization_barrier(far))
    nothing = jnp.zeros_like(low)
    behind = mine(6).astype(F32) + behind + jnp.concatenate([low, nothing])
    ahead = mine(2).astype(F32) + ahead + jnp.concatenate([nothing, high])
    near = (
        shifted(behind.astype(BF16), ranks, -2),
        shifted(ahead.astype(BF16), ranks, 2),
        shifted(mine(7), ranks, -1),
        shifted(mine(1), ranks, 1),
    )
    total = mine(0).astype(F32)
    for value in lax.optimization_barrier(near):
        total = total + value.astype(F32)
    return total.astype(BF16)


def along(value, axis, step):
    def target(i):
        y, x, core = i // 8, i // 2 % 4, i % 2
        if axis == "y":
            y = (y + step) % 4
        elif axis == "x":
            x = (x + step) % 4
        else:
            core = 1 - core
        return y * 8 + x * 2 + core

    return lax.ppermute(value, "seq", [(i, target(i)) for i in range(32)])


def gather_pages(keys, values):
    lines = []
    for value, axis in ((keys, "x"), (values, "y")):
        lines.append([value] + [along(value, axis, step) for step in (3, 2, 1)])
    lines = lax.optimization_barrier(lines)
    lines = lax.optimization_barrier([jnp.concatenate(line) for line in lines])
    ahead = [(along(line, axis, 3), along(line, axis, 1)) for line, axis in zip(lines, "yx")]
    near = [along(line, "core", 1) for line in lines]
    ahead, near = lax.optimization_barrier((ahead, near))
    halves = [
        (along(behind[:4], axis, 1), along(front[4:], axis, 3))
        for (front, behind), axis in zip(ahead, "yx")
    ]
    crossed = [(along(front, "core", 1), along(behind, "core", 1)) for front, behind in ahead]
    halves, crossed = lax.optimization_barrier((halves, crossed))
    result = []
    for line, near_line, (front, behind), (low, high), (far_front, far_behind) in zip(
        lines, near, ahead, halves, crossed
    ):
        far_low, far_high = along(low, "core", 1), along(high, "core", 1)
        result.append(
            [line, front, low, high, behind]
            + [near_line, far_front, far_low, far_high, far_behind]
        )
    return result[0], result[1], ahead


def local(
    hidden,
    attention_norm_gain,
    query_key_value_weight,
    output_weight,
    adapter_down_weight,
    adapter_up_weight,
    final_norm_gain,
    head,
    prompt_key_slots,
    prompt_value_slots,
    counts,
    page_slot_index,
    owner,
    targets,
):
    tok_rows, model = hidden.shape
    rollouts_here = tok_rows // LEN
    width_here = output_weight.shape[0]
    heads_here = width_here // HEAD_WIDTH
    ranks = lax.axis_size("tensor")
    first = lax.axis_index("seq") * rollouts_here
    me = lax.axis_index("seq")
    key_pieces, value_pieces, stage = gather_pages(prompt_key_slots, prompt_value_slots)
    head_rows, _ = lax.optimization_barrier((head.T, stage))
    head_columns = lax.all_gather(head_rows, "seq", axis=0, tiled=True)

    groups_iota = jnp.arange(counts.shape[0], dtype=jnp.int32)
    my_groups = lax.dynamic_slice_in_dim(owner, first, rollouts_here, 0)
    my_pages = jnp.sum(
        jnp.where(my_groups[:, None] == groups_iota[None, :], counts[None, :], 0), axis=1
    )
    positions = jnp.repeat(my_pages, LEN) * PAGE + jnp.arange(tok_rows, dtype=jnp.int32) % LEN
    half = HEAD_WIDTH // 2
    place_in_head = jnp.arange(width_here, dtype=jnp.int32) % half
    frequency = 10000.0 ** (-place_in_head.astype(F32) * 2.0 / HEAD_WIDTH)
    angles = positions.astype(F32)[:, None] * frequency[None, :]
    qkv = project(
        hidden,
        attention_norm_gain[None, :],
        query_key_value_weight,
        jnp.cos(angles),
        jnp.sin(angles),
    )
    rank_pad = PAD - adapter_down_weight.shape[1]
    branch = attend(
        jnp.stack([first, me // 8, me // 2 % 4, me % 2]).astype(jnp.int32),
        counts,
        page_slot_index,
        owner,
        qkv,
        key_pieces,
        value_pieces,
        output_weight,
        jnp.pad(adapter_down_weight, ((0, 0), (0, rank_pad))),
    )
    mine = reduce_rows(branch, ranks)
    rank = lax.axis_index("tensor")
    size = tok_rows // ranks
    up = jnp.pad(adapter_up_weight, ((0, rank_pad), (0, 0)))
    head_columns = pltpu.with_memory_space_constraint(head_columns, pltpu.HBM)

    def score_blocks(offsets, blocks):
        part = score(
            jnp.stack([rank] + [(rank + offset) % ranks for offset in offsets]).astype(jnp.int32),
            hidden,
            up,
            final_norm_gain[None, :],
            targets[:, None],
            head_columns,
            blocks,
        ).reshape(8, 2, len(offsets), size)
        return {offset: part[:, :, n] for n, offset in enumerate(offsets)}

    near = [shifted(mine, ranks, step) for step in (-1, 1, -2, 2)]
    near = lax.optimization_barrier(near)
    after_one, before_one, after_two, before_two = near
    far = [
        shifted(after_two, ranks, -1),
        shifted(before_two, ranks, 1),
        shifted(after_two[: size // 2], ranks, -2),
        shifted(before_two[size // 2 :], ranks, 2),
    ]
    stats = score_blocks((0, 1, 7, 2, 6), [mine] + near)
    far = [far[0], far[1], jnp.concatenate([far[2], far[3]])]
    stats.update(score_blocks((3, 5, 4), far))
    line = jnp.stack([stats[k] for k in range(ranks)] * 2, axis=2)
    turned = lax.dynamic_slice_in_dim(line, ranks - rank, ranks, 2).reshape(8, 2 * tok_rows)
    every = lax.all_to_all(
        jnp.broadcast_to(turned[None], (ranks, 8, 2 * tok_rows)), "tensor", 0, 0, tiled=True
    )
    maxima, totals, picked = every[:, 0], every[:, 1], every[:, 2]
    largest = jnp.max(maxima, axis=0)
    total = jnp.sum(totals * jnp.exp(maxima - largest[None]), axis=0)
    log_probs = jnp.sum(picked, axis=0) - largest - jnp.log(total)
    return (log_probs[:tok_rows], log_probs[tok_rows:])


def solution(mesh):
    return jax.shard_map(
        local,
        mesh=mesh,
        in_specs=(
            P("seq", None),
            P(),
            P(None, None, "tensor"),
            P("tensor", None),
            P("tensor", None),
            P(),
            P(),
            P("tensor", "seq"),
            P("seq", None, "tensor"),
            P("seq", None, "tensor"),
            P(),
            P(),
            P(),
            P("seq"),
        ),
        out_specs=(P("seq"), P("seq")),
        check_vma=False,
    )
```

```python
import math

import jax
import jax.numpy as jnp
from jax import lax
from jax.experimental import pallas as pl
from jax.experimental.pallas import tpu as pltpu
from jax.sharding import PartitionSpec as P

HEAD_WIDTH = 96
LEN = 64
PAGE = 128
MAXP = 8


EPSILON = 1e-05
NEGATIVE = -1e30
PAD = 128
BLOCK = LEN // 2
VMEM_LIMIT = 28 * 1024 * 1024
F32 = jnp.float32
BF16 = jnp.bfloat16


def rms_norm(values, gain):
    mean_sq = jnp.mean(values * values, axis=-1, keepdims=True)
    return (values * lax.rsqrt(mean_sq + EPSILON) * gain.astype(F32)).astype(BF16)


def project_kernel(hidden_ref, gain_ref, weight_ref, cos_ref, sin_ref, out_ref, normed):
    part = pl.program_id(0)

    @pl.when(part == 0)
    def _():
        normed[...] = rms_norm(hidden_ref[...].astype(F32), gain_ref[...])

    product = jnp.dot(normed[...], weight_ref[0], preferred_element_type=F32)

    @pl.when(part < 2)
    def _():
        width = product.shape[1]
        half = HEAD_WIDTH // 2
        lane = lax.broadcasted_iota(jnp.int32, product.shape, 1) % HEAD_WIDTH
        partner = jnp.where(
            lane < half, -pltpu.roll(product, width - half, 1), pltpu.roll(product, half, 1)
        )
        out_ref[0] = (product * cos_ref[...] + partner * sin_ref[...]).astype(BF16)

    @pl.when(part == 2)
    def _():
        out_ref[0] = product.astype(BF16)


def project(hidden, gain, weight, cosine, sinus):
    rows, width = hidden.shape
    parts, _, cols = weight.shape
    whole = lambda i: (0, 0)
    return pl.pallas_call(
        project_kernel,
        grid=(parts,),
        in_specs=[
            pl.BlockSpec((rows, width), whole),
            pl.BlockSpec((1, width), whole),
            pl.BlockSpec((1, width, cols), lambda i: (i, 0, 0)),
            pl.BlockSpec((rows, cols), whole),
            pl.BlockSpec((rows, cols), whole),
        ],
        out_specs=pl.BlockSpec((1, rows, cols), lambda i: (i, 0, 0)),
        out_shape=jax.ShapeDtypeStruct((parts, rows, cols), BF16),
        scratch_shapes=[pltpu.VMEM((rows, width), BF16)],
        compiler_params=pltpu.CompilerParams(vmem_limit_bytes=VMEM_LIMIT),
        name="project",
    )(hidden, gain, weight, cosine, sinus)


def dot_nt(left, right):
    return lax.dot_general(left, right, (((1,), (1,)), ((), ())), preferred_element_type=F32)


def attend_kernel(*refs):
    first_ref, counts_ref, index_ref, owner_ref = refs[:4]
    qkv_ref = refs[4]
    out_ref, keys, values, sems = refs[-4:]
    pieces = refs[5:-4]
    rollouts = keys.shape[0]
    width = qkv_ref.shape[2]
    heads = width // HEAD_WIDTH
    scale = 1.0 / math.sqrt(HEAD_WIDTH)
    first = first_ref[0]
    my_y, my_x, my_core = first_ref[1], first_ref[2], first_ref[3]

    def start_copies(r, j):
        slot = index_ref[owner_ref[first + r] * MAXP + j]
        device = slot // 2
        down_y = (device // 8 - my_y + 4) % 4
        down_x = (device // 2 % 4 - my_x + 4) % 4
        other = (device % 2 != my_core).astype(jnp.int32)
        rows = pl.ds(pl.multiple_of(j * PAGE, PAGE), PAGE)
        for which, (buffer, far, near) in enumerate(
            ((keys, down_y, down_x), (values, down_x, down_y))
        ):
            at = near * 4 + 2 * (device % 2 != which).astype(jnp.int32) + slot % 2
            high = ((far == 2) & (at >= 8)).astype(jnp.int32)
            piece = far + high + (far == 3).astype(jnp.int32)
            piece = piece + 5 * (my_core != which).astype(jnp.int32)
            at = at - 8 * high
            for p, ref in enumerate(pieces):

                @pl.when(piece == p)
                def _():
                    row = jnp.minimum(at, ref.shape[0] - 1)
                    pltpu.make_async_copy(
                        ref.at[row], buffer.at[r, rows], sems.at[r, which, j]
                    ).start()

        return 0

    def live_pages(r):
        return counts_ref[owner_ref[first + r]]

    def covering(live):
        return jnp.where(live <= 2, 2, jnp.where(live <= 4, 4, MAXP))

    def start_rollout(r, _):
        return lax.fori_loop(0, covering(live_pages(r)), lambda j, _: start_copies(r, j), 0)

    lax.fori_loop(0, rollouts, start_rollout, 0)
    lane_head = lax.broadcasted_iota(jnp.int32, (LEN, width), 1) // HEAD_WIDTH
    own_row = lax.broadcasted_iota(jnp.int32, (heads * LEN, LEN), 0) % LEN
    own_col = lax.broadcasted_iota(jnp.int32, (heads * LEN, LEN), 1)

    def mix_rollout(r, _):
        live = live_pages(r)
        rows = pl.ds(pl.multiple_of(r * LEN, LEN), LEN)

        def mix(pages):
            query = qkv_ref[0, rows, :].astype(F32)
            stacked = jnp.concatenate(
                [jnp.where(lane_head == h, query, 0.0) for h in range(heads)], axis=0
            ).astype(BF16)
            own = dot_nt(stacked, qkv_ref[1, rows, :]) * scale
            own = jnp.where(own_col <= own_row, own, NEGATIVE)
            for j in range(pages):
                for which, buffer in enumerate((keys, values)):
                    pltpu.make_async_copy(
                        pieces[0].at[0],
                        buffer.at[r, pl.ds(j * PAGE, PAGE)],
                        sems.at[r, which, j],
                    ).wait()
            span = pl.ds(0, pages * PAGE)
            cached = dot_nt(stacked, keys[r, span]) * scale
            page_of = lax.broadcasted_iota(jnp.int32, cached.shape, 1) // PAGE
            cached = jnp.where(page_of < live, cached, NEGATIVE)
            largest = jnp.maximum(
                jnp.max(own, axis=1, keepdims=True), jnp.max(cached, axis=1, keepdims=True)
            )
            own = jnp.exp(own - largest)
            cached = jnp.exp(cached - largest)
            total = jnp.sum(own, axis=1, keepdims=True) + jnp.sum(cached, axis=1, keepdims=True)
            mixed = jnp.dot(
                cached.astype(BF16), values[r, span], preferred_element_type=F32
            ) + jnp.dot(own.astype(BF16), qkv_ref[2, rows, :], preferred_element_type=F32)
            mixed = mixed / total
            picked = jnp.zeros((LEN, width), F32)
            for h in range(heads):
                picked = jnp.where(lane_head == h, mixed[h * LEN : (h + 1) * LEN], picked)
            for parity in range(2):
                out_ref[parity, pl.ds(pl.multiple_of(r * BLOCK, BLOCK), BLOCK), :] = picked[
                    parity * BLOCK : (parity + 1) * BLOCK
                ].astype(BF16)

        for pages in (2, 4, MAXP):
            pl.when(covering(live) == pages)(lambda pages=pages: mix(pages))
        return 0

    lax.fori_loop(0, rollouts, mix_rollout, 0)


def attend(first, counts, index, owner, qkv, pieces):
    _, rows, width = qkv.shape
    rollouts = rows // LEN
    vmem = pl.BlockSpec(memory_space=pltpu.VMEM)
    pieces = [pltpu.with_memory_space_constraint(piece, pltpu.HBM) for piece in pieces]
    return pl.pallas_call(
        attend_kernel,
        grid_spec=pltpu.PrefetchScalarGridSpec(
            num_scalar_prefetch=4,
            grid=(),
            in_specs=[vmem] + [pl.BlockSpec(memory_space=pltpu.HBM)] * len(pieces),
            out_specs=vmem,
            scratch_shapes=[
                pltpu.VMEM((rollouts, MAXP * PAGE, width), BF16),
                pltpu.VMEM((rollouts, MAXP * PAGE, width), BF16),
                pltpu.SemaphoreType.DMA((rollouts, 2, MAXP)),
            ],
        ),
        out_shape=jax.ShapeDtypeStruct((2, rows // 2, width), BF16),
        compiler_params=pltpu.CompilerParams(vmem_limit_bytes=VMEM_LIMIT),
        name="attend",
    )(first, counts, index, owner, qkv, *pieces)


def branch_kernel(*refs):
    mine_ref, theirs_ref = refs[:2]
    out_ref = refs[-1]
    chunks = refs[2:-1]
    count = len(chunks) // 2
    start = 0
    for own, partner in zip(chunks[:count], chunks[count:]):
        columns = slice(start, start + own.shape[1])
        out_ref[:, columns] = (
            jnp.dot(mine_ref[...], own[...], preferred_element_type=F32)
            + jnp.dot(theirs_ref[...], partner[...], preferred_element_type=F32)
        ).astype(BF16)
        start += own.shape[1]


def branch_part(mine, theirs, own, partner):
    width = sum(chunk.shape[1] for chunk in own)
    operands = [mine, theirs] + [
        pltpu.with_memory_space_constraint(chunk, pltpu.HBM)
        for chunk in list(own) + list(partner)
    ]
    whole = lambda i: (0, 0)
    out = jax.ShapeDtypeStruct((mine.shape[0], width), BF16)
    return pl.pallas_call(
        branch_kernel,
        grid=(1,),
        in_specs=[pl.BlockSpec(operand.shape, whole) for operand in operands],
        out_specs=pl.BlockSpec(out.shape, whole),
        out_shape=out,
        compiler_params=pltpu.CompilerParams(vmem_limit_bytes=VMEM_LIMIT),
        name="branch",
    )(*operands)


def two_parts(value):
    high = value.astype(BF16)
    return high, (value - high.astype(F32)).astype(BF16)


def score_kernel(*refs):
    place_ref, up_ref, gain_ref, head_ref = refs[:4]
    out_ref, normed, deltas, scales, wanted, largest, total, picked = refs[-8:]
    inputs = refs[4:-8]
    step = pl.program_id(0)
    rank, model = up_ref.shape
    rows = deltas.shape[0]

    @pl.when(step == 0)
    def _():
        start = 0
        gain = gain_ref[...].astype(F32)
        up = up_ref[...]
        for hidden_ref, target_ref, block in zip(inputs[::3], inputs[1::3], inputs[2::3]):
            at = slice(start, start + block.shape[0])
            start += block.shape[0]
            delta = block[:, model : model + rank]
            reference = hidden_ref[...].astype(F32) + block[:, :model].astype(F32)
            policy = reference + jnp.dot(delta, up, preferred_element_type=F32)
            reference_scale = lax.rsqrt(
                jnp.mean(reference * reference, axis=1, keepdims=True) + EPSILON
            )
            policy_scale = lax.rsqrt(jnp.mean(policy * policy, axis=1, keepdims=True) + EPSILON)
            normed[at, :] = (reference * reference_scale * gain).astype(BF16)
            deltas[at, :] = jnp.concatenate([delta, delta], axis=1)
            scales[0, at, :] = policy_scale / reference_scale
            scales[1, at, :] = policy_scale
            wanted[at, :] = target_ref[...]
        high, low = two_parts(up.astype(F32) * gain)
        normed[rows : rows + rank, :] = high
        normed[rows + rank :, :] = low
        largest[...] = jnp.full_like(largest, NEGATIVE)
        total[...] = jnp.zeros_like(total)
        picked[...] = jnp.zeros_like(picked)

    product = jnp.dot(normed[...], head_ref[...], preferred_element_type=F32)
    reference_logits = product[:rows]
    high, low = two_parts(product[rows : rows + rank] + product[rows + rank :])
    adapted = jnp.dot(
        deltas[...], jnp.concatenate([high, low], axis=0), preferred_element_type=F32
    )
    policy_logits = scales[0] * reference_logits + scales[1] * adapted
    columns = lax.broadcasted_iota(jnp.int32, reference_logits.shape, 1)
    tile = head_ref.shape[1]
    hit = columns == wanted[...] - (place_ref[0] * pl.num_programs(0) + step) * tile
    for which, logits in enumerate((policy_logits, reference_logits)):
        picked[which] += jnp.sum(jnp.where(hit, logits, 0.0), axis=1, keepdims=True)
        before = largest[which]
        after = jnp.maximum(before, jnp.max(logits, axis=1, keepdims=True))
        total[which] = total[which] * jnp.exp(before - after) + jnp.sum(
            jnp.exp(logits - after), axis=1, keepdims=True
        )
        largest[which] = after

    @pl.when(step == pl.num_programs(0) - 1)
    def _():
        lane = lax.broadcasted_iota(jnp.int32, (2, rows, 128), 2)
        packed = jnp.where(
            lane == 0, largest[...], jnp.where(lane == 1, total[...], picked[...])
        )
        out_ref[...] = jnp.transpose(packed.reshape(2 * rows, 128))[:8, :]


def score(place, hidden, up, gain, targets, head, blocks):
    model = hidden.shape[1]
    vocab = head.shape[1]
    rank = up.shape[0]
    rows = sum(block.shape[0] for block in blocks)
    tile = 256
    whole = lambda i, p: (0, 0)
    per_block, operands = [], []
    for k, block in enumerate(blocks):
        size = block.shape[0]
        here = lambda i, p, k=k: (p[1 + k], 0)
        per_block += [
            pl.BlockSpec((size, model), here),
            pl.BlockSpec((size, 1), here),
            pl.BlockSpec(block.shape, whole),
        ]
        operands += [hidden, targets, block]
    column = pltpu.VMEM((2, rows, 1), F32)
    return pl.pallas_call(
        score_kernel,
        grid_spec=pltpu.PrefetchScalarGridSpec(
            num_scalar_prefetch=1,
            grid=(vocab // tile,),
            in_specs=[
                pl.BlockSpec(up.shape, whole),
                pl.BlockSpec(gain.shape, whole),
                pl.BlockSpec((model, tile), lambda i, p: (0, i)),
            ]
            + per_block,
            out_specs=pl.BlockSpec((8, 2 * rows), whole),
            scratch_shapes=[
                pltpu.VMEM((rows + 2 * rank, model), BF16),
                pltpu.VMEM((rows, 2 * rank), BF16),
                column,
                pltpu.VMEM((rows, 1), jnp.int32),
                column,
                column,
                column,
            ],
        ),
        out_shape=jax.ShapeDtypeStruct((8, 2 * rows), F32),
        compiler_params=pltpu.CompilerParams(vmem_limit_bytes=VMEM_LIMIT),
        cost_estimate=pl.CostEstimate(
            flops=4 * rows * model * vocab,
            transcendentals=2 * rows * vocab,
            bytes_accessed=2 * model * vocab,
        ),
        name="score",
    )(place, up, gain, head, *operands)


def shifted(value, ranks, step):
    return lax.ppermute(value, "tensor", [(i, (i + step) % ranks) for i in range(ranks)])


def partnered(value, ranks):
    return lax.ppermute(value, "tensor", [(i, i ^ 1) for i in range(ranks)])


def reduce_rows(branch, ranks):
    me = lax.axis_index("tensor")
    size = branch.shape[0] // (ranks // 2)

    def block(step):
        at = (me + step) % ranks // 2 * size
        return lax.dynamic_slice_in_dim(branch, at, size, 0)

    arrived = [shifted(block(step), ranks, step) for step in (ranks // 2, 2, ranks - 2)]
    total = block(0).astype(F32)
    for value in lax.optimization_barrier(arrived):
        total = total + value.astype(F32)
    return total.astype(BF16)


def crossed(value):
    return lax.ppermute(value, "seq", [(i, i ^ 1) for i in range(32)])


def turned(value, stage, step):
    def target(i):
        y, x, core = i // 8, i // 2 % 4, i % 2
        if core == stage:
            x = (x + step) % 4
        else:
            y = (y + step) % 4
        return y * 8 + x * 2 + core

    return lax.ppermute(value, "seq", [(i, target(i)) for i in range(32)])


def gather_pages(keys, values, chunks, ranks):
    first_core = lax.axis_index("seq") % 2 == 0
    kept = jnp.where(first_core, keys, values)
    sent = jnp.where(first_core, values, keys)
    pair = jnp.concatenate([kept, crossed(sent)])
    partner = [partnered(chunks[0], ranks)]
    line = [pair] + [turned(pair, 0, step) for step in (3, 2, 1)]
    line, partner[0] = lax.optimization_barrier((line, partner[0]))
    line = lax.optimization_barrier(jnp.concatenate(line))
    front, behind = turned(line, 1, 3), turned(line, 1, 1)
    near = crossed(line)
    sources = lax.optimization_barrier((chunks[1], line))
    partner.append(partnered(sources[0], ranks))
    front, behind, second = lax.optimization_barrier((front, behind, partner[1]))
    partner[1] = second
    middle = front.shape[0] // 2
    low, high = turned(behind[:middle], 1, 1), turned(front[middle:], 1, 3)
    sources = lax.optimization_barrier((chunks[2], front))
    partner.append(partnered(sources[0], ranks))
    far_front, far_behind = crossed(front), crossed(behind)
    low, high, third = lax.optimization_barrier((low, high, partner[2]))
    partner[2] = third
    sources = lax.optimization_barrier((chunks[3], low))
    partner.append(partnered(sources[0], ranks))
    pieces = [line, front, low, high, behind]
    pieces += [near, far_front, crossed(low), crossed(high), far_behind]
    return pieces, partner, front


def local(
    hidden,
    attention_norm_gain,
    query_key_value_weight,
    output_weight,
    adapter_down_weight,
    adapter_up_weight,
    final_norm_gain,
    head,
    prompt_key_slots,
    prompt_value_slots,
    counts,
    page_slot_index,
    owner,
    targets,
):
    tok_rows, model = hidden.shape
    rollouts_here = tok_rows // LEN
    width_here = output_weight.shape[0]
    heads_here = width_here // HEAD_WIDTH
    ranks = lax.axis_size("tensor")
    first = lax.axis_index("seq") * rollouts_here
    me = lax.axis_index("seq")
    rank = lax.axis_index("tensor")
    down = jnp.pad(adapter_down_weight, ((0, 0), (0, PAD - adapter_down_weight.shape[1])))
    cuts = (0, model // 6, model // 6 * 3, model // 6 * 4, model)
    chunks = [output_weight[:, a:b] for a, b in zip(cuts, cuts[1:])]
    chunks[-1] = jnp.concatenate([chunks[-1], down], axis=1)
    pieces, partner_chunks, stage = gather_pages(
        prompt_key_slots, prompt_value_slots, chunks, ranks
    )
    head_rows, _ = lax.optimization_barrier((head.T, stage))
    head_columns = lax.all_gather(head_rows, "seq", axis=0, tiled=True)

    groups_iota = jnp.arange(counts.shape[0], dtype=jnp.int32)
    my_groups = lax.dynamic_slice_in_dim(owner, first, rollouts_here, 0)
    my_pages = jnp.sum(
        jnp.where(my_groups[:, None] == groups_iota[None, :], counts[None, :], 0), axis=1
    )
    positions = jnp.repeat(my_pages, LEN) * PAGE + jnp.arange(tok_rows, dtype=jnp.int32) % LEN
    half = HEAD_WIDTH // 2
    place_in_head = jnp.arange(width_here, dtype=jnp.int32) % half
    frequency = 10000.0 ** (-place_in_head.astype(F32) * 2.0 / HEAD_WIDTH)
    angles = positions.astype(F32)[:, None] * frequency[None, :]
    qkv = project(
        hidden,
        attention_norm_gain[None, :],
        query_key_value_weight,
        jnp.cos(angles),
        jnp.sin(angles),
    )
    attended = attend(
        jnp.stack([first, me // 8, me // 2 % 4, me % 2]).astype(jnp.int32),
        counts,
        page_slot_index,
        owner,
        qkv,
        pieces,
    )
    branch = branch_part(
        lax.dynamic_index_in_dim(attended, rank % 2, 0, False),
        partnered(lax.dynamic_index_in_dim(attended, 1 - rank % 2, 0, False), ranks),
        chunks,
        partner_chunks,
    )
    mine = reduce_rows(branch, ranks)
    size = tok_rows // ranks
    half = size // 2
    head_columns = pltpu.with_memory_space_constraint(head_columns, pltpu.HBM)

    def score_blocks(places, blocks):
        return score(
            jnp.stack([rank] + places).astype(jnp.int32),
            hidden,
            adapter_up_weight,
            final_norm_gain[None, :],
            targets[:, None],
            head_columns,
            blocks,
        )

    def by_offset(offsets, part):
        part = part.reshape(8, 2, len(offsets), size)
        return {offset: part[:, :, n] for n, offset in enumerate(offsets)}

    def place(offset):
        return (rank + offset) % ranks

    near = [shifted(mine, ranks, step) for step in (-1, 1, -2, 2)]
    near = lax.optimization_barrier(near)
    _, _, after_two, before_two = near
    far = [
        shifted(after_two, ranks, -1),
        shifted(before_two, ranks, 1),
        shifted(after_two[:half], ranks, -2),
        shifted(before_two[half:], ranks, 2),
    ]
    near_offsets = (0, 1, ranks - 1, 2, ranks - 2)
    near_part = score_blocks([place(n) for n in near_offsets], [mine] + near)
    far, near_part = lax.optimization_barrier((far, near_part))
    far_offsets = (3, ranks - 3, ranks // 2)
    opposite = 2 * place(ranks // 2)
    far_part = score_blocks([place(3), place(ranks - 3), opposite, opposite + 1], far)
    stats = by_offset(near_offsets, near_part) | by_offset(far_offsets, far_part)
    line = jnp.stack([stats[k] for k in range(ranks)] * 2, axis=2)
    ordered = lax.dynamic_slice_in_dim(line, ranks - rank, ranks, 2).reshape(8, 2 * tok_rows)
    every = lax.all_to_all(
        jnp.broadcast_to(ordered[None], (ranks, 8, 2 * tok_rows)), "tensor", 0, 0, tiled=True
    )
    maxima, totals, picked = every[:, 0], every[:, 1], every[:, 2]
    largest = jnp.max(maxima, axis=0)
    total = jnp.sum(totals * jnp.exp(maxima - largest[None]), axis=0)
    log_probs = jnp.sum(picked, axis=0) - largest - jnp.log(total)
    return (log_probs[:tok_rows], log_probs[tok_rows:])


def solution(mesh):
    return jax.shard_map(
        local,
        mesh=mesh,
        in_specs=(
            P("seq", None),
            P(),
            P(None, None, "tensor"),
            P("tensor", None),
            P("tensor", None),
            P(),
            P(),
            P("tensor", "seq"),
            P("seq", None, "tensor"),
            P("seq", None, "tensor"),
            P(),
            P(),
            P(),
            P("seq"),
        ),
        out_specs=(P("seq"), P("seq")),
        check_vma=False,
    )
```

```python
import math

import jax
import jax.numpy as jnp
from jax import lax
from jax.experimental import pallas as pl
from jax.experimental.pallas import tpu as pltpu
from jax.sharding import PartitionSpec as P

HEAD_WIDTH = 96
LEN = 64
PAGE = 128
MAXP = 8


EPSILON = 1e-05
NEGATIVE = -1e30
PAD = 128
BLOCK = LEN // 2
VMEM_LIMIT = 28 * 1024 * 1024
F32 = jnp.float32
BF16 = jnp.bfloat16


def rms_norm(values, gain):
    mean_sq = jnp.mean(values * values, axis=-1, keepdims=True)
    return (values * lax.rsqrt(mean_sq + EPSILON) * gain.astype(F32)).astype(BF16)


def project_kernel(hidden_ref, gain_ref, weight_ref, cos_ref, sin_ref, out_ref, normed):
    part = pl.program_id(0)

    @pl.when(part == 0)
    def _():
        normed[...] = rms_norm(hidden_ref[...].astype(F32), gain_ref[...])

    product = jnp.dot(normed[...], weight_ref[0], preferred_element_type=F32)

    @pl.when(part < 2)
    def _():
        width = product.shape[1]
        half = HEAD_WIDTH // 2
        lane = lax.broadcasted_iota(jnp.int32, product.shape, 1) % HEAD_WIDTH
        partner = jnp.where(
            lane < half, -pltpu.roll(product, width - half, 1), pltpu.roll(product, half, 1)
        )
        out_ref[0] = (product * cos_ref[...] + partner * sin_ref[...]).astype(BF16)

    @pl.when(part == 2)
    def _():
        out_ref[0] = product.astype(BF16)


def project(hidden, gain, weight, cosine, sinus):
    rows, width = hidden.shape
    parts, _, cols = weight.shape
    whole = lambda i: (0, 0)
    return pl.pallas_call(
        project_kernel,
        grid=(parts,),
        in_specs=[
            pl.BlockSpec((rows, width), whole),
            pl.BlockSpec((1, width), whole),
            pl.BlockSpec((1, width, cols), lambda i: (i, 0, 0)),
            pl.BlockSpec((rows, cols), whole),
            pl.BlockSpec((rows, cols), whole),
        ],
        out_specs=pl.BlockSpec((1, rows, cols), lambda i: (i, 0, 0)),
        out_shape=jax.ShapeDtypeStruct((parts, rows, cols), BF16),
        scratch_shapes=[pltpu.VMEM((rows, width), BF16)],
        compiler_params=pltpu.CompilerParams(vmem_limit_bytes=VMEM_LIMIT),
        name="project",
    )(hidden, gain, weight, cosine, sinus)


def dot_nt(left, right):
    return lax.dot_general(left, right, (((1,), (1,)), ((), ())), preferred_element_type=F32)


def attend_kernel(*refs):
    first_ref, counts_ref, index_ref, owner_ref = refs[:4]
    qkv_ref, cached_values_ref = refs[4:6]
    out_ref, keys, values, sems = refs[-4:]
    pieces = refs[6:-4]
    rollouts = keys.shape[0]
    width = qkv_ref.shape[2]
    heads = width // HEAD_WIDTH
    scale = 1.0 / math.sqrt(HEAD_WIDTH)
    first = first_ref[0]
    my_y, my_x, my_core = first_ref[1], first_ref[2], first_ref[3]

    def start_copies(r, j):
        slot = index_ref[owner_ref[first + r] * MAXP + j]
        device, path = slot // 2, slot % 2
        down_y = (device // 8 - my_y + 4) % 4
        down_x = (device // 2 % 4 - my_x + 4) % 4
        far = jnp.where(path == 0, down_y, down_x)
        near = jnp.where(path == 0, down_x, down_y)
        at = near * 2 + (device % 2 != path).astype(jnp.int32)
        high = ((far == 2) & (at >= 4)).astype(jnp.int32)
        piece = far + high + (far == 3).astype(jnp.int32)
        piece = piece + 5 * (my_core != path).astype(jnp.int32)
        at = at - 4 * high
        rows = pl.ds(pl.multiple_of(j * PAGE, PAGE), PAGE)
        pltpu.make_async_copy(
            cached_values_ref.at[slot], values.at[r, rows], sems.at[r, 1, j]
        ).start()
        for p, ref in enumerate(pieces):

            @pl.when(piece == p)
            def _():
                row = jnp.minimum(at, ref.shape[0] - 1)
                pltpu.make_async_copy(ref.at[row], keys.at[r, rows], sems.at[r, 0, j]).start()

        return 0

    def live_pages(r):
        return counts_ref[owner_ref[first + r]]

    def covering(live):
        return jnp.where(live <= 2, 2, jnp.where(live <= 4, 4, MAXP))

    def start_rollout(r, _):
        return lax.fori_loop(0, covering(live_pages(r)), lambda j, _: start_copies(r, j), 0)

    lax.fori_loop(0, rollouts, start_rollout, 0)
    lane_head = lax.broadcasted_iota(jnp.int32, (LEN, width), 1) // HEAD_WIDTH
    own_row = lax.broadcasted_iota(jnp.int32, (heads * LEN, LEN), 0) % LEN
    own_col = lax.broadcasted_iota(jnp.int32, (heads * LEN, LEN), 1)

    def mix_rollout(r, _):
        live = live_pages(r)
        rows = pl.ds(pl.multiple_of(r * LEN, LEN), LEN)

        def mix(pages):
            query = qkv_ref[0, rows, :].astype(F32)
            stacked = jnp.concatenate(
                [jnp.where(lane_head == h, query, 0.0) for h in range(heads)], axis=0
            ).astype(BF16)
            own = dot_nt(stacked, qkv_ref[1, rows, :]) * scale
            own = jnp.where(own_col <= own_row, own, NEGATIVE)
            for j in range(pages):
                for which, buffer in enumerate((keys, values)):
                    pltpu.make_async_copy(
                        pieces[0].at[0],
                        buffer.at[r, pl.ds(j * PAGE, PAGE)],
                        sems.at[r, which, j],
                    ).wait()
            span = pl.ds(0, pages * PAGE)
            cached = dot_nt(stacked, keys[r, span]) * scale
            page_of = lax.broadcasted_iota(jnp.int32, cached.shape, 1) // PAGE
            cached = jnp.where(page_of < live, cached, NEGATIVE)
            largest = jnp.maximum(
                jnp.max(own, axis=1, keepdims=True), jnp.max(cached, axis=1, keepdims=True)
            )
            own = jnp.exp(own - largest)
            cached = jnp.exp(cached - largest)
            total = jnp.sum(own, axis=1, keepdims=True) + jnp.sum(cached, axis=1, keepdims=True)
            mixed = jnp.dot(
                cached.astype(BF16), values[r, span], preferred_element_type=F32
            ) + jnp.dot(own.astype(BF16), qkv_ref[2, rows, :], preferred_element_type=F32)
            mixed = mixed / total
            picked = jnp.zeros((LEN, width), F32)
            for h in range(heads):
                picked = jnp.where(lane_head == h, mixed[h * LEN : (h + 1) * LEN], picked)
            for parity in range(2):
                out_ref[parity, pl.ds(pl.multiple_of(r * BLOCK, BLOCK), BLOCK), :] = picked[
                    parity * BLOCK : (parity + 1) * BLOCK
                ].astype(BF16)

        for pages in (2, 4, MAXP):
            pl.when(covering(live) == pages)(lambda pages=pages: mix(pages))
        return 0

    lax.fori_loop(0, rollouts, mix_rollout, 0)


def attend(first, counts, index, owner, qkv, cached_values, pieces):
    _, rows, width = qkv.shape
    rollouts = rows // LEN
    vmem = pl.BlockSpec(memory_space=pltpu.VMEM)
    cached = [
        pltpu.with_memory_space_constraint(piece, pltpu.HBM) for piece in [cached_values] + pieces
    ]
    return pl.pallas_call(
        attend_kernel,
        grid_spec=pltpu.PrefetchScalarGridSpec(
            num_scalar_prefetch=4,
            grid=(),
            in_specs=[vmem] + [pl.BlockSpec(memory_space=pltpu.HBM)] * len(cached),
            out_specs=vmem,
            scratch_shapes=[
                pltpu.VMEM((rollouts, MAXP * PAGE, width), BF16),
                pltpu.VMEM((rollouts, MAXP * PAGE, width), BF16),
                pltpu.SemaphoreType.DMA((rollouts, 2, MAXP)),
            ],
        ),
        out_shape=jax.ShapeDtypeStruct((2, rows // 2, width), BF16),
        compiler_params=pltpu.CompilerParams(vmem_limit_bytes=VMEM_LIMIT),
        name="attend",
    )(first, counts, index, owner, qkv, *cached)


def branch_kernel(mine_ref, theirs_ref, own_ref, partner_ref, out_ref):
    out_ref[...] = (
        jnp.dot(mine_ref[...], own_ref[...], preferred_element_type=F32)
        + jnp.dot(theirs_ref[...], partner_ref[...], preferred_element_type=F32)
    ).astype(BF16)


def branch_part(mine, theirs, own, partner):
    rows, width = mine.shape
    columns = own.shape[1]
    tile = columns // 5
    own, partner = (pltpu.with_memory_space_constraint(w, pltpu.HBM) for w in (own, partner))
    whole = lambda i: (0, 0)
    across = lambda i: (0, i)
    return pl.pallas_call(
        branch_kernel,
        grid=(columns // tile,),
        in_specs=[pl.BlockSpec((rows, width), whole)] * 2
        + [pl.BlockSpec((width, tile), across)] * 2,
        out_specs=pl.BlockSpec((rows, tile), across),
        out_shape=jax.ShapeDtypeStruct((rows, columns), BF16),
        compiler_params=pltpu.CompilerParams(vmem_limit_bytes=VMEM_LIMIT),
        name="branch",
    )(mine, theirs, own, partner)


def two_parts(value):
    high = value.astype(BF16)
    return high, (value - high.astype(F32)).astype(BF16)


def score_kernel(*refs):
    place_ref, up_ref, gain_ref, head_ref = refs[:4]
    out_ref, normed, deltas, scales, wanted, logits, adapters, packed = refs[-8:]
    inputs = refs[4:-8]
    step = pl.program_id(0)
    steps, _, depth = normed.shape
    rank, model = up_ref.shape
    rows = deltas.shape[0]
    vocab = head_ref.shape[1]

    def store_normed(at, value):
        for k in range(steps):
            normed[k, at, :] = value[:, k * depth : (k + 1) * depth]

    @pl.when(step == 0)
    def _():
        start = 0
        gain = gain_ref[...].astype(F32)
        up = up_ref[...]
        for hidden_ref, target_ref, block in zip(inputs[::3], inputs[1::3], inputs[2::3]):
            at = slice(start, start + block.shape[0])
            start += block.shape[0]
            delta = block[:, model : model + rank]
            reference = hidden_ref[...].astype(F32) + block[:, :model].astype(F32)
            policy = reference + jnp.dot(delta, up, preferred_element_type=F32)
            reference_scale = lax.rsqrt(
                jnp.mean(reference * reference, axis=1, keepdims=True) + EPSILON
            )
            policy_scale = lax.rsqrt(jnp.mean(policy * policy, axis=1, keepdims=True) + EPSILON)
            store_normed(at, (reference * reference_scale * gain).astype(BF16))
            deltas[at, :] = jnp.concatenate([delta, delta], axis=1)
            scales[0, at, :] = policy_scale / reference_scale
            scales[1, at, :] = policy_scale
            wanted[at, :] = target_ref[...] - place_ref[0] * vocab
        high, low = two_parts(up.astype(F32) * gain)
        store_normed(slice(rows, rows + rank), high)
        store_normed(slice(rows + rank, rows + 2 * rank), low)
        logits[...] = jnp.zeros_like(logits)

    tile = 256

    def multiply(n, _):
        columns = pl.ds(pl.multiple_of(n * tile, tile), tile)
        logits[:, columns] += jnp.dot(
            normed[step], head_ref[:, columns], preferred_element_type=F32
        )
        return 0

    lax.fori_loop(0, vocab // tile, multiply, 0)

    @pl.when(step == steps - 1)
    def _():
        high, low = two_parts(logits[rows : rows + rank, :] + logits[rows + rank :, :])
        adapters[:rank, :] = high
        adapters[rank:, :] = low
        size = 32

        def summarize(n, _):
            at = pl.ds(pl.multiple_of(n * size, size), size)
            reference_logits = logits[at, :]
            adapted = jnp.dot(deltas[at, :], adapters[...], preferred_element_type=F32)
            policy_logits = scales[0, at, :] * reference_logits + scales[1, at, :] * adapted
            hit = lax.broadcasted_iota(jnp.int32, (size, vocab), 1) == wanted[at, :]
            lane = lax.broadcasted_iota(jnp.int32, (size, 128), 1)
            for which, here in enumerate((policy_logits, reference_logits)):
                picked = jnp.sum(jnp.where(hit, here, 0.0), axis=1, keepdims=True)
                largest = jnp.max(here, axis=1, keepdims=True)
                total = jnp.sum(jnp.exp(here - largest), axis=1, keepdims=True)
                packed[which, at, :] = jnp.where(
                    lane == 0, largest, jnp.where(lane == 1, total, picked)
                )
            return 0

        lax.fori_loop(0, rows // size, summarize, 0)
        out_ref[...] = jnp.transpose(packed[...].reshape(2 * rows, 128))[:8, :]


def score(place, hidden, up, gain, targets, head, blocks):
    model = hidden.shape[1]
    vocab = head.shape[1]
    rank = up.shape[0]
    rows = sum(block.shape[0] for block in blocks)
    steps = 4
    depth = model // steps
    whole = lambda i, p: (0, 0)
    per_block, operands = [], []
    for k, block in enumerate(blocks):
        size = block.shape[0]
        here = lambda i, p, k=k: (p[1 + k], 0)
        per_block += [
            pl.BlockSpec((size, model), here),
            pl.BlockSpec((size, 1), here),
            pl.BlockSpec(block.shape, whole),
        ]
        operands += [hidden, targets, block]
    return pl.pallas_call(
        score_kernel,
        grid_spec=pltpu.PrefetchScalarGridSpec(
            num_scalar_prefetch=1,
            grid=(steps,),
            in_specs=[
                pl.BlockSpec(up.shape, whole),
                pl.BlockSpec(gain.shape, whole),
                pl.BlockSpec((depth, vocab), lambda i, p: (i, 0)),
            ]
            + per_block,
            out_specs=pl.BlockSpec((8, 2 * rows), whole),
            scratch_shapes=[
                pltpu.VMEM((steps, rows + 2 * rank, depth), BF16),
                pltpu.VMEM((rows, 2 * rank), BF16),
                pltpu.VMEM((2, rows, 1), F32),
                pltpu.VMEM((rows, 1), jnp.int32),
                pltpu.VMEM((rows + 2 * rank, vocab), F32),
                pltpu.VMEM((2 * rank, vocab), BF16),
                pltpu.VMEM((2, rows, 128), F32),
            ],
        ),
        out_shape=jax.ShapeDtypeStruct((8, 2 * rows), F32),
        compiler_params=pltpu.CompilerParams(vmem_limit_bytes=VMEM_LIMIT),
        cost_estimate=pl.CostEstimate(
            flops=4 * rows * model * vocab,
            transcendentals=2 * rows * vocab,
            bytes_accessed=2 * model * vocab,
        ),
        name="score",
    )(place, up, gain, head, *operands)


def shifted(value, ranks, step):
    return lax.ppermute(value, "tensor", [(i, (i + step) % ranks) for i in range(ranks)])


def partnered(value, ranks):
    return lax.ppermute(value, "tensor", [(i, i ^ 1) for i in range(ranks)])


def reduce_rows(branch, ranks):
    me = lax.axis_index("tensor")
    size = branch.shape[0] // (ranks // 2)

    def block(step):
        at = (me + step) % ranks // 2 * size
        return lax.dynamic_slice_in_dim(branch, at, size, 0)

    arrived = [shifted(block(step), ranks, step) for step in (ranks // 2, 2, ranks - 2)]
    total = block(0).astype(F32)
    for value in lax.optimization_barrier(arrived):
        total = total + value.astype(F32)
    return total.astype(BF16)


def crossed(value):
    return lax.ppermute(value, "seq", [(i, i ^ 1) for i in range(32)])


def turned(value, stage, step):
    def target(i):
        y, x, core = i // 8, i // 2 % 4, i % 2
        if core == stage:
            x = (x + step) % 4
        else:
            y = (y + step) % 4
        return y * 8 + x * 2 + core

    return lax.ppermute(value, "seq", [(i, target(i)) for i in range(32)])


def gather_keys(keys, weights, project_now, ranks):
    core = lax.axis_index("seq") % 2
    kept = lax.dynamic_slice_in_dim(keys, core, 1, 0)
    sent = lax.dynamic_slice_in_dim(keys, 1 - core, 1, 0)
    pair = jnp.concatenate([kept, crossed(sent)])
    partner = partnered(weights, ranks)
    line = lax.optimization_barrier([pair] + [turned(pair, 0, step) for step in (3, 2, 1)])
    line = lax.optimization_barrier(jnp.concatenate(line))
    front, behind = turned(line, 1, 3), turned(line, 1, 1)
    near = crossed(line)
    front, behind, qkv = lax.optimization_barrier((front, behind, project_now()))
    middle = front.shape[0] // 2
    low, high = turned(behind[:middle], 1, 1), turned(front[middle:], 1, 3)
    far_front, far_behind = crossed(front), crossed(behind)
    low, high, partner = lax.optimization_barrier((low, high, partner))
    pieces = [line, front, low, high, behind]
    pieces += [near, far_front, crossed(low), crossed(high), far_behind]
    return pieces, partner, qkv


def local(
    hidden,
    attention_norm_gain,
    query_key_value_weight,
    output_weight,
    adapter_down_weight,
    adapter_up_weight,
    final_norm_gain,
    head,
    prompt_key_slots,
    prompt_value_slots,
    counts,
    page_slot_index,
    owner,
    targets,
):
    tok_rows, model = hidden.shape
    rollouts_here = tok_rows // LEN
    width_here = output_weight.shape[0]
    heads_here = width_here // HEAD_WIDTH
    ranks = lax.axis_size("tensor")
    first = lax.axis_index("seq") * rollouts_here
    me = lax.axis_index("seq")
    rank = lax.axis_index("tensor")
    down = jnp.pad(adapter_down_weight, ((0, 0), (0, PAD - adapter_down_weight.shape[1])))
    weights = jnp.concatenate([output_weight, down], axis=1)
    cached_values = lax.all_gather(prompt_value_slots, "seq", axis=0, tiled=True)
    groups_iota = jnp.arange(counts.shape[0], dtype=jnp.int32)
    my_groups = lax.dynamic_slice_in_dim(owner, first, rollouts_here, 0)
    my_pages = jnp.sum(
        jnp.where(my_groups[:, None] == groups_iota[None, :], counts[None, :], 0), axis=1
    )
    positions = jnp.repeat(my_pages, LEN) * PAGE + jnp.arange(tok_rows, dtype=jnp.int32) % LEN
    half = HEAD_WIDTH // 2
    place_in_head = jnp.arange(width_here, dtype=jnp.int32) % half
    frequency = 10000.0 ** (-place_in_head.astype(F32) * 2.0 / HEAD_WIDTH)
    angles = positions.astype(F32)[:, None] * frequency[None, :]
    pieces, partner_weights, qkv = gather_keys(
        prompt_key_slots,
        weights,
        lambda: project(
            hidden,
            attention_norm_gain[None, :],
            query_key_value_weight,
            jnp.cos(angles),
            jnp.sin(angles),
        ),
        ranks,
    )
    head_rows, cached_values, pieces = lax.optimization_barrier((head.T, cached_values, pieces))
    head_columns = lax.all_gather(head_rows, "seq", axis=0, tiled=True)
    attended = attend(
        jnp.stack([first, me // 8, me // 2 % 4, me % 2]).astype(jnp.int32),
        counts,
        page_slot_index,
        owner,
        qkv,
        cached_values,
        pieces,
    )
    branch = branch_part(
        lax.dynamic_index_in_dim(attended, rank % 2, 0, False),
        partnered(lax.dynamic_index_in_dim(attended, 1 - rank % 2, 0, False), ranks),
        weights,
        partner_weights,
    )
    mine = reduce_rows(branch, ranks)
    size = tok_rows // ranks
    half = size // 2
    head_columns = pltpu.with_memory_space_constraint(head_columns, pltpu.HBM)

    def score_blocks(places, blocks):
        return score(
            jnp.stack([rank] + places).astype(jnp.int32),
            hidden,
            adapter_up_weight,
            final_norm_gain[None, :],
            targets[:, None],
            head_columns,
            blocks,
        )

    def by_offset(offsets, part):
        part = part.reshape(8, 2, len(offsets), size)
        return {offset: part[:, :, n] for n, offset in enumerate(offsets)}

    def place(offset):
        return (rank + offset) % ranks

    near = [shifted(mine, ranks, step) for step in (-1, 1, -2, 2)]
    near = lax.optimization_barrier(near)
    _, _, after_two, before_two = near
    far = [
        shifted(after_two, ranks, -1),
        shifted(before_two, ranks, 1),
        shifted(after_two[:half], ranks, -2),
        shifted(before_two[half:], ranks, 2),
    ]
    near_offsets = (0, 1, ranks - 1, 2, ranks - 2)
    near_part = score_blocks([place(n) for n in near_offsets], [mine] + near)
    far, near_part = lax.optimization_barrier((far, near_part))
    far_offsets = (3, ranks - 3, ranks // 2)
    opposite = 2 * place(ranks // 2)
    far_part = score_blocks([place(3), place(ranks - 3), opposite, opposite + 1], far)
    stats = by_offset(near_offsets, near_part) | by_offset(far_offsets, far_part)
    line = jnp.stack([stats[k] for k in range(ranks)] * 2, axis=2)
    ordered = lax.dynamic_slice_in_dim(line, ranks - rank, ranks, 2).reshape(8, 2 * tok_rows)
    every = lax.all_to_all(
        jnp.broadcast_to(ordered[None], (ranks, 8, 2 * tok_rows)), "tensor", 0, 0, tiled=True
    )
    maxima, totals, picked = every[:, 0], every[:, 1], every[:, 2]
    largest = jnp.max(maxima, axis=0)
    total = jnp.sum(totals * jnp.exp(maxima - largest[None]), axis=0)
    log_probs = jnp.sum(picked, axis=0) - largest - jnp.log(total)
    return (log_probs[:tok_rows], log_probs[tok_rows:])


def solution(mesh):
    return jax.shard_map(
        local,
        mesh=mesh,
        in_specs=(
            P("seq", None),
            P(),
            P(None, None, "tensor"),
            P("tensor", None),
            P("tensor", None),
            P(),
            P(),
            P("tensor", "seq"),
            P("seq", None, "tensor"),
            P("seq", None, "tensor"),
            P(),
            P(),
            P(),
            P("seq"),
        ),
        out_specs=(P("seq"), P("seq")),
        check_vma=False,
    )
```

```python
import math

import jax
import jax.numpy as jnp
from jax import lax
from jax.experimental import pallas as pl
from jax.experimental.pallas import tpu as pltpu
from jax.sharding import PartitionSpec as P

HEAD_WIDTH = 96
LEN = 64
PAGE = 128
MAXP = 8


EPSILON = 1e-05
NEGATIVE = -1e30
PAD = 128
BLOCK = LEN // 2
VMEM_LIMIT = 28 * 1024 * 1024
F32 = jnp.float32
BF16 = jnp.bfloat16


def rms_norm(values, gain):
    mean_sq = jnp.mean(values * values, axis=-1, keepdims=True)
    return (values * lax.rsqrt(mean_sq + EPSILON) * gain.astype(F32)).astype(BF16)


def project_kernel(hidden_ref, gain_ref, weight_ref, cos_ref, sin_ref, out_ref, normed):
    part = pl.program_id(0)

    @pl.when(part == 0)
    def _():
        normed[...] = rms_norm(hidden_ref[...].astype(F32), gain_ref[...])

    product = jnp.dot(normed[...], weight_ref[0], preferred_element_type=F32)

    @pl.when(part < 2)
    def _():
        width = product.shape[1]
        half = HEAD_WIDTH // 2
        lane = lax.broadcasted_iota(jnp.int32, product.shape, 1) % HEAD_WIDTH
        partner = jnp.where(
            lane < half, -pltpu.roll(product, width - half, 1), pltpu.roll(product, half, 1)
        )
        out_ref[0] = (product * cos_ref[...] + partner * sin_ref[...]).astype(BF16)

    @pl.when(part == 2)
    def _():
        out_ref[0] = product.astype(BF16)


def project(hidden, gain, weight, cosine, sinus):
    rows, width = hidden.shape
    parts, _, cols = weight.shape
    whole = lambda i: (0, 0)
    return pl.pallas_call(
        project_kernel,
        grid=(parts,),
        in_specs=[
            pl.BlockSpec((rows, width), whole),
            pl.BlockSpec((1, width), whole),
            pl.BlockSpec((1, width, cols), lambda i: (i, 0, 0)),
            pl.BlockSpec((rows, cols), whole),
            pl.BlockSpec((rows, cols), whole),
        ],
        out_specs=pl.BlockSpec((1, rows, cols), lambda i: (i, 0, 0)),
        out_shape=jax.ShapeDtypeStruct((parts, rows, cols), BF16),
        scratch_shapes=[pltpu.VMEM((rows, width), BF16)],
        compiler_params=pltpu.CompilerParams(vmem_limit_bytes=VMEM_LIMIT),
        name="project",
    )(hidden, gain, weight, cosine, sinus)


def dot_nt(left, right):
    return lax.dot_general(left, right, (((1,), (1,)), ((), ())), preferred_element_type=F32)


def attend_kernel(*refs):
    first_ref, counts_ref, index_ref, owner_ref = refs[:4]
    qkv_ref, cached_values_ref = refs[4:6]
    out_ref, keys, values, sems = refs[-4:]
    pieces = refs[6:-4]
    rollouts = keys.shape[0]
    width = qkv_ref.shape[2]
    heads = width // HEAD_WIDTH
    scale = 1.0 / math.sqrt(HEAD_WIDTH)
    first = first_ref[0]
    my_y, my_x, my_core = first_ref[1], first_ref[2], first_ref[3]

    def start_copies(r, j):
        slot = index_ref[owner_ref[first + r] * MAXP + j]
        device, path = slot // 2, slot % 2
        down_y = (device // 8 - my_y + 4) % 4
        down_x = (device // 2 % 4 - my_x + 4) % 4
        far = jnp.where(path == 0, down_y, down_x)
        near = jnp.where(path == 0, down_x, down_y)
        at = near * 2 + (device % 2 != path).astype(jnp.int32)
        piece = far + 4 * (my_core != path).astype(jnp.int32)
        rows = pl.ds(pl.multiple_of(j * PAGE, PAGE), PAGE)
        pltpu.make_async_copy(
            cached_values_ref.at[slot], values.at[r, rows], sems.at[r, 1, j]
        ).start()
        for p, ref in enumerate(pieces):

            @pl.when(piece == p)
            def _():
                pltpu.make_async_copy(ref.at[at], keys.at[r, rows], sems.at[r, 0, j]).start()

        return 0

    def live_pages(r):
        return counts_ref[owner_ref[first + r]]

    def covering(live):
        return jnp.where(live <= 2, 2, jnp.where(live <= 4, 4, MAXP))

    def start_rollout(r, _):
        return lax.fori_loop(0, covering(live_pages(r)), lambda j, _: start_copies(r, j), 0)

    lax.fori_loop(0, rollouts, start_rollout, 0)
    lane_head = lax.broadcasted_iota(jnp.int32, (LEN, width), 1) // HEAD_WIDTH
    own_row = lax.broadcasted_iota(jnp.int32, (heads * LEN, LEN), 0) % LEN
    own_col = lax.broadcasted_iota(jnp.int32, (heads * LEN, LEN), 1)

    def mix_rollout(r, _):
        live = live_pages(r)
        rows = pl.ds(pl.multiple_of(r * LEN, LEN), LEN)

        def mix(pages):
            query = qkv_ref[0, rows, :].astype(F32)
            stacked = jnp.concatenate(
                [jnp.where(lane_head == h, query, 0.0) for h in range(heads)], axis=0
            ).astype(BF16)
            own = dot_nt(stacked, qkv_ref[1, rows, :]) * scale
            own = jnp.where(own_col <= own_row, own, NEGATIVE)
            for j in range(pages):
                for which, buffer in enumerate((keys, values)):
                    pltpu.make_async_copy(
                        pieces[0].at[0],
                        buffer.at[r, pl.ds(j * PAGE, PAGE)],
                        sems.at[r, which, j],
                    ).wait()
            span = pl.ds(0, pages * PAGE)
            cached = dot_nt(stacked, keys[r, span]) * scale
            page_of = lax.broadcasted_iota(jnp.int32, cached.shape, 1) // PAGE
            cached = jnp.where(page_of < live, cached, NEGATIVE)
            largest = jnp.maximum(
                jnp.max(own, axis=1, keepdims=True), jnp.max(cached, axis=1, keepdims=True)
            )
            own = jnp.exp(own - largest)
            cached = jnp.exp(cached - largest)
            total = jnp.sum(own, axis=1, keepdims=True) + jnp.sum(cached, axis=1, keepdims=True)
            mixed = jnp.dot(
                cached.astype(BF16), values[r, span], preferred_element_type=F32
            ) + jnp.dot(own.astype(BF16), qkv_ref[2, rows, :], preferred_element_type=F32)
            mixed = mixed / total
            picked = jnp.zeros((LEN, width), F32)
            for h in range(heads):
                picked = jnp.where(lane_head == h, mixed[h * LEN : (h + 1) * LEN], picked)
            for parity in range(2):
                out_ref[parity, pl.ds(pl.multiple_of(r * BLOCK, BLOCK), BLOCK), :] = picked[
                    parity * BLOCK : (parity + 1) * BLOCK
                ].astype(BF16)

        for pages in (2, 4, MAXP):
            pl.when(covering(live) == pages)(lambda pages=pages: mix(pages))
        return 0

    lax.fori_loop(0, rollouts, mix_rollout, 0)


def attend(first, counts, index, owner, qkv, cached_values, pieces):
    _, rows, width = qkv.shape
    rollouts = rows // LEN
    vmem = pl.BlockSpec(memory_space=pltpu.VMEM)
    cached = [
        pltpu.with_memory_space_constraint(piece, pltpu.HBM) for piece in [cached_values] + pieces
    ]
    return pl.pallas_call(
        attend_kernel,
        grid_spec=pltpu.PrefetchScalarGridSpec(
            num_scalar_prefetch=4,
            grid=(),
            in_specs=[vmem] + [pl.BlockSpec(memory_space=pltpu.HBM)] * len(cached),
            out_specs=vmem,
            scratch_shapes=[
                pltpu.VMEM((rollouts, MAXP * PAGE, width), BF16),
                pltpu.VMEM((rollouts, MAXP * PAGE, width), BF16),
                pltpu.SemaphoreType.DMA((rollouts, 2, MAXP)),
            ],
        ),
        out_shape=jax.ShapeDtypeStruct((2, rows // 2, width), BF16),
        compiler_params=pltpu.CompilerParams(vmem_limit_bytes=VMEM_LIMIT),
        name="attend",
    )(first, counts, index, owner, qkv, *cached)


def two_parts(value):
    high = value.astype(BF16)
    return high, (value - high.astype(F32)).astype(BF16)


def settle_kernel(place_ref, hidden_ref, up_ref, gain_ref, *refs):
    *parts, out_ref = refs
    model = hidden_ref.shape[1]
    rank = up_ref.shape[0]
    total = parts[0][...].astype(F32)
    for part in parts[1:]:
        total = total + part[...].astype(F32)
    reference = hidden_ref[...].astype(F32) + total[:, :model]
    delta = total[:, model:]
    high, low = two_parts(delta)
    policy = (
        reference
        + jnp.dot(high[:, :rank], up_ref[...], preferred_element_type=F32)
        + jnp.dot(low[:, :rank], up_ref[...], preferred_element_type=F32)
    )
    reference_scale = lax.rsqrt(jnp.mean(reference * reference, axis=1, keepdims=True) + EPSILON)
    policy_scale = lax.rsqrt(jnp.mean(policy * policy, axis=1, keepdims=True) + EPSILON)
    out_ref[:, :model] = (reference * reference_scale * gain_ref[...].astype(F32)).astype(BF16)
    lane = lax.broadcasted_iota(jnp.int32, delta.shape, 1)
    beside = high.astype(F32) + pltpu.roll(low.astype(F32), rank, 1)
    at = 2 * rank
    for scale in (policy_scale / reference_scale, policy_scale):
        for _ in range(3):
            part = scale.astype(BF16).astype(F32)
            beside = jnp.where(lane == at, part, beside)
            scale = scale - part
            at += 1
    out_ref[:, model:] = beside.astype(BF16)


def settle(place, hidden, up, gain, *parts):
    whole = lambda i, p: (0, 0)
    size, width = parts[0].shape
    return pl.pallas_call(
        settle_kernel,
        grid_spec=pltpu.PrefetchScalarGridSpec(
            num_scalar_prefetch=1,
            grid=(1,),
            in_specs=[
                pl.BlockSpec((size, hidden.shape[1]), lambda i, p: (p[0], 0)),
                pl.BlockSpec(up.shape, whole),
                pl.BlockSpec(gain.shape, whole),
            ]
            + [pl.BlockSpec(part.shape, whole) for part in parts],
            out_specs=pl.BlockSpec((size, width), whole),
        ),
        out_shape=jax.ShapeDtypeStruct((size, width), BF16),
        compiler_params=pltpu.CompilerParams(vmem_limit_bytes=VMEM_LIMIT),
        name="settle",
    )(place, hidden, up, gain, *parts)


def score_kernel(*refs):
    place_ref, up_ref, gain_ref, head_ref = refs[:4]
    out_ref, normed, deltas, scales, wanted, largest, total, picked = refs[-8:]
    inputs = refs[4:-8]
    step = pl.program_id(0)
    rank, model = up_ref.shape
    rows = deltas.shape[0]
    tile = head_ref.shape[1]

    @pl.when(step == 0)
    def _():
        start = 0
        for target_ref, block in zip(inputs[::2], inputs[1::2]):
            at = slice(start, start + block.shape[0])
            start += block.shape[0]
            normed[at, :] = block[:, :model]
            beside = block[:, model:]
            deltas[at, :] = beside[:, : 2 * rank]
            beside = beside.astype(F32)
            lane = lax.broadcasted_iota(jnp.int32, beside.shape, 1) - 2 * rank
            for which in range(2):
                parts = (lane >= 3 * which) & (lane < 3 * which + 3)
                scales[which, at, :] = jnp.sum(
                    jnp.where(parts, beside, 0.0), axis=1, keepdims=True
                )
            wanted[at, :] = target_ref[...] - place_ref[0] * pl.num_programs(0) * tile
        high, low = two_parts(up_ref[...].astype(F32) * gain_ref[...].astype(F32))
        normed[rows : rows + rank, :] = high
        normed[rows + rank :, :] = low
        largest[...] = jnp.full_like(largest, NEGATIVE)
        total[...] = jnp.zeros_like(total)
        picked[...] = jnp.zeros_like(picked)

    product = jnp.dot(normed[...], head_ref[...], preferred_element_type=F32)
    reference_logits = product[:rows]
    adapted = jnp.zeros_like(reference_logits)
    for part in two_parts(product[rows : rows + rank] + product[rows + rank :]):
        adapted += jnp.dot(
            deltas[...], jnp.concatenate([part, part], axis=0), preferred_element_type=F32
        )
    policy_logits = scales[0] * reference_logits + scales[1] * adapted
    columns = lax.broadcasted_iota(jnp.int32, reference_logits.shape, 1)
    hit = columns == wanted[...] - step * tile
    for which, logits in enumerate((policy_logits, reference_logits)):
        picked[which] += jnp.sum(jnp.where(hit, logits, 0.0), axis=1, keepdims=True)
        before = largest[which]
        after = jnp.maximum(before, jnp.max(logits, axis=1, keepdims=True))
        total[which] = total[which] * jnp.exp(before - after) + jnp.sum(
            jnp.exp(logits - after), axis=1, keepdims=True
        )
        largest[which] = after

    @pl.when(step == pl.num_programs(0) - 1)
    def _():
        lane = lax.broadcasted_iota(jnp.int32, (2, rows, 128), 2)
        packed = jnp.where(
            lane == 0, largest[...], jnp.where(lane == 1, total[...], picked[...])
        )
        out_ref[...] = jnp.transpose(packed.reshape(2 * rows, 128))[:8, :]


def score(place, up, gain, targets, head, blocks):
    rank, model = up.shape
    vocab = head.shape[1]
    rows = sum(block.shape[0] for block in blocks)
    tile = 512
    whole = lambda i, p: (0, 0)
    per_block, operands = [], []
    for k, block in enumerate(blocks):
        per_block += [
            pl.BlockSpec((block.shape[0], 1), lambda i, p, k=k: (p[1 + k], 0)),
            pl.BlockSpec(block.shape, whole),
        ]
        operands += [targets, block]
    column = pltpu.VMEM((2, rows, 1), F32)
    return pl.pallas_call(
        score_kernel,
        grid_spec=pltpu.PrefetchScalarGridSpec(
            num_scalar_prefetch=1,
            grid=(vocab // tile,),
            in_specs=[
                pl.BlockSpec(up.shape, whole),
                pl.BlockSpec(gain.shape, whole),
                pl.BlockSpec((model, tile), lambda i, p: (0, i)),
            ]
            + per_block,
            out_specs=pl.BlockSpec((8, 2 * rows), whole),
            scratch_shapes=[
                pltpu.VMEM((rows + 2 * rank, model), BF16),
                pltpu.VMEM((rows, 2 * rank), BF16),
                column,
                pltpu.VMEM((rows, 1), jnp.int32),
                column,
                column,
                column,
            ],
        ),
        out_shape=jax.ShapeDtypeStruct((8, 2 * rows), F32),
        compiler_params=pltpu.CompilerParams(vmem_limit_bytes=VMEM_LIMIT),
        cost_estimate=pl.CostEstimate(
            flops=4 * rows * model * vocab,
            transcendentals=2 * rows * vocab,
            bytes_accessed=2 * model * vocab,
        ),
        name="score",
    )(place, up, gain, head, *operands)


def shifted(value, ranks, step):
    return lax.ppermute(value, "tensor", [(i, (i + step) % ranks) for i in range(ranks)])


def partnered(value, ranks):
    return lax.ppermute(value, "tensor", [(i, i ^ 1) for i in range(ranks)])


def reduce_rows(branch, ranks):
    me = lax.axis_index("tensor")
    size = branch.shape[0] // (ranks // 2)

    def block(step):
        at = (me + step) % ranks // 2 * size
        return lax.dynamic_slice_in_dim(branch, at, size, 0)

    arrived = [shifted(block(step), ranks, step) for step in (ranks // 2, 2, ranks - 2)]
    return [block(0)] + list(lax.optimization_barrier(arrived))


def crossed(value):
    return lax.ppermute(value, "seq", [(i, i ^ 1) for i in range(32)])


def turned(value, stage, step):
    def target(i):
        y, x, core = i // 8, i // 2 % 4, i % 2
        if core == stage:
            x = (x + step) % 4
        else:
            y = (y + step) % 4
        return y * 8 + x * 2 + core

    return lax.ppermute(value, "seq", [(i, target(i)) for i in range(32)])


def gather_keys(keys, weights, project_now, ranks):
    core = lax.axis_index("seq") % 2
    kept = lax.dynamic_slice_in_dim(keys, core, 1, 0)
    sent = lax.dynamic_slice_in_dim(keys, 1 - core, 1, 0)
    pair = jnp.concatenate([kept, crossed(sent)])
    partner = partnered(weights, ranks)
    line = lax.optimization_barrier([pair] + [turned(pair, 0, step) for step in (3, 2, 1)])
    line = lax.optimization_barrier(jnp.concatenate(line))
    ahead = [turned(line, 1, step) for step in (3, 2, 1)]
    near = crossed(line)
    ahead, qkv = lax.optimization_barrier((ahead, project_now()))
    pieces = [line] + ahead + [near] + [crossed(piece) for piece in ahead]
    return pieces, partner, qkv


def local(
    hidden,
    attention_norm_gain,
    query_key_value_weight,
    output_weight,
    adapter_down_weight,
    adapter_up_weight,
    final_norm_gain,
    head,
    prompt_key_slots,
    prompt_value_slots,
    counts,
    page_slot_index,
    owner,
    targets,
):
    tok_rows, model = hidden.shape
    rollouts_here = tok_rows // LEN
    width_here = output_weight.shape[0]
    heads_here = width_here // HEAD_WIDTH
    ranks = lax.axis_size("tensor")
    first = lax.axis_index("seq") * rollouts_here
    me = lax.axis_index("seq")
    rank = lax.axis_index("tensor")
    down = jnp.pad(adapter_down_weight, ((0, 0), (0, PAD - adapter_down_weight.shape[1])))
    weights = jnp.concatenate([output_weight, down], axis=1)
    cached_values = lax.all_gather(prompt_value_slots, "seq", axis=0, tiled=True)
    groups_iota = jnp.arange(counts.shape[0], dtype=jnp.int32)
    my_groups = lax.dynamic_slice_in_dim(owner, first, rollouts_here, 0)
    my_pages = jnp.sum(
        jnp.where(my_groups[:, None] == groups_iota[None, :], counts[None, :], 0), axis=1
    )
    positions = jnp.repeat(my_pages, LEN) * PAGE + jnp.arange(tok_rows, dtype=jnp.int32) % LEN
    half = HEAD_WIDTH // 2
    place_in_head = jnp.arange(width_here, dtype=jnp.int32) % half
    frequency = 10000.0 ** (-place_in_head.astype(F32) * 2.0 / HEAD_WIDTH)
    angles = positions.astype(F32)[:, None] * frequency[None, :]
    pieces, partner_weights, qkv = gather_keys(
        prompt_key_slots,
        weights,
        lambda: project(
            hidden,
            attention_norm_gain[None, :],
            query_key_value_weight,
            jnp.cos(angles),
            jnp.sin(angles),
        ),
        ranks,
    )
    head_rows, cached_values, pieces, partner_weights = lax.optimization_barrier(
        (head.T, cached_values, pieces, partner_weights)
    )
    head_columns = lax.all_gather(head_rows, "seq", axis=0, tiled=True)
    attended = attend(
        jnp.stack([first, me // 8, me // 2 % 4, me % 2]).astype(jnp.int32),
        counts,
        page_slot_index,
        owner,
        qkv,
        cached_values,
        pieces,
    )
    theirs = partnered(lax.dynamic_index_in_dim(attended, 1 - rank % 2, 0, False), ranks)
    own = lax.dynamic_index_in_dim(attended, rank % 2, 0, False)
    branch = jnp.dot(own, weights, preferred_element_type=F32)
    branch = branch + jnp.dot(theirs, partner_weights, preferred_element_type=F32)
    branch = branch.astype(BF16)
    mine = settle(
        rank[None].astype(jnp.int32),
        hidden,
        adapter_up_weight,
        final_norm_gain[None, :],
        *reduce_rows(branch, ranks),
    )
    size = tok_rows // ranks
    half = size // 2
    head_columns = pltpu.with_memory_space_constraint(head_columns, pltpu.HBM)

    def score_blocks(places, blocks):
        return score(
            jnp.stack([rank] + places).astype(jnp.int32),
            adapter_up_weight,
            final_norm_gain[None, :],
            targets[:, None],
            head_columns,
            blocks,
        )

    def by_offset(offsets, part):
        part = part.reshape(8, 2, len(offsets), size)
        return {offset: part[:, :, n] for n, offset in enumerate(offsets)}

    def place(offset):
        return (rank + offset) % ranks

    near = [shifted(mine, ranks, step) for step in (-1, 1, -2, 2)]
    near = lax.optimization_barrier(near)
    _, _, after_two, before_two = near
    far = [
        shifted(after_two, ranks, -1),
        shifted(before_two, ranks, 1),
        shifted(after_two[:half], ranks, -2),
        shifted(before_two[half:], ranks, 2),
    ]
    near_offsets = (0, 1, ranks - 1, 2, ranks - 2)
    near_part = score_blocks([place(n) for n in near_offsets], [mine] + near)
    far, near_part = lax.optimization_barrier((far, near_part))
    far_offsets = (3, ranks - 3, ranks // 2)
    opposite = 2 * place(ranks // 2)
    far_part = score_blocks([place(3), place(ranks - 3), opposite, opposite + 1], far)
    stats = by_offset(near_offsets, near_part) | by_offset(far_offsets, far_part)
    line = jnp.stack([stats[k] for k in range(ranks)] * 2, axis=2)
    ordered = lax.dynamic_slice_in_dim(line, ranks - rank, ranks, 2).reshape(8, 2 * tok_rows)
    every = lax.all_to_all(
        jnp.broadcast_to(ordered[None], (ranks, 8, 2 * tok_rows)), "tensor", 0, 0, tiled=True
    )
    maxima, totals, picked = every[:, 0], every[:, 1], every[:, 2]
    largest = jnp.max(maxima, axis=0)
    total = jnp.sum(totals * jnp.exp(maxima - largest[None]), axis=0)
    log_probs = jnp.sum(picked, axis=0) - largest - jnp.log(total)
    return (log_probs[:tok_rows], log_probs[tok_rows:])


def solution(mesh):
    return jax.shard_map(
        local,
        mesh=mesh,
        in_specs=(
            P("seq", None),
            P(),
            P(None, None, "tensor"),
            P("tensor", None),
            P("tensor", None),
            P(),
            P(),
            P("tensor", "seq"),
            P("seq", None, "tensor"),
            P("seq", None, "tensor"),
            P(),
            P(),
            P(),
            P("seq"),
        ),
        out_specs=(P("seq"), P("seq")),
        check_vma=False,
    )
```

```python
import math

import jax
import jax.numpy as jnp
from jax import lax
from jax.experimental import pallas as pl
from jax.experimental.pallas import tpu as pltpu
from jax.sharding import PartitionSpec as P

HEAD_WIDTH = 96
LEN = 64
PAGE = 128
MAXP = 8


EPSILON = 1e-05
NEGATIVE = -1e30
PAD = 128
BLOCK = LEN // 2
VMEM_LIMIT = 28 * 1024 * 1024
F32 = jnp.float32
BF16 = jnp.bfloat16


def rms_norm(values, gain):
    mean_sq = jnp.mean(values * values, axis=-1, keepdims=True)
    return (values * lax.rsqrt(mean_sq + EPSILON) * gain.astype(F32)).astype(BF16)


def project_kernel(hidden_ref, gain_ref, weight_ref, cos_ref, sin_ref, out_ref, normed):
    part = pl.program_id(0)

    @pl.when(part == 0)
    def _():
        normed[...] = rms_norm(hidden_ref[...].astype(F32), gain_ref[...])

    product = jnp.dot(normed[...], weight_ref[0], preferred_element_type=F32)

    @pl.when(part < 2)
    def _():
        width = product.shape[1]
        half = HEAD_WIDTH // 2
        lane = lax.broadcasted_iota(jnp.int32, product.shape, 1) % HEAD_WIDTH
        partner = jnp.where(
            lane < half, -pltpu.roll(product, width - half, 1), pltpu.roll(product, half, 1)
        )
        out_ref[0] = (product * cos_ref[...] + partner * sin_ref[...]).astype(BF16)

    @pl.when(part == 2)
    def _():
        out_ref[0] = product.astype(BF16)


def project(hidden, gain, weight, cosine, sinus):
    rows, width = hidden.shape
    parts, _, cols = weight.shape
    whole = lambda i: (0, 0)
    return pl.pallas_call(
        project_kernel,
        grid=(parts,),
        in_specs=[
            pl.BlockSpec((rows, width), whole),
            pl.BlockSpec((1, width), whole),
            pl.BlockSpec((1, width, cols), lambda i: (i, 0, 0)),
            pl.BlockSpec((rows, cols), whole),
            pl.BlockSpec((rows, cols), whole),
        ],
        out_specs=pl.BlockSpec((1, rows, cols), lambda i: (i, 0, 0)),
        out_shape=jax.ShapeDtypeStruct((parts, rows, cols), BF16),
        scratch_shapes=[pltpu.VMEM((rows, width), BF16)],
        compiler_params=pltpu.CompilerParams(vmem_limit_bytes=VMEM_LIMIT),
        name="project",
    )(hidden, gain, weight, cosine, sinus)


def dot_nt(left, right):
    return lax.dot_general(left, right, (((1,), (1,)), ((), ())), preferred_element_type=F32)


def attend_kernel(*refs):
    first_ref, counts_ref, index_ref, owner_ref = refs[:4]
    qkv_ref = refs[4]
    out_ref, keys, values, sems = refs[-4:]
    pieces = refs[5:-4]
    rollouts = keys.shape[0]
    width = qkv_ref.shape[2]
    heads = width // HEAD_WIDTH
    scale = 1.0 / math.sqrt(HEAD_WIDTH)
    first = first_ref[0]
    my_y, my_x, my_core = first_ref[1], first_ref[2], first_ref[3]

    def start_copies(r, j):
        slot = index_ref[owner_ref[first + r] * MAXP + j]
        device = slot // 2
        down_y = (device // 8 - my_y + 4) % 4
        down_x = (device // 2 % 4 - my_x + 4) % 4
        rows = pl.ds(pl.multiple_of(j * PAGE, PAGE), PAGE)
        for path, (buffer, far, near) in enumerate(
            ((keys, down_y, down_x), (values, down_x, down_y))
        ):
            at = near * 4 + 2 * (device % 2 != path).astype(jnp.int32) + slot % 2
            piece = far + 4 * (my_core != path).astype(jnp.int32)
            for p, ref in enumerate(pieces):

                @pl.when(piece == p)
                def _():
                    pltpu.make_async_copy(
                        ref.at[at], buffer.at[r, rows], sems.at[r, path, j]
                    ).start()

        return 0

    def live_pages(r):
        return counts_ref[owner_ref[first + r]]

    def covering(live):
        return jnp.where(live <= 2, 2, jnp.where(live <= 4, 4, MAXP))

    def start_rollout(r, _):
        return lax.fori_loop(0, covering(live_pages(r)), lambda j, _: start_copies(r, j), 0)

    lax.fori_loop(0, rollouts, start_rollout, 0)
    lane_head = lax.broadcasted_iota(jnp.int32, (LEN, width), 1) // HEAD_WIDTH
    own_row = lax.broadcasted_iota(jnp.int32, (heads * LEN, LEN), 0) % LEN
    own_col = lax.broadcasted_iota(jnp.int32, (heads * LEN, LEN), 1)

    def mix_rollout(r, _):
        live = live_pages(r)
        rows = pl.ds(pl.multiple_of(r * LEN, LEN), LEN)

        def mix(pages):
            query = qkv_ref[0, rows, :].astype(F32)
            stacked = jnp.concatenate(
                [jnp.where(lane_head == h, query, 0.0) for h in range(heads)], axis=0
            ).astype(BF16)
            own = dot_nt(stacked, qkv_ref[1, rows, :]) * scale
            own = jnp.where(own_col <= own_row, own, NEGATIVE)
            for j in range(pages):
                for which, buffer in enumerate((keys, values)):
                    pltpu.make_async_copy(
                        pieces[0].at[0],
                        buffer.at[r, pl.ds(j * PAGE, PAGE)],
                        sems.at[r, which, j],
                    ).wait()
            span = pl.ds(0, pages * PAGE)
            cached = dot_nt(stacked, keys[r, span]) * scale
            page_of = lax.broadcasted_iota(jnp.int32, cached.shape, 1) // PAGE
            cached = jnp.where(page_of < live, cached, NEGATIVE)
            largest = jnp.maximum(
                jnp.max(own, axis=1, keepdims=True), jnp.max(cached, axis=1, keepdims=True)
            )
            own = jnp.exp(own - largest)
            cached = jnp.exp(cached - largest)
            total = jnp.sum(own, axis=1, keepdims=True) + jnp.sum(cached, axis=1, keepdims=True)
            mixed = jnp.dot(
                cached.astype(BF16), values[r, span], preferred_element_type=F32
            ) + jnp.dot(own.astype(BF16), qkv_ref[2, rows, :], preferred_element_type=F32)
            mixed = mixed / total
            picked = jnp.zeros((LEN, width), F32)
            for h in range(heads):
                picked = jnp.where(lane_head == h, mixed[h * LEN : (h + 1) * LEN], picked)
            for parity in range(2):
                out_ref[parity, pl.ds(pl.multiple_of(r * BLOCK, BLOCK), BLOCK), :] = picked[
                    parity * BLOCK : (parity + 1) * BLOCK
                ].astype(BF16)

        for pages in (2, 4, MAXP):
            pl.when(covering(live) == pages)(lambda pages=pages: mix(pages))
        return 0

    lax.fori_loop(0, rollouts, mix_rollout, 0)


def attend(first, counts, index, owner, qkv, pieces):
    _, rows, width = qkv.shape
    rollouts = rows // LEN
    vmem = pl.BlockSpec(memory_space=pltpu.VMEM)
    pieces = [pltpu.with_memory_space_constraint(piece, pltpu.HBM) for piece in pieces]
    return pl.pallas_call(
        attend_kernel,
        grid_spec=pltpu.PrefetchScalarGridSpec(
            num_scalar_prefetch=4,
            grid=(),
            in_specs=[vmem] + [pl.BlockSpec(memory_space=pltpu.HBM)] * len(pieces),
            out_specs=vmem,
            scratch_shapes=[
                pltpu.VMEM((rollouts, MAXP * PAGE, width), BF16),
                pltpu.VMEM((rollouts, MAXP * PAGE, width), BF16),
                pltpu.SemaphoreType.DMA((rollouts, 2, MAXP)),
            ],
        ),
        out_shape=jax.ShapeDtypeStruct((2, rows // 2, width), BF16),
        compiler_params=pltpu.CompilerParams(vmem_limit_bytes=VMEM_LIMIT),
        name="attend",
    )(first, counts, index, owner, qkv, *pieces)


def two_parts(value):
    high = value.astype(BF16)
    return high, (value - high.astype(F32)).astype(BF16)


def settle_kernel(place_ref, hidden_ref, up_ref, gain_ref, *refs):
    *parts, out_ref = refs
    model = hidden_ref.shape[1]
    rank = up_ref.shape[0]
    total = parts[0][...].astype(F32)
    for part in parts[1:]:
        total = total + part[...].astype(F32)
    reference = hidden_ref[...].astype(F32) + total[:, :model]
    delta = total[:, model:]
    high, low = two_parts(delta)
    policy = (
        reference
        + jnp.dot(high[:, :rank], up_ref[...], preferred_element_type=F32)
        + jnp.dot(low[:, :rank], up_ref[...], preferred_element_type=F32)
    )
    reference_scale = lax.rsqrt(jnp.mean(reference * reference, axis=1, keepdims=True) + EPSILON)
    policy_scale = lax.rsqrt(jnp.mean(policy * policy, axis=1, keepdims=True) + EPSILON)
    out_ref[:, :model] = (reference * reference_scale * gain_ref[...].astype(F32)).astype(BF16)
    lane = lax.broadcasted_iota(jnp.int32, delta.shape, 1)
    beside = high.astype(F32) + pltpu.roll(low.astype(F32), rank, 1)
    at = 2 * rank
    for scale in (policy_scale / reference_scale, policy_scale):
        for _ in range(3):
            part = scale.astype(BF16).astype(F32)
            beside = jnp.where(lane == at, part, beside)
            scale = scale - part
            at += 1
    out_ref[:, model:] = beside.astype(BF16)


def settle(place, hidden, up, gain, *parts):
    whole = lambda i, p: (0, 0)
    size, width = parts[0].shape
    return pl.pallas_call(
        settle_kernel,
        grid_spec=pltpu.PrefetchScalarGridSpec(
            num_scalar_prefetch=1,
            grid=(1,),
            in_specs=[
                pl.BlockSpec((size, hidden.shape[1]), lambda i, p: (p[0], 0)),
                pl.BlockSpec(up.shape, whole),
                pl.BlockSpec(gain.shape, whole),
            ]
            + [pl.BlockSpec(part.shape, whole) for part in parts],
            out_specs=pl.BlockSpec((size, width), whole),
        ),
        out_shape=jax.ShapeDtypeStruct((size, width), BF16),
        compiler_params=pltpu.CompilerParams(vmem_limit_bytes=VMEM_LIMIT),
        name="settle",
    )(place, hidden, up, gain, *parts)


def score_kernel(*refs):
    place_ref, up_ref, gain_ref = refs[:3]
    pieces = refs[3:11]
    out_ref, normed, deltas, scales, wanted, largest, total, picked, head, sems = refs[-10:]
    inputs = refs[11:-10]
    rank, model = up_ref.shape
    rows = deltas.shape[0]
    vocab = head.shape[1]
    part_rows = pieces[0].shape[0] // 8
    spans = sems.shape[0]
    span = vocab // spans
    my_y, my_x, my_core = place_ref[1], place_ref[2], place_ref[3]

    for which in range(spans):
        columns = slice(which * span, (which + 1) * span)
        for p, piece in enumerate(pieces):
            path = my_core if p < 4 else 1 - my_core

            def start_part(n, _, piece=piece, far=p % 4, path=path, which=which, columns=columns):
                near = n // 2
                y = (my_y + jnp.where(path == 0, far, near)) % 4
                x = (my_x + jnp.where(path == 0, near, far)) % 4
                core = jnp.where(n % 2 == 0, path, 1 - path)
                row = (y * 8 + x * 2 + core) * 2 * part_rows + path * part_rows
                pltpu.make_async_copy(
                    piece.at[pl.ds(pl.multiple_of(n * part_rows, 16), part_rows), columns],
                    head.at[pl.ds(pl.multiple_of(row, 16), part_rows), columns],
                    sems.at[which],
                ).start()
                return 0

            lax.fori_loop(0, 8, start_part, 0)

    start = 0
    for target_ref, block in zip(inputs[::2], inputs[1::2]):
        at = slice(start, start + block.shape[0])
        start += block.shape[0]
        normed[at, :] = block[:, :model]
        beside = block[:, model:]
        deltas[at, :] = beside[:, : 2 * rank]
        beside = beside.astype(F32)
        lane = lax.broadcasted_iota(jnp.int32, beside.shape, 1) - 2 * rank
        for which in range(2):
            parts = (lane >= 3 * which) & (lane < 3 * which + 3)
            scales[which, at, :] = jnp.sum(jnp.where(parts, beside, 0.0), axis=1, keepdims=True)
        wanted[at, :] = target_ref[...] - place_ref[0] * vocab
    high, low = two_parts(up_ref[...].astype(F32) * gain_ref[...].astype(F32))
    normed[rows : rows + rank, :] = high
    normed[rows + rank :, :] = low
    largest[...] = jnp.full_like(largest, NEGATIVE)
    total[...] = jnp.zeros_like(total)
    picked[...] = jnp.zeros_like(picked)
    tile = 512

    def score_tile(n, _):
        product = jnp.dot(
            normed[...],
            head[:, pl.ds(pl.multiple_of(n * tile, tile), tile)],
            preferred_element_type=F32,
        )
        reference_logits = product[:rows]
        adapted = jnp.zeros_like(reference_logits)
        for part in two_parts(product[rows : rows + rank] + product[rows + rank :]):
            adapted += jnp.dot(
                deltas[...], jnp.concatenate([part, part], axis=0), preferred_element_type=F32
            )
        policy_logits = scales[0] * reference_logits + scales[1] * adapted
        columns = lax.broadcasted_iota(jnp.int32, reference_logits.shape, 1)
        hit = columns == wanted[...] - n * tile
        for which, logits in enumerate((policy_logits, reference_logits)):
            picked[which] += jnp.sum(jnp.where(hit, logits, 0.0), axis=1, keepdims=True)
            before = largest[which]
            after = jnp.maximum(before, jnp.max(logits, axis=1, keepdims=True))
            total[which] = total[which] * jnp.exp(before - after) + jnp.sum(
                jnp.exp(logits - after), axis=1, keepdims=True
            )
            largest[which] = after
        return 0

    def score_span(which, _):
        columns = pl.ds(pl.multiple_of(which * span, span), span)
        pltpu.make_async_copy(head.at[:, columns], head.at[:, columns], sems.at[which]).wait()
        per_span = span // tile
        return lax.fori_loop(which * per_span, (which + 1) * per_span, score_tile, 0)

    lax.fori_loop(0, spans, score_span, 0)
    lane = lax.broadcasted_iota(jnp.int32, (2, rows, 128), 2)
    packed = jnp.where(lane == 0, largest[...], jnp.where(lane == 1, total[...], picked[...]))
    out_ref[...] = jnp.transpose(packed.reshape(2 * rows, 128))[:8, :]


def score(place, up, gain, targets, pieces, blocks):
    rank, model = up.shape
    vocab = pieces[0].shape[1]
    rows = sum(block.shape[0] for block in blocks)
    whole = lambda i, p: (0, 0)
    pieces = [pltpu.with_memory_space_constraint(piece, pltpu.HBM) for piece in pieces]
    per_block, operands = [], []
    for k, block in enumerate(blocks):
        per_block += [
            pl.BlockSpec((block.shape[0], 1), lambda i, p, k=k: (p[4 + k], 0)),
            pl.BlockSpec(block.shape, whole),
        ]
        operands += [targets, block]
    column = pltpu.VMEM((2, rows, 1), F32)
    return pl.pallas_call(
        score_kernel,
        grid_spec=pltpu.PrefetchScalarGridSpec(
            num_scalar_prefetch=1,
            grid=(1,),
            in_specs=[pl.BlockSpec(up.shape, whole), pl.BlockSpec(gain.shape, whole)]
            + [pl.BlockSpec(memory_space=pltpu.HBM)] * len(pieces)
            + per_block,
            out_specs=pl.BlockSpec((8, 2 * rows), whole),
            scratch_shapes=[
                pltpu.VMEM((rows + 2 * rank, model), BF16),
                pltpu.VMEM((rows, 2 * rank), BF16),
                column,
                pltpu.VMEM((rows, 1), jnp.int32),
                column,
                column,
                column,
                pltpu.VMEM((model, vocab), BF16),
                pltpu.SemaphoreType.DMA((2,)),
            ],
        ),
        out_shape=jax.ShapeDtypeStruct((8, 2 * rows), F32),
        compiler_params=pltpu.CompilerParams(vmem_limit_bytes=VMEM_LIMIT),
        cost_estimate=pl.CostEstimate(
            flops=4 * rows * model * vocab,
            transcendentals=2 * rows * vocab,
            bytes_accessed=2 * model * vocab,
        ),
        name="score",
    )(place, up, gain, *pieces, *operands)


def shifted(value, ranks, step):
    return lax.ppermute(value, "tensor", [(i, (i + step) % ranks) for i in range(ranks)])


def partnered(value, ranks):
    return lax.ppermute(value, "tensor", [(i, i ^ 1) for i in range(ranks)])


def reduce_rows(branch, ranks):
    me = lax.axis_index("tensor")
    size = branch.shape[0] // (ranks // 2)

    def block(step):
        at = (me + step) % ranks // 2 * size
        return lax.dynamic_slice_in_dim(branch, at, size, 0)

    arrived = [shifted(block(step), ranks, step) for step in (ranks // 2, 2, ranks - 2)]
    return [block(0)] + arrived


def crossed(value):
    return lax.ppermute(value, "seq", [(i, i ^ 1) for i in range(32)])


def turned(value, stage, step):
    def target(i):
        y, x, core = i // 8, i // 2 % 4, i % 2
        if core == stage:
            x = (x + step) % 4
        else:
            y = (y + step) % 4
        return y * 8 + x * 2 + core

    return lax.ppermute(value, "seq", [(i, target(i)) for i in range(32)])


def start_pair(first, second):
    first_core = lax.axis_index("seq") % 2 == 0
    kept = jnp.where(first_core, first, second)
    sent = jnp.where(first_core, second, first)
    return jnp.concatenate([kept, crossed(sent)])


def along_first(pair):
    return [pair] + [turned(pair, 0, step) for step in (3, 2, 1)]


def local(
    hidden,
    attention_norm_gain,
    query_key_value_weight,
    output_weight,
    adapter_down_weight,
    adapter_up_weight,
    final_norm_gain,
    head,
    prompt_key_slots,
    prompt_value_slots,
    counts,
    page_slot_index,
    owner,
    targets,
):
    tok_rows, model = hidden.shape
    rollouts_here = tok_rows // LEN
    width_here = output_weight.shape[0]
    heads_here = width_here // HEAD_WIDTH
    ranks = lax.axis_size("tensor")
    first = lax.axis_index("seq") * rollouts_here
    me = lax.axis_index("seq")
    rank = lax.axis_index("tensor")
    down = jnp.pad(adapter_down_weight, ((0, 0), (0, PAD - adapter_down_weight.shape[1])))
    weights = jnp.concatenate([output_weight, down], axis=1)
    groups_iota = jnp.arange(counts.shape[0], dtype=jnp.int32)
    my_groups = lax.dynamic_slice_in_dim(owner, first, rollouts_here, 0)
    my_pages = jnp.sum(
        jnp.where(my_groups[:, None] == groups_iota[None, :], counts[None, :], 0), axis=1
    )
    positions = jnp.repeat(my_pages, LEN) * PAGE + jnp.arange(tok_rows, dtype=jnp.int32) % LEN
    half = HEAD_WIDTH // 2
    place_in_head = jnp.arange(width_here, dtype=jnp.int32) % half
    frequency = 10000.0 ** (-place_in_head.astype(F32) * 2.0 / HEAD_WIDTH)
    angles = positions.astype(F32)[:, None] * frequency[None, :]
    pair = start_pair(prompt_key_slots, prompt_value_slots)
    partner_weights = partnered(weights, ranks)
    line = lax.optimization_barrier(along_first(pair))
    line = lax.optimization_barrier(jnp.concatenate(line))
    ahead = [turned(line, 1, step) for step in (3, 2, 1)]
    near = crossed(line)
    qkv = project(
        hidden,
        attention_norm_gain[None, :],
        query_key_value_weight,
        jnp.cos(angles),
        jnp.sin(angles),
    )
    ahead, qkv, head_columns = lax.optimization_barrier((ahead, qkv, head.T))
    pieces = [line] + ahead + [near] + [crossed(piece) for piece in ahead]
    half = head_columns.shape[0] // 2
    head_pair = start_pair(head_columns[:half], head_columns[half:])
    pieces, head_pair = lax.optimization_barrier((pieces, head_pair))
    head_line = along_first(head_pair)
    attended = attend(
        jnp.stack([first, me // 8, me // 2 % 4, me % 2]).astype(jnp.int32),
        counts,
        page_slot_index,
        owner,
        qkv,
        pieces,
    )
    theirs = partnered(lax.dynamic_index_in_dim(attended, 1 - rank % 2, 0, False), ranks)
    own = lax.dynamic_index_in_dim(attended, rank % 2, 0, False)
    theirs, head_line, partner_weights = lax.optimization_barrier(
        (theirs, head_line, partner_weights)
    )
    head_line = lax.optimization_barrier(jnp.concatenate(head_line))
    head_ahead = [turned(head_line, 1, 3), turned(head_line, 1, 1)]
    branch = jnp.dot(own, weights, preferred_element_type=F32)
    branch = branch + jnp.dot(theirs, partner_weights, preferred_element_type=F32)
    parts, head_line, head_ahead = lax.optimization_barrier(
        (reduce_rows(branch.astype(BF16), ranks), head_line, head_ahead)
    )
    mine = settle(
        rank[None].astype(jnp.int32),
        hidden,
        adapter_up_weight,
        final_norm_gain[None, :],
        *parts,
    )
    size = tok_rows // ranks
    half = size // 2

    def score_blocks(places, blocks):
        return score(
            jnp.stack([rank, me // 8, me // 2 % 4, me % 2] + places).astype(jnp.int32),
            adapter_up_weight,
            final_norm_gain[None, :],
            targets[:, None],
            head_pieces,
            blocks,
        )

    def by_offset(offsets, part):
        part = part.reshape(8, 2, len(offsets), size)
        return {offset: part[:, :, n] for n, offset in enumerate(offsets)}

    def place(offset):
        return (rank + offset) % ranks

    head_opposite = turned(head_line, 1, 2)
    after_one, before_one, line_swapped, first_swapped, third = lax.optimization_barrier(
        (
            shifted(mine, ranks, -1),
            shifted(mine, ranks, 1),
            crossed(head_line),
            crossed(head_ahead[0]),
            head_ahead[1],
        )
    )
    after_two, before_two, head_opposite, third_swapped = lax.optimization_barrier(
        (
            shifted(after_one, ranks, -1),
            shifted(before_one, ranks, 1),
            head_opposite,
            crossed(third),
        )
    )
    near = [after_one, before_one, after_two, before_two]
    head_pieces = [head_line, head_ahead[0], head_opposite, head_ahead[1]]
    head_pieces += [line_swapped, first_swapped, crossed(head_opposite), third_swapped]
    far = [
        shifted(after_two, ranks, -1),
        shifted(before_two, ranks, 1),
        shifted(after_two[:half], ranks, -2),
        shifted(before_two[half:], ranks, 2),
    ]
    near_offsets = (0, 1, ranks - 1, 2, ranks - 2)
    near_part = score_blocks([place(n) for n in near_offsets], [mine] + near)
    far, near_part = lax.optimization_barrier((far, near_part))
    far_offsets = (3, ranks - 3, ranks // 2)
    opposite = 2 * place(ranks // 2)
    far_part = score_blocks([place(3), place(ranks - 3), opposite, opposite + 1], far)
    stats = by_offset(near_offsets, near_part) | by_offset(far_offsets, far_part)
    line = jnp.stack([stats[k] for k in range(ranks)] * 2, axis=2)
    ordered = lax.dynamic_slice_in_dim(line, ranks - rank, ranks, 2).reshape(8, 2 * tok_rows)
    every = lax.all_to_all(
        jnp.broadcast_to(ordered[None], (ranks, 8, 2 * tok_rows)), "tensor", 0, 0, tiled=True
    )
    maxima, totals, picked = every[:, 0], every[:, 1], every[:, 2]
    largest = jnp.max(maxima, axis=0)
    total = jnp.sum(totals * jnp.exp(maxima - largest[None]), axis=0)
    log_probs = jnp.sum(picked, axis=0) - largest - jnp.log(total)
    return (log_probs[:tok_rows], log_probs[tok_rows:])


def solution(mesh):
    return jax.shard_map(
        local,
        mesh=mesh,
        in_specs=(
            P("seq", None),
            P(),
            P(None, None, "tensor"),
            P("tensor", None),
            P("tensor", None),
            P(),
            P(),
            P("tensor", "seq"),
            P("seq", None, "tensor"),
            P("seq", None, "tensor"),
            P(),
            P(),
            P(),
            P("seq"),
        ),
        out_specs=(P("seq"), P("seq")),
        check_vma=False,
    )
```

```python
import math

import jax
import jax.numpy as jnp
from jax import lax
from jax.experimental import pallas as pl
from jax.experimental.pallas import tpu as pltpu
from jax.sharding import PartitionSpec as P

HEAD_WIDTH = 96
LEN = 64
PAGE = 128
MAXP = 8


EPSILON = 1e-05
NEGATIVE = -1e30
PAD = 128
BLOCK = LEN // 2
VMEM_LIMIT = 28 * 1024 * 1024
F32 = jnp.float32
BF16 = jnp.bfloat16


def rms_norm(values, gain):
    mean_sq = jnp.mean(values * values, axis=-1, keepdims=True)
    return (values * lax.rsqrt(mean_sq + EPSILON) * gain.astype(F32)).astype(BF16)


def project_kernel(hidden_ref, gain_ref, weight_ref, cos_ref, sin_ref, out_ref, normed):
    part = pl.program_id(0)

    @pl.when(part == 0)
    def _():
        normed[...] = rms_norm(hidden_ref[...].astype(F32), gain_ref[...])

    product = jnp.dot(normed[...], weight_ref[0], preferred_element_type=F32)

    @pl.when(part < 2)
    def _():
        width = product.shape[1]
        half = HEAD_WIDTH // 2
        lane = lax.broadcasted_iota(jnp.int32, product.shape, 1) % HEAD_WIDTH
        partner = jnp.where(
            lane < half, -pltpu.roll(product, width - half, 1), pltpu.roll(product, half, 1)
        )
        out_ref[0] = (product * cos_ref[...] + partner * sin_ref[...]).astype(BF16)

    @pl.when(part == 2)
    def _():
        out_ref[0] = product.astype(BF16)


def project(hidden, gain, weight, cosine, sinus):
    rows, width = hidden.shape
    parts, _, cols = weight.shape
    whole = lambda i: (0, 0)
    return pl.pallas_call(
        project_kernel,
        grid=(parts,),
        in_specs=[
            pl.BlockSpec((rows, width), whole),
            pl.BlockSpec((1, width), whole),
            pl.BlockSpec((1, width, cols), lambda i: (i, 0, 0)),
            pl.BlockSpec((rows, cols), whole),
            pl.BlockSpec((rows, cols), whole),
        ],
        out_specs=pl.BlockSpec((1, rows, cols), lambda i: (i, 0, 0)),
        out_shape=jax.ShapeDtypeStruct((parts, rows, cols), BF16),
        scratch_shapes=[pltpu.VMEM((rows, width), BF16)],
        compiler_params=pltpu.CompilerParams(vmem_limit_bytes=VMEM_LIMIT),
        name="project",
    )(hidden, gain, weight, cosine, sinus)


def dot_nt(left, right):
    return lax.dot_general(left, right, (((1,), (1,)), ((), ())), preferred_element_type=F32)


def attend_kernel(*refs):
    first_ref, counts_ref, index_ref, owner_ref = refs[:4]
    qkv_ref = refs[4]
    out_ref, keys, values, sems = refs[-4:]
    pieces = refs[5:-4]
    rollouts = keys.shape[0]
    width = qkv_ref.shape[2]
    heads = width // HEAD_WIDTH
    scale = 1.0 / math.sqrt(HEAD_WIDTH)
    first = first_ref[0]
    my_y, my_x, my_core = first_ref[1], first_ref[2], first_ref[3]

    def start_copies(r, j):
        slot = index_ref[owner_ref[first + r] * MAXP + j]
        device = slot // 2
        down_y = (device // 8 - my_y + 4) % 4
        down_x = (device // 2 % 4 - my_x + 4) % 4
        rows = pl.ds(pl.multiple_of(j * PAGE, PAGE), PAGE)
        for path, (buffer, far, near) in enumerate(
            ((keys, down_y, down_x), (values, down_x, down_y))
        ):
            at = near * 4 + 2 * (device % 2 != path).astype(jnp.int32) + slot % 2
            piece = far + 4 * (my_core != path).astype(jnp.int32)
            for p, ref in enumerate(pieces):

                @pl.when(piece == p)
                def _():
                    pltpu.make_async_copy(
                        ref.at[at], buffer.at[r, rows], sems.at[r, path, j]
                    ).start()

        return 0

    def live_pages(r):
        return counts_ref[owner_ref[first + r]]

    def covering(live):
        return jnp.where(live <= 2, 2, jnp.where(live <= 4, 4, MAXP))

    def start_rollout(r, _):
        return lax.fori_loop(0, covering(live_pages(r)), lambda j, _: start_copies(r, j), 0)

    lax.fori_loop(0, rollouts, start_rollout, 0)
    lane_head = lax.broadcasted_iota(jnp.int32, (LEN, width), 1) // HEAD_WIDTH
    own_row = lax.broadcasted_iota(jnp.int32, (heads * LEN, LEN), 0) % LEN
    own_col = lax.broadcasted_iota(jnp.int32, (heads * LEN, LEN), 1)

    def mix_rollout(r, _):
        live = live_pages(r)
        rows = pl.ds(pl.multiple_of(r * LEN, LEN), LEN)

        def mix(pages):
            query = qkv_ref[0, rows, :].astype(F32)
            stacked = jnp.concatenate(
                [jnp.where(lane_head == h, query, 0.0) for h in range(heads)], axis=0
            ).astype(BF16)
            own = dot_nt(stacked, qkv_ref[1, rows, :]) * scale
            own = jnp.where(own_col <= own_row, own, NEGATIVE)
            for j in range(pages):
                for which, buffer in enumerate((keys, values)):
                    pltpu.make_async_copy(
                        pieces[0].at[0],
                        buffer.at[r, pl.ds(j * PAGE, PAGE)],
                        sems.at[r, which, j],
                    ).wait()
            span = pl.ds(0, pages * PAGE)
            cached = dot_nt(stacked, keys[r, span]) * scale
            page_of = lax.broadcasted_iota(jnp.int32, cached.shape, 1) // PAGE
            cached = jnp.where(page_of < live, cached, NEGATIVE)
            largest = jnp.maximum(
                jnp.max(own, axis=1, keepdims=True), jnp.max(cached, axis=1, keepdims=True)
            )
            own = jnp.exp(own - largest)
            cached = jnp.exp(cached - largest)
            total = jnp.sum(own, axis=1, keepdims=True) + jnp.sum(cached, axis=1, keepdims=True)
            mixed = jnp.dot(
                cached.astype(BF16), values[r, span], preferred_element_type=F32
            ) + jnp.dot(own.astype(BF16), qkv_ref[2, rows, :], preferred_element_type=F32)
            mixed = mixed / total
            picked = jnp.zeros((LEN, width), F32)
            for h in range(heads):
                picked = jnp.where(lane_head == h, mixed[h * LEN : (h + 1) * LEN], picked)
            for parity in range(2):
                out_ref[parity, pl.ds(pl.multiple_of(r * BLOCK, BLOCK), BLOCK), :] = picked[
                    parity * BLOCK : (parity + 1) * BLOCK
                ].astype(BF16)

        for pages in (2, 4, MAXP):
            pl.when(covering(live) == pages)(lambda pages=pages: mix(pages))
        return 0

    lax.fori_loop(0, rollouts, mix_rollout, 0)


def attend(first, counts, index, owner, qkv, pieces):
    _, rows, width = qkv.shape
    rollouts = rows // LEN
    vmem = pl.BlockSpec(memory_space=pltpu.VMEM)
    pieces = [pltpu.with_memory_space_constraint(piece, pltpu.HBM) for piece in pieces]
    return pl.pallas_call(
        attend_kernel,
        grid_spec=pltpu.PrefetchScalarGridSpec(
            num_scalar_prefetch=4,
            grid=(),
            in_specs=[vmem] + [pl.BlockSpec(memory_space=pltpu.HBM)] * len(pieces),
            out_specs=vmem,
            scratch_shapes=[
                pltpu.VMEM((rollouts, MAXP * PAGE, width), BF16),
                pltpu.VMEM((rollouts, MAXP * PAGE, width), BF16),
                pltpu.SemaphoreType.DMA((rollouts, 2, MAXP)),
            ],
        ),
        out_shape=jax.ShapeDtypeStruct((2, rows // 2, width), BF16),
        compiler_params=pltpu.CompilerParams(vmem_limit_bytes=VMEM_LIMIT),
        name="attend",
    )(first, counts, index, owner, qkv, *pieces)


def two_parts(value):
    high = value.astype(BF16)
    return high, (value - high.astype(F32)).astype(BF16)


def settle_kernel(place_ref, hidden_ref, up_ref, gain_ref, *refs):
    *parts, out_ref = refs
    model = hidden_ref.shape[1]
    rank = up_ref.shape[0]
    total = parts[0][...].astype(F32)
    for part in parts[1:]:
        total = total + part[...].astype(F32)
    reference = hidden_ref[...].astype(F32) + total[:, :model]
    delta = total[:, model:]
    high, low = two_parts(delta)
    policy = (
        reference
        + jnp.dot(high[:, :rank], up_ref[...], preferred_element_type=F32)
        + jnp.dot(low[:, :rank], up_ref[...], preferred_element_type=F32)
    )
    reference_scale = lax.rsqrt(jnp.mean(reference * reference, axis=1, keepdims=True) + EPSILON)
    policy_scale = lax.rsqrt(jnp.mean(policy * policy, axis=1, keepdims=True) + EPSILON)
    out_ref[:, :model] = (reference * reference_scale * gain_ref[...].astype(F32)).astype(BF16)
    lane = lax.broadcasted_iota(jnp.int32, delta.shape, 1)
    beside = high.astype(F32) + pltpu.roll(low.astype(F32), rank, 1)
    at = 2 * rank
    for scale in (policy_scale / reference_scale, policy_scale):
        for _ in range(3):
            part = scale.astype(BF16).astype(F32)
            beside = jnp.where(lane == at, part, beside)
            scale = scale - part
            at += 1
    out_ref[:, model:] = beside.astype(BF16)


def settle(place, hidden, up, gain, *parts):
    whole = lambda i, p: (0, 0)
    size, width = parts[0].shape
    return pl.pallas_call(
        settle_kernel,
        grid_spec=pltpu.PrefetchScalarGridSpec(
            num_scalar_prefetch=1,
            grid=(1,),
            in_specs=[
                pl.BlockSpec((size, hidden.shape[1]), lambda i, p: (p[0], 0)),
                pl.BlockSpec(up.shape, whole),
                pl.BlockSpec(gain.shape, whole),
            ]
            + [pl.BlockSpec(part.shape, whole) for part in parts],
            out_specs=pl.BlockSpec((size, width), whole),
        ),
        out_shape=jax.ShapeDtypeStruct((size, width), BF16),
        compiler_params=pltpu.CompilerParams(vmem_limit_bytes=VMEM_LIMIT),
        name="settle",
    )(place, hidden, up, gain, *parts)


def score_kernel(*refs):
    place_ref, up_ref, gain_ref = refs[:3]
    pieces = refs[3:11]
    out_ref, normed, deltas, scales, wanted, largest, total, picked, head, sems = refs[-10:]
    inputs = refs[11:-10]
    rank, model = up_ref.shape
    rows = deltas.shape[0]
    vocab = head.shape[1]
    part_rows = pieces[0].shape[0] // 8
    spans = sems.shape[0]
    span = vocab // spans
    my_y, my_x, my_core = place_ref[1], place_ref[2], place_ref[3]

    for which in range(spans):
        columns = slice(which * span, (which + 1) * span)
        for p, piece in enumerate(pieces):
            path = my_core if p < 4 else 1 - my_core

            def start_part(n, _, piece=piece, far=p % 4, path=path, which=which, columns=columns):
                near = n // 2
                y = (my_y + jnp.where(path == 0, far, near)) % 4
                x = (my_x + jnp.where(path == 0, near, far)) % 4
                core = jnp.where(n % 2 == 0, path, 1 - path)
                row = (y * 8 + x * 2 + core) * 2 * part_rows + path * part_rows
                pltpu.make_async_copy(
                    piece.at[pl.ds(pl.multiple_of(n * part_rows, 16), part_rows), columns],
                    head.at[pl.ds(pl.multiple_of(row, 16), part_rows), columns],
                    sems.at[which],
                ).start()
                return 0

            lax.fori_loop(0, 8, start_part, 0)

    start = 0
    for target_ref, block in zip(inputs[::2], inputs[1::2]):
        at = slice(start, start + block.shape[0])
        start += block.shape[0]
        normed[at, :] = block[:, :model]
        beside = block[:, model:]
        deltas[at, :] = beside[:, : 2 * rank]
        beside = beside.astype(F32)
        lane = lax.broadcasted_iota(jnp.int32, beside.shape, 1) - 2 * rank
        for which in range(2):
            parts = (lane >= 3 * which) & (lane < 3 * which + 3)
            scales[which, at, :] = jnp.sum(jnp.where(parts, beside, 0.0), axis=1, keepdims=True)
        wanted[at, :] = target_ref[...] - place_ref[0] * vocab
    high, low = two_parts(up_ref[...].astype(F32) * gain_ref[...].astype(F32))
    normed[rows : rows + rank, :] = high
    normed[rows + rank :, :] = low
    largest[...] = jnp.full_like(largest, NEGATIVE)
    total[...] = jnp.zeros_like(total)
    picked[...] = jnp.zeros_like(picked)
    tile = 512

    def score_tile(n, _):
        product = jnp.dot(
            normed[...],
            head[:, pl.ds(pl.multiple_of(n * tile, tile), tile)],
            preferred_element_type=F32,
        )
        reference_logits = product[:rows]
        adapted = jnp.zeros_like(reference_logits)
        for part in two_parts(product[rows : rows + rank] + product[rows + rank :]):
            adapted += jnp.dot(
                deltas[...], jnp.concatenate([part, part], axis=0), preferred_element_type=F32
            )
        policy_logits = scales[0] * reference_logits + scales[1] * adapted
        columns = lax.broadcasted_iota(jnp.int32, reference_logits.shape, 1)
        hit = columns == wanted[...] - n * tile
        for which, logits in enumerate((policy_logits, reference_logits)):
            picked[which] += jnp.sum(jnp.where(hit, logits, 0.0), axis=1, keepdims=True)
            before = largest[which]
            after = jnp.maximum(before, jnp.max(logits, axis=1, keepdims=True))
            total[which] = total[which] * jnp.exp(before - after) + jnp.sum(
                jnp.exp(logits - after), axis=1, keepdims=True
            )
            largest[which] = after
        return 0

    def score_span(which, _):
        columns = pl.ds(pl.multiple_of(which * span, span), span)
        pltpu.make_async_copy(head.at[:, columns], head.at[:, columns], sems.at[which]).wait()
        per_span = span // tile
        return lax.fori_loop(which * per_span, (which + 1) * per_span, score_tile, 0)

    lax.fori_loop(0, spans, score_span, 0)
    lane = lax.broadcasted_iota(jnp.int32, (2, rows, 128), 2)
    packed = jnp.where(lane == 0, largest[...], jnp.where(lane == 1, total[...], picked[...]))
    out_ref[...] = jnp.transpose(packed.reshape(2 * rows, 128))[:8, :]


def score(place, up, gain, targets, pieces, blocks):
    rank, model = up.shape
    vocab = pieces[0].shape[1]
    rows = sum(block.shape[0] for block in blocks)
    whole = lambda i, p: (0, 0)
    pieces = [pltpu.with_memory_space_constraint(piece, pltpu.HBM) for piece in pieces]
    per_block, operands = [], []
    for k, block in enumerate(blocks):
        per_block += [
            pl.BlockSpec((block.shape[0], 1), lambda i, p, k=k: (p[4 + k], 0)),
            pl.BlockSpec(block.shape, whole),
        ]
        operands += [targets, block]
    column = pltpu.VMEM((2, rows, 1), F32)
    return pl.pallas_call(
        score_kernel,
        grid_spec=pltpu.PrefetchScalarGridSpec(
            num_scalar_prefetch=1,
            grid=(1,),
            in_specs=[pl.BlockSpec(up.shape, whole), pl.BlockSpec(gain.shape, whole)]
            + [pl.BlockSpec(memory_space=pltpu.HBM)] * len(pieces)
            + per_block,
            out_specs=pl.BlockSpec((8, 2 * rows), whole),
            scratch_shapes=[
                pltpu.VMEM((rows + 2 * rank, model), BF16),
                pltpu.VMEM((rows, 2 * rank), BF16),
                column,
                pltpu.VMEM((rows, 1), jnp.int32),
                column,
                column,
                column,
                pltpu.VMEM((model, vocab), BF16),
                pltpu.SemaphoreType.DMA((2,)),
            ],
        ),
        out_shape=jax.ShapeDtypeStruct((8, 2 * rows), F32),
        compiler_params=pltpu.CompilerParams(vmem_limit_bytes=VMEM_LIMIT),
        cost_estimate=pl.CostEstimate(
            flops=4 * rows * model * vocab,
            transcendentals=2 * rows * vocab,
            bytes_accessed=2 * model * vocab,
        ),
        name="score",
    )(place, up, gain, *pieces, *operands)


def shifted(value, ranks, step):
    return lax.ppermute(value, "tensor", [(i, (i + step) % ranks) for i in range(ranks)])


def partnered(value, ranks):
    return lax.ppermute(value, "tensor", [(i, i ^ 1) for i in range(ranks)])


def reduce_rows(branch, ranks):
    me = lax.axis_index("tensor")
    size = branch.shape[0] // (ranks // 2)

    def block(step):
        at = (me + step) % ranks // 2 * size
        return lax.dynamic_slice_in_dim(branch, at, size, 0)

    arrived = [shifted(block(step), ranks, step) for step in (ranks // 2, 2, ranks - 2)]
    return [block(0)] + arrived


def crossed(value):
    return lax.ppermute(value, "seq", [(i, i ^ 1) for i in range(32)])


def turned(value, stage, step):
    def target(i):
        y, x, core = i // 8, i // 2 % 4, i % 2
        if core == stage:
            x = (x + step) % 4
        else:
            y = (y + step) % 4
        return y * 8 + x * 2 + core

    return lax.ppermute(value, "seq", [(i, target(i)) for i in range(32)])


def start_pair(first, second):
    first_core = lax.axis_index("seq") % 2 == 0
    kept = jnp.where(first_core, first, second)
    sent = jnp.where(first_core, second, first)
    return jnp.concatenate([kept, crossed(sent)])


def along_first(pair):
    return [pair] + [turned(pair, 0, step) for step in (3, 2, 1)]


def local(
    hidden,
    attention_norm_gain,
    query_key_value_weight,
    output_weight,
    adapter_down_weight,
    adapter_up_weight,
    final_norm_gain,
    head,
    prompt_key_slots,
    prompt_value_slots,
    counts,
    page_slot_index,
    owner,
    targets,
):
    tok_rows, model = hidden.shape
    rollouts_here = tok_rows // LEN
    width_here = output_weight.shape[0]
    heads_here = width_here // HEAD_WIDTH
    ranks = lax.axis_size("tensor")
    first = lax.axis_index("seq") * rollouts_here
    me = lax.axis_index("seq")
    rank = lax.axis_index("tensor")
    down = jnp.pad(adapter_down_weight, ((0, 0), (0, PAD - adapter_down_weight.shape[1])))
    weights = jnp.concatenate([output_weight, down], axis=1)
    groups_iota = jnp.arange(counts.shape[0], dtype=jnp.int32)
    my_groups = lax.dynamic_slice_in_dim(owner, first, rollouts_here, 0)
    my_pages = jnp.sum(
        jnp.where(my_groups[:, None] == groups_iota[None, :], counts[None, :], 0), axis=1
    )
    positions = jnp.repeat(my_pages, LEN) * PAGE + jnp.arange(tok_rows, dtype=jnp.int32) % LEN
    half = HEAD_WIDTH // 2
    place_in_head = jnp.arange(width_here, dtype=jnp.int32) % half
    frequency = 10000.0 ** (-place_in_head.astype(F32) * 2.0 / HEAD_WIDTH)
    angles = positions.astype(F32)[:, None] * frequency[None, :]
    pair = start_pair(prompt_key_slots, prompt_value_slots)
    partner_weights = partnered(weights, ranks)
    line = lax.optimization_barrier(along_first(pair))
    line = lax.optimization_barrier(jnp.concatenate(line))
    ahead = [turned(line, 1, step) for step in (3, 2, 1)]
    near = crossed(line)
    qkv = project(
        hidden,
        attention_norm_gain[None, :],
        query_key_value_weight,
        jnp.cos(angles),
        jnp.sin(angles),
    )
    ahead, near, qkv, head_columns = lax.optimization_barrier((ahead, near, qkv, head.T))
    pieces = [line] + ahead + [near] + [crossed(piece) for piece in ahead]
    half = head_columns.shape[0] // 2
    head_pair = start_pair(head_columns[:half], head_columns[half:])
    head_line = along_first(head_pair)
    attended = attend(
        jnp.stack([first, me // 8, me // 2 % 4, me % 2]).astype(jnp.int32),
        counts,
        page_slot_index,
        owner,
        qkv,
        pieces,
    )
    theirs = partnered(lax.dynamic_index_in_dim(attended, 1 - rank % 2, 0, False), ranks)
    attended, head_line, partner_weights = lax.optimization_barrier(
        (attended, head_line, partner_weights)
    )
    own = lax.dynamic_index_in_dim(attended, rank % 2, 0, False)
    head_line = lax.optimization_barrier(jnp.concatenate(head_line))
    head_ahead = [turned(head_line, 1, 3), turned(head_line, 1, 1)]
    branch = jnp.dot(own, weights, preferred_element_type=F32)
    branch = branch + jnp.dot(theirs, partner_weights, preferred_element_type=F32)
    parts = reduce_rows(branch.astype(BF16), ranks)
    parts, head_line, head_ahead = lax.optimization_barrier((parts, head_line, head_ahead))
    head_opposite = turned(head_line, 1, 2)
    mine = settle(
        rank[None].astype(jnp.int32),
        hidden,
        adapter_up_weight,
        final_norm_gain[None, :],
        *parts,
    )
    size = tok_rows // ranks
    half = size // 2

    def score_blocks(places, blocks):
        return score(
            jnp.stack([rank, me // 8, me // 2 % 4, me % 2] + places).astype(jnp.int32),
            adapter_up_weight,
            final_norm_gain[None, :],
            targets[:, None],
            head_pieces,
            blocks,
        )

    def by_offset(offsets, part):
        part = part.reshape(8, 2, len(offsets), size)
        return {offset: part[:, :, n] for n, offset in enumerate(offsets)}

    def place(offset):
        return (rank + offset) % ranks

    after_one, before_one, line_swapped, first_swapped, third = lax.optimization_barrier(
        (
            shifted(mine, ranks, -1),
            shifted(mine, ranks, 1),
            crossed(head_line),
            crossed(head_ahead[0]),
            head_ahead[1],
        )
    )
    after_two, before_two, head_opposite, third_swapped = lax.optimization_barrier(
        (
            shifted(after_one, ranks, -1),
            shifted(before_one, ranks, 1),
            head_opposite,
            crossed(third),
        )
    )
    near = [after_one, before_one, after_two, before_two]
    head_pieces = [head_line, head_ahead[0], head_opposite, head_ahead[1]]
    head_pieces += [line_swapped, first_swapped, crossed(head_opposite), third_swapped]
    far = [
        shifted(after_two, ranks, -1),
        shifted(before_two, ranks, 1),
        shifted(after_two[:half], ranks, -2),
        shifted(before_two[half:], ranks, 2),
    ]
    near_offsets = (0, 1, ranks - 1, 2, ranks - 2)
    near_part = score_blocks([place(n) for n in near_offsets], [mine] + near)
    far, near_part = lax.optimization_barrier((far, near_part))
    far_offsets = (3, ranks - 3, ranks // 2)
    opposite = 2 * place(ranks // 2)
    far_part = score_blocks([place(3), place(ranks - 3), opposite, opposite + 1], far)
    stats = by_offset(near_offsets, near_part) | by_offset(far_offsets, far_part)
    line = jnp.stack([stats[k] for k in range(ranks)] * 2, axis=2)
    ordered = lax.dynamic_slice_in_dim(line, ranks - rank, ranks, 2).reshape(8, 2 * tok_rows)
    every = lax.all_to_all(
        jnp.broadcast_to(ordered[None], (ranks, 8, 2 * tok_rows)), "tensor", 0, 0, tiled=True
    )
    maxima, totals, picked = every[:, 0], every[:, 1], every[:, 2]
    largest = jnp.max(maxima, axis=0)
    total = jnp.sum(totals * jnp.exp(maxima - largest[None]), axis=0)
    log_probs = jnp.sum(picked, axis=0) - largest - jnp.log(total)
    return (log_probs[:tok_rows], log_probs[tok_rows:])


def solution(mesh):
    return jax.shard_map(
        local,
        mesh=mesh,
        in_specs=(
            P("seq", None),
            P(),
            P(None, None, "tensor"),
            P("tensor", None),
            P("tensor", None),
            P(),
            P(),
            P("tensor", "seq"),
            P("seq", None, "tensor"),
            P("seq", None, "tensor"),
            P(),
            P(),
            P(),
            P("seq"),
        ),
        out_specs=(P("seq"), P("seq")),
        check_vma=False,
    )
```

```python
import math

import jax
import jax.numpy as jnp
from jax import lax
from jax.experimental import pallas as pl
from jax.experimental.pallas import tpu as pltpu
from jax.sharding import PartitionSpec as P

HEAD_WIDTH = 96
LEN = 64
PAGE = 128
MAXP = 8


EPSILON = 1e-05
NEGATIVE = -1e30
PAD = 128
BLOCK = LEN // 2
VMEM_LIMIT = 28 * 1024 * 1024
F32 = jnp.float32
BF16 = jnp.bfloat16


def rms_norm(values, gain):
    mean_sq = jnp.mean(values * values, axis=-1, keepdims=True)
    return (values * lax.rsqrt(mean_sq + EPSILON) * gain.astype(F32)).astype(BF16)


def project_kernel(hidden_ref, gain_ref, weight_ref, cos_ref, sin_ref, out_ref, normed):
    part = pl.program_id(0)

    @pl.when(part == 0)
    def _():
        normed[...] = rms_norm(hidden_ref[...].astype(F32), gain_ref[...])

    product = jnp.dot(normed[...], weight_ref[0], preferred_element_type=F32)

    @pl.when(part < 2)
    def _():
        width = product.shape[1]
        half = HEAD_WIDTH // 2
        lane = lax.broadcasted_iota(jnp.int32, product.shape, 1) % HEAD_WIDTH
        partner = jnp.where(
            lane < half, -pltpu.roll(product, width - half, 1), pltpu.roll(product, half, 1)
        )
        out_ref[0] = (product * cos_ref[...] + partner * sin_ref[...]).astype(BF16)

    @pl.when(part == 2)
    def _():
        out_ref[0] = product.astype(BF16)


def project(hidden, gain, weight, cosine, sinus):
    rows, width = hidden.shape
    parts, _, cols = weight.shape
    whole = lambda i: (0, 0)
    return pl.pallas_call(
        project_kernel,
        grid=(parts,),
        in_specs=[
            pl.BlockSpec((rows, width), whole),
            pl.BlockSpec((1, width), whole),
            pl.BlockSpec((1, width, cols), lambda i: (i, 0, 0)),
            pl.BlockSpec((rows, cols), whole),
            pl.BlockSpec((rows, cols), whole),
        ],
        out_specs=pl.BlockSpec((1, rows, cols), lambda i: (i, 0, 0)),
        out_shape=jax.ShapeDtypeStruct((parts, rows, cols), BF16),
        scratch_shapes=[pltpu.VMEM((rows, width), BF16)],
        compiler_params=pltpu.CompilerParams(vmem_limit_bytes=VMEM_LIMIT),
        name="project",
    )(hidden, gain, weight, cosine, sinus)


def dot_nt(left, right):
    return lax.dot_general(left, right, (((1,), (1,)), ((), ())), preferred_element_type=F32)


def attend_kernel(*refs):
    first_ref, counts_ref, index_ref, owner_ref = refs[:4]
    qkv_ref = refs[4]
    out_ref, keys, values, sems = refs[-4:]
    pieces = refs[5:-4]
    rollouts = keys.shape[0]
    width = qkv_ref.shape[2]
    heads = width // HEAD_WIDTH
    scale = 1.0 / math.sqrt(HEAD_WIDTH)
    first = first_ref[0]
    my_y, my_x, my_core = first_ref[1], first_ref[2], first_ref[3]

    def start_copies(r, j):
        slot = index_ref[owner_ref[first + r] * MAXP + j]
        device = slot // 2
        down_y = (device // 8 - my_y + 4) % 4
        down_x = (device // 2 % 4 - my_x + 4) % 4
        rows = pl.ds(pl.multiple_of(j * PAGE, PAGE), PAGE)
        for path, (buffer, far, near) in enumerate(
            ((keys, down_y, down_x), (values, down_x, down_y))
        ):
            at = near * 4 + 2 * (device % 2 != path).astype(jnp.int32) + slot % 2
            piece = far + 4 * (my_core != path).astype(jnp.int32)
            for p, ref in enumerate(pieces):

                @pl.when(piece == p)
                def _():
                    pltpu.make_async_copy(
                        ref.at[at], buffer.at[r, rows], sems.at[r, path, j]
                    ).start()

        return 0

    def live_pages(r):
        return counts_ref[owner_ref[first + r]]

    def covering(live):
        return jnp.where(live <= 2, 2, jnp.where(live <= 4, 4, MAXP))

    def start_rollout(r, _):
        return lax.fori_loop(0, covering(live_pages(r)), lambda j, _: start_copies(r, j), 0)

    lax.fori_loop(0, rollouts, start_rollout, 0)
    lane_head = lax.broadcasted_iota(jnp.int32, (LEN, width), 1) // HEAD_WIDTH
    own_row = lax.broadcasted_iota(jnp.int32, (heads * LEN, LEN), 0) % LEN
    own_col = lax.broadcasted_iota(jnp.int32, (heads * LEN, LEN), 1)

    def mix_rollout(r, _):
        live = live_pages(r)
        rows = pl.ds(pl.multiple_of(r * LEN, LEN), LEN)

        def mix(pages):
            query = qkv_ref[0, rows, :].astype(F32)
            stacked = jnp.concatenate(
                [jnp.where(lane_head == h, query, 0.0) for h in range(heads)], axis=0
            ).astype(BF16)
            own = dot_nt(stacked, qkv_ref[1, rows, :]) * scale
            own = jnp.where(own_col <= own_row, own, NEGATIVE)
            for j in range(pages):
                for which, buffer in enumerate((keys, values)):
                    pltpu.make_async_copy(
                        pieces[0].at[0],
                        buffer.at[r, pl.ds(j * PAGE, PAGE)],
                        sems.at[r, which, j],
                    ).wait()
            span = pl.ds(0, pages * PAGE)
            cached = dot_nt(stacked, keys[r, span]) * scale
            page_of = lax.broadcasted_iota(jnp.int32, cached.shape, 1) // PAGE
            cached = jnp.where(page_of < live, cached, NEGATIVE)
            largest = jnp.maximum(
                jnp.max(own, axis=1, keepdims=True), jnp.max(cached, axis=1, keepdims=True)
            )
            own = jnp.exp(own - largest)
            cached = jnp.exp(cached - largest)
            total = jnp.sum(own, axis=1, keepdims=True) + jnp.sum(cached, axis=1, keepdims=True)
            mixed = jnp.dot(
                cached.astype(BF16), values[r, span], preferred_element_type=F32
            ) + jnp.dot(own.astype(BF16), qkv_ref[2, rows, :], preferred_element_type=F32)
            mixed = mixed / total
            picked = jnp.zeros((LEN, width), F32)
            for h in range(heads):
                picked = jnp.where(lane_head == h, mixed[h * LEN : (h + 1) * LEN], picked)
            for parity in range(2):
                out_ref[parity, pl.ds(pl.multiple_of(r * BLOCK, BLOCK), BLOCK), :] = picked[
                    parity * BLOCK : (parity + 1) * BLOCK
                ].astype(BF16)

        for pages in (2, 4, MAXP):
            pl.when(covering(live) == pages)(lambda pages=pages: mix(pages))
        return 0

    lax.fori_loop(0, rollouts, mix_rollout, 0)


def attend(first, counts, index, owner, qkv, pieces):
    _, rows, width = qkv.shape
    rollouts = rows // LEN
    vmem = pl.BlockSpec(memory_space=pltpu.VMEM)
    pieces = [pltpu.with_memory_space_constraint(piece, pltpu.HBM) for piece in pieces]
    return pl.pallas_call(
        attend_kernel,
        grid_spec=pltpu.PrefetchScalarGridSpec(
            num_scalar_prefetch=4,
            grid=(),
            in_specs=[vmem] + [pl.BlockSpec(memory_space=pltpu.HBM)] * len(pieces),
            out_specs=vmem,
            scratch_shapes=[
                pltpu.VMEM((rollouts, MAXP * PAGE, width), BF16),
                pltpu.VMEM((rollouts, MAXP * PAGE, width), BF16),
                pltpu.SemaphoreType.DMA((rollouts, 2, MAXP)),
            ],
        ),
        out_shape=jax.ShapeDtypeStruct((2, rows // 2, width), BF16),
        compiler_params=pltpu.CompilerParams(vmem_limit_bytes=VMEM_LIMIT),
        name="attend",
    )(first, counts, index, owner, qkv, *pieces)


def two_parts(value):
    high = value.astype(BF16)
    return high, (value - high.astype(F32)).astype(BF16)


def settle_kernel(place_ref, hidden_ref, up_ref, gain_ref, *refs):
    *parts, out_ref = refs
    model = hidden_ref.shape[1]
    rank = up_ref.shape[0]
    total = parts[0][...].astype(F32)
    for part in parts[1:]:
        total = total + part[...].astype(F32)
    reference = hidden_ref[...].astype(F32) + total[:, :model]
    delta = total[:, model:]
    high, low = two_parts(delta)
    policy = (
        reference
        + jnp.dot(high[:, :rank], up_ref[...], preferred_element_type=F32)
        + jnp.dot(low[:, :rank], up_ref[...], preferred_element_type=F32)
    )
    reference_scale = lax.rsqrt(jnp.mean(reference * reference, axis=1, keepdims=True) + EPSILON)
    policy_scale = lax.rsqrt(jnp.mean(policy * policy, axis=1, keepdims=True) + EPSILON)
    out_ref[:, :model] = (reference * reference_scale * gain_ref[...].astype(F32)).astype(BF16)
    lane = lax.broadcasted_iota(jnp.int32, delta.shape, 1)
    beside = high.astype(F32) + pltpu.roll(low.astype(F32), rank, 1)
    at = 2 * rank
    for scale in (policy_scale / reference_scale, policy_scale):
        for _ in range(3):
            part = scale.astype(BF16).astype(F32)
            beside = jnp.where(lane == at, part, beside)
            scale = scale - part
            at += 1
    out_ref[:, model:] = beside.astype(BF16)


def settle(place, hidden, up, gain, *parts):
    whole = lambda i, p: (0, 0)
    size, width = parts[0].shape
    return pl.pallas_call(
        settle_kernel,
        grid_spec=pltpu.PrefetchScalarGridSpec(
            num_scalar_prefetch=1,
            grid=(1,),
            in_specs=[
                pl.BlockSpec((size, hidden.shape[1]), lambda i, p: (p[0], 0)),
                pl.BlockSpec(up.shape, whole),
                pl.BlockSpec(gain.shape, whole),
            ]
            + [pl.BlockSpec(part.shape, whole) for part in parts],
            out_specs=pl.BlockSpec((size, width), whole),
        ),
        out_shape=jax.ShapeDtypeStruct((size, width), BF16),
        compiler_params=pltpu.CompilerParams(vmem_limit_bytes=VMEM_LIMIT),
        name="settle",
    )(place, hidden, up, gain, *parts)


def score_kernel(*refs):
    place_ref, up_ref, gain_ref = refs[:3]
    pieces = refs[3:11]
    out_ref, normed, deltas, scales, wanted, largest, total, picked, head, sems = refs[-10:]
    inputs = refs[11:-10]
    rank, model = up_ref.shape
    rows = deltas.shape[0]
    vocab = head.shape[1]
    part_rows = pieces[0].shape[0] // 8
    spans = sems.shape[0]
    span = vocab // spans
    my_y, my_x, my_core = place_ref[1], place_ref[2], place_ref[3]

    for which in range(spans):
        columns = slice(which * span, (which + 1) * span)
        for p, piece in enumerate(pieces):
            path = my_core if p < 4 else 1 - my_core

            def start_part(n, _, piece=piece, far=p % 4, path=path, which=which, columns=columns):
                near = n // 2
                y = (my_y + jnp.where(path == 0, far, near)) % 4
                x = (my_x + jnp.where(path == 0, near, far)) % 4
                core = jnp.where(n % 2 == 0, path, 1 - path)
                row = (y * 8 + x * 2 + core) * 2 * part_rows + path * part_rows
                pltpu.make_async_copy(
                    piece.at[pl.ds(pl.multiple_of(n * part_rows, 16), part_rows), columns],
                    head.at[pl.ds(pl.multiple_of(row, 16), part_rows), columns],
                    sems.at[which],
                ).start()
                return 0

            lax.fori_loop(0, 8, start_part, 0)

    start = 0
    for target_ref, block in zip(inputs[::2], inputs[1::2]):
        at = slice(start, start + block.shape[0])
        start += block.shape[0]
        normed[at, :] = block[:, :model]
        beside = block[:, model:]
        deltas[at, :] = beside[:, : 2 * rank]
        beside = beside.astype(F32)
        lane = lax.broadcasted_iota(jnp.int32, beside.shape, 1) - 2 * rank
        for which in range(2):
            parts = (lane >= 3 * which) & (lane < 3 * which + 3)
            scales[which, at, :] = jnp.sum(jnp.where(parts, beside, 0.0), axis=1, keepdims=True)
        wanted[at, :] = target_ref[...] - place_ref[0] * vocab
    high, low = two_parts(up_ref[...].astype(F32) * gain_ref[...].astype(F32))
    normed[rows : rows + rank, :] = high
    normed[rows + rank :, :] = low
    largest[...] = jnp.full_like(largest, NEGATIVE)
    total[...] = jnp.zeros_like(total)
    picked[...] = jnp.zeros_like(picked)
    tile = 512

    def score_tile(n, _):
        product = jnp.dot(
            normed[...],
            head[:, pl.ds(pl.multiple_of(n * tile, tile), tile)],
            preferred_element_type=F32,
        )
        reference_logits = product[:rows]
        adapted = jnp.zeros_like(reference_logits)
        for part in two_parts(product[rows : rows + rank] + product[rows + rank :]):
            adapted += jnp.dot(
                deltas[...], jnp.concatenate([part, part], axis=0), preferred_element_type=F32
            )
        policy_logits = scales[0] * reference_logits + scales[1] * adapted
        columns = lax.broadcasted_iota(jnp.int32, reference_logits.shape, 1)
        hit = columns == wanted[...] - n * tile
        for which, logits in enumerate((policy_logits, reference_logits)):
            picked[which] += jnp.sum(jnp.where(hit, logits, 0.0), axis=1, keepdims=True)
            before = largest[which]
            after = jnp.maximum(before, jnp.max(logits, axis=1, keepdims=True))
            total[which] = total[which] * jnp.exp(before - after) + jnp.sum(
                jnp.exp(logits - after), axis=1, keepdims=True
            )
            largest[which] = after
        return 0

    def score_span(which, _):
        columns = pl.ds(pl.multiple_of(which * span, span), span)
        pltpu.make_async_copy(head.at[:, columns], head.at[:, columns], sems.at[which]).wait()
        per_span = span // tile
        return lax.fori_loop(which * per_span, (which + 1) * per_span, score_tile, 0)

    lax.fori_loop(0, spans, score_span, 0)
    lane = lax.broadcasted_iota(jnp.int32, (2, rows, 128), 2)
    packed = jnp.where(lane == 0, largest[...], jnp.where(lane == 1, total[...], picked[...]))
    out_ref[...] = jnp.transpose(packed.reshape(2 * rows, 128))[:8, :]


def score(place, up, gain, targets, pieces, blocks):
    rank, model = up.shape
    vocab = pieces[0].shape[1]
    rows = sum(block.shape[0] for block in blocks)
    whole = lambda i, p: (0, 0)
    pieces = [pltpu.with_memory_space_constraint(piece, pltpu.HBM) for piece in pieces]
    per_block, operands = [], []
    for k, block in enumerate(blocks):
        per_block += [
            pl.BlockSpec((block.shape[0], 1), lambda i, p, k=k: (p[4 + k], 0)),
            pl.BlockSpec(block.shape, whole),
        ]
        operands += [targets, block]
    column = pltpu.VMEM((2, rows, 1), F32)
    return pl.pallas_call(
        score_kernel,
        grid_spec=pltpu.PrefetchScalarGridSpec(
            num_scalar_prefetch=1,
            grid=(1,),
            in_specs=[pl.BlockSpec(up.shape, whole), pl.BlockSpec(gain.shape, whole)]
            + [pl.BlockSpec(memory_space=pltpu.HBM)] * len(pieces)
            + per_block,
            out_specs=pl.BlockSpec((8, 2 * rows), whole),
            scratch_shapes=[
                pltpu.VMEM((rows + 2 * rank, model), BF16),
                pltpu.VMEM((rows, 2 * rank), BF16),
                column,
                pltpu.VMEM((rows, 1), jnp.int32),
                column,
                column,
                column,
                pltpu.VMEM((model, vocab), BF16),
                pltpu.SemaphoreType.DMA((2,)),
            ],
        ),
        out_shape=jax.ShapeDtypeStruct((8, 2 * rows), F32),
        compiler_params=pltpu.CompilerParams(vmem_limit_bytes=VMEM_LIMIT),
        cost_estimate=pl.CostEstimate(
            flops=4 * rows * model * vocab,
            transcendentals=2 * rows * vocab,
            bytes_accessed=2 * model * vocab,
        ),
        name="score",
    )(place, up, gain, *pieces, *operands)


def shifted(value, ranks, step):
    return lax.ppermute(value, "tensor", [(i, (i + step) % ranks) for i in range(ranks)])


def partnered(value, ranks):
    return lax.ppermute(value, "tensor", [(i, i ^ 1) for i in range(ranks)])


def reduce_rows(branch, ranks):
    me = lax.axis_index("tensor")
    size = branch.shape[0] // (ranks // 2)

    def block(step):
        at = (me + step) % ranks // 2 * size
        return lax.dynamic_slice_in_dim(branch, at, size, 0)

    arrived = [shifted(block(step), ranks, step) for step in (ranks // 2, 2, ranks - 2)]
    return [block(0)] + arrived


def crossed(value):
    return lax.ppermute(value, "seq", [(i, i ^ 1) for i in range(32)])


def turned(value, stage, step):
    def target(i):
        y, x, core = i // 8, i // 2 % 4, i % 2
        if core == stage:
            x = (x + step) % 4
        else:
            y = (y + step) % 4
        return y * 8 + x * 2 + core

    return lax.ppermute(value, "seq", [(i, target(i)) for i in range(32)])


def start_pair(first, second):
    first_core = lax.axis_index("seq") % 2 == 0
    kept = jnp.where(first_core, first, second)
    sent = jnp.where(first_core, second, first)
    return jnp.concatenate([kept, crossed(sent)])


def along_first(pair):
    return [pair] + [turned(pair, 0, step) for step in (3, 2, 1)]


def local(
    hidden,
    attention_norm_gain,
    query_key_value_weight,
    output_weight,
    adapter_down_weight,
    adapter_up_weight,
    final_norm_gain,
    head,
    prompt_key_slots,
    prompt_value_slots,
    counts,
    page_slot_index,
    owner,
    targets,
):
    tok_rows, model = hidden.shape
    rollouts_here = tok_rows // LEN
    width_here = output_weight.shape[0]
    heads_here = width_here // HEAD_WIDTH
    ranks = lax.axis_size("tensor")
    first = lax.axis_index("seq") * rollouts_here
    me = lax.axis_index("seq")
    rank = lax.axis_index("tensor")
    down = jnp.pad(adapter_down_weight, ((0, 0), (0, PAD - adapter_down_weight.shape[1])))
    groups_iota = jnp.arange(counts.shape[0], dtype=jnp.int32)
    my_groups = lax.dynamic_slice_in_dim(owner, first, rollouts_here, 0)
    my_pages = jnp.sum(
        jnp.where(my_groups[:, None] == groups_iota[None, :], counts[None, :], 0), axis=1
    )
    positions = jnp.repeat(my_pages, LEN) * PAGE + jnp.arange(tok_rows, dtype=jnp.int32) % LEN
    half = HEAD_WIDTH // 2
    place_in_head = jnp.arange(width_here, dtype=jnp.int32) % half
    frequency = 10000.0 ** (-place_in_head.astype(F32) * 2.0 / HEAD_WIDTH)
    angles = positions.astype(F32)[:, None] * frequency[None, :]
    pair = start_pair(prompt_key_slots, prompt_value_slots)
    partner_weights = partnered(output_weight, ranks)
    partner_down = partnered(down, ranks)
    line = lax.optimization_barrier(along_first(pair))
    line = lax.optimization_barrier(jnp.concatenate(line))
    ahead = [turned(line, 1, step) for step in (3, 2, 1)]
    near = crossed(line)
    qkv = project(
        hidden,
        attention_norm_gain[None, :],
        query_key_value_weight,
        jnp.cos(angles),
        jnp.sin(angles),
    )
    ahead, near, qkv, head_columns, partner_weights = lax.optimization_barrier(
        (ahead, near, qkv, head.T, partner_weights)
    )
    pieces = [line] + ahead + [near] + [crossed(piece) for piece in ahead]
    half = head_columns.shape[0] // 2
    head_pair = start_pair(head_columns[:half], head_columns[half:])
    head_line = along_first(head_pair)
    attended = attend(
        jnp.stack([first, me // 8, me // 2 % 4, me % 2]).astype(jnp.int32),
        counts,
        page_slot_index,
        owner,
        qkv,
        pieces,
    )
    theirs = partnered(lax.dynamic_index_in_dim(attended, 1 - rank % 2, 0, False), ranks)
    attended, head_line, partner_down = lax.optimization_barrier(
        (attended, head_line, partner_down)
    )
    own = lax.dynamic_index_in_dim(attended, rank % 2, 0, False)
    head_line = lax.optimization_barrier(jnp.concatenate(head_line))
    head_ahead = [turned(head_line, 1, 3), turned(head_line, 1, 1)]
    branch = [
        jnp.dot(own, factor, preferred_element_type=F32)
        + jnp.dot(theirs, partner_factor, preferred_element_type=F32)
        for factor, partner_factor in (
            (output_weight, partner_weights),
            (down, partner_down),
        )
    ]
    parts = reduce_rows(jnp.concatenate([part.astype(BF16) for part in branch], axis=1), ranks)
    parts, head_line, head_ahead = lax.optimization_barrier((parts, head_line, head_ahead))
    head_opposite = turned(head_line, 1, 2)
    mine = settle(
        rank[None].astype(jnp.int32),
        hidden,
        adapter_up_weight,
        final_norm_gain[None, :],
        *parts,
    )
    size = tok_rows // ranks
    half = size // 2

    def score_blocks(places, blocks):
        return score(
            jnp.stack([rank, me // 8, me // 2 % 4, me % 2] + places).astype(jnp.int32),
            adapter_up_weight,
            final_norm_gain[None, :],
            targets[:, None],
            head_pieces,
            blocks,
        )

    def by_offset(offsets, part):
        part = part.reshape(8, 2, len(offsets), size)
        return {offset: part[:, :, n] for n, offset in enumerate(offsets)}

    def place(offset):
        return (rank + offset) % ranks

    after_one, before_one, line_swapped, first_swapped, third = lax.optimization_barrier(
        (
            shifted(mine, ranks, -1),
            shifted(mine, ranks, 1),
            crossed(head_line),
            crossed(head_ahead[0]),
            head_ahead[1],
        )
    )
    after_two, before_two, head_opposite, third_swapped = lax.optimization_barrier(
        (
            shifted(after_one, ranks, -1),
            shifted(before_one, ranks, 1),
            head_opposite,
            crossed(third),
        )
    )
    head_pieces = [head_line, head_ahead[0], head_opposite, head_ahead[1]]
    head_pieces += [line_swapped, first_swapped, crossed(head_opposite), third_swapped]
    blocks = [
        mine,
        after_one,
        before_one,
        after_two,
        before_two,
        shifted(after_two, ranks, -1),
        shifted(before_two, ranks, 1),
        shifted(after_two[:half], ranks, -2),
        shifted(before_two[half:], ranks, 2),
    ]
    offsets = (0, 1, ranks - 1, 2, ranks - 2, 3, ranks - 3)
    opposite = 2 * place(ranks // 2)
    part = score_blocks([place(n) for n in offsets] + [opposite, opposite + 1], blocks)
    stats = by_offset(offsets + (ranks // 2,), part)
    line = jnp.stack([stats[k] for k in range(ranks)] * 2, axis=2)
    ordered = lax.dynamic_slice_in_dim(line, ranks - rank, ranks, 2).reshape(8, 2 * tok_rows)
    every = lax.all_to_all(
        jnp.broadcast_to(ordered[None], (ranks, 8, 2 * tok_rows)), "tensor", 0, 0, tiled=True
    )
    maxima, totals, picked = every[:, 0], every[:, 1], every[:, 2]
    largest = jnp.max(maxima, axis=0)
    total = jnp.sum(totals * jnp.exp(maxima - largest[None]), axis=0)
    log_probs = jnp.sum(picked, axis=0) - largest - jnp.log(total)
    return (log_probs[:tok_rows], log_probs[tok_rows:])


def solution(mesh):
    return jax.shard_map(
        local,
        mesh=mesh,
        in_specs=(
            P("seq", None),
            P(),
            P(None, None, "tensor"),
            P("tensor", None),
            P("tensor", None),
            P(),
            P(),
            P("tensor", "seq"),
            P("seq", None, "tensor"),
            P("seq", None, "tensor"),
            P(),
            P(),
            P(),
            P("seq"),
        ),
        out_specs=(P("seq"), P("seq")),
        check_vma=False,
    )
```

```python
import math

import jax
import jax.numpy as jnp
from jax import lax
from jax.experimental import pallas as pl
from jax.experimental.pallas import tpu as pltpu
from jax.sharding import PartitionSpec as P

HEAD_WIDTH = 96
LEN = 64
PAGE = 128
MAXP = 8


EPSILON = 1e-05
NEGATIVE = -1e30
PAD = 128
BLOCK = LEN // 2
VMEM_LIMIT = 28 * 1024 * 1024
F32 = jnp.float32
BF16 = jnp.bfloat16


def rms_norm(values, gain):
    mean_sq = jnp.mean(values * values, axis=-1, keepdims=True)
    return (values * lax.rsqrt(mean_sq + EPSILON) * gain.astype(F32)).astype(BF16)


def project_kernel(hidden_ref, gain_ref, weight_ref, cos_ref, sin_ref, out_ref, normed):
    part = pl.program_id(0)

    @pl.when(part == 0)
    def _():
        normed[...] = rms_norm(hidden_ref[...].astype(F32), gain_ref[...])

    product = jnp.dot(normed[...], weight_ref[0], preferred_element_type=F32)

    @pl.when(part < 2)
    def _():
        width = product.shape[1]
        half = HEAD_WIDTH // 2
        lane = lax.broadcasted_iota(jnp.int32, product.shape, 1) % HEAD_WIDTH
        partner = jnp.where(
            lane < half, -pltpu.roll(product, width - half, 1), pltpu.roll(product, half, 1)
        )
        out_ref[0] = (product * cos_ref[...] + partner * sin_ref[...]).astype(BF16)

    @pl.when(part == 2)
    def _():
        out_ref[0] = product.astype(BF16)


def project(hidden, gain, weight, cosine, sinus):
    rows, width = hidden.shape
    parts, _, cols = weight.shape
    whole = lambda i: (0, 0)
    return pl.pallas_call(
        project_kernel,
        grid=(parts,),
        in_specs=[
            pl.BlockSpec((rows, width), whole),
            pl.BlockSpec((1, width), whole),
            pl.BlockSpec((1, width, cols), lambda i: (i, 0, 0)),
            pl.BlockSpec((rows, cols), whole),
            pl.BlockSpec((rows, cols), whole),
        ],
        out_specs=pl.BlockSpec((1, rows, cols), lambda i: (i, 0, 0)),
        out_shape=jax.ShapeDtypeStruct((parts, rows, cols), BF16),
        scratch_shapes=[pltpu.VMEM((rows, width), BF16)],
        compiler_params=pltpu.CompilerParams(vmem_limit_bytes=VMEM_LIMIT),
        name="project",
    )(hidden, gain, weight, cosine, sinus)


def dot_nt(left, right):
    return lax.dot_general(left, right, (((1,), (1,)), ((), ())), preferred_element_type=F32)


def attend_kernel(*refs):
    first_ref, counts_ref, index_ref, owner_ref = refs[:4]
    qkv_ref = refs[4]
    out_ref, keys, values, sems = refs[-4:]
    pieces = refs[5:-4]
    rollouts = keys.shape[0]
    width = qkv_ref.shape[2]
    heads = width // HEAD_WIDTH
    scale = 1.0 / math.sqrt(HEAD_WIDTH)
    first = first_ref[0]
    my_y, my_x, my_core = first_ref[1], first_ref[2], first_ref[3]

    def start_copies(r, j):
        slot = index_ref[owner_ref[first + r] * MAXP + j]
        device = slot // 2
        down_y = (device // 8 - my_y + 4) % 4
        down_x = (device // 2 % 4 - my_x + 4) % 4
        rows = pl.ds(pl.multiple_of(j * PAGE, PAGE), PAGE)
        for path, (buffer, far, near) in enumerate(
            ((keys, down_y, down_x), (values, down_x, down_y))
        ):
            at = near * 4 + 2 * (device % 2 != path).astype(jnp.int32) + slot % 2
            piece = far + 4 * (my_core != path).astype(jnp.int32)
            for p, ref in enumerate(pieces):

                @pl.when(piece == p)
                def _():
                    pltpu.make_async_copy(
                        ref.at[at], buffer.at[r, rows], sems.at[r, path, j]
                    ).start()

        return 0

    def live_pages(r):
        return counts_ref[owner_ref[first + r]]

    def covering(live):
        return jnp.where(live <= 2, 2, jnp.where(live <= 4, 4, MAXP))

    def start_rollout(r, _):
        return lax.fori_loop(0, covering(live_pages(r)), lambda j, _: start_copies(r, j), 0)

    lax.fori_loop(0, rollouts, start_rollout, 0)
    lane_head = lax.broadcasted_iota(jnp.int32, (LEN, width), 1) // HEAD_WIDTH
    own_row = lax.broadcasted_iota(jnp.int32, (heads * LEN, LEN), 0) % LEN
    own_col = lax.broadcasted_iota(jnp.int32, (heads * LEN, LEN), 1)

    def mix_rollout(r, _):
        live = live_pages(r)
        rows = pl.ds(pl.multiple_of(r * LEN, LEN), LEN)

        def mix(pages):
            query = qkv_ref[0, rows, :].astype(F32)
            stacked = jnp.concatenate(
                [jnp.where(lane_head == h, query, 0.0) for h in range(heads)], axis=0
            ).astype(BF16)
            own = dot_nt(stacked, qkv_ref[1, rows, :]) * scale
            own = jnp.where(own_col <= own_row, own, NEGATIVE)
            for j in range(pages):
                for which, buffer in enumerate((keys, values)):
                    pltpu.make_async_copy(
                        pieces[0].at[0],
                        buffer.at[r, pl.ds(j * PAGE, PAGE)],
                        sems.at[r, which, j],
                    ).wait()
            span = pl.ds(0, pages * PAGE)
            cached = dot_nt(stacked, keys[r, span]) * scale
            page_of = lax.broadcasted_iota(jnp.int32, cached.shape, 1) // PAGE
            cached = jnp.where(page_of < live, cached, NEGATIVE)
            largest = jnp.maximum(
                jnp.max(own, axis=1, keepdims=True), jnp.max(cached, axis=1, keepdims=True)
            )
            own = jnp.exp(own - largest)
            cached = jnp.exp(cached - largest)
            total = jnp.sum(own, axis=1, keepdims=True) + jnp.sum(cached, axis=1, keepdims=True)
            mixed = jnp.dot(
                cached.astype(BF16), values[r, span], preferred_element_type=F32
            ) + jnp.dot(own.astype(BF16), qkv_ref[2, rows, :], preferred_element_type=F32)
            mixed = mixed / total
            picked = jnp.zeros((LEN, width), F32)
            for h in range(heads):
                picked = jnp.where(lane_head == h, mixed[h * LEN : (h + 1) * LEN], picked)
            for parity in range(2):
                out_ref[parity, pl.ds(pl.multiple_of(r * BLOCK, BLOCK), BLOCK), :] = picked[
                    parity * BLOCK : (parity + 1) * BLOCK
                ].astype(BF16)

        for pages in (2, 4, MAXP):
            pl.when(covering(live) == pages)(lambda pages=pages: mix(pages))
        return 0

    lax.fori_loop(0, rollouts, mix_rollout, 0)


def attend(first, counts, index, owner, qkv, pieces):
    _, rows, width = qkv.shape
    rollouts = rows // LEN
    vmem = pl.BlockSpec(memory_space=pltpu.VMEM)
    pieces = [pltpu.with_memory_space_constraint(piece, pltpu.HBM) for piece in pieces]
    return pl.pallas_call(
        attend_kernel,
        grid_spec=pltpu.PrefetchScalarGridSpec(
            num_scalar_prefetch=4,
            grid=(),
            in_specs=[vmem] + [pl.BlockSpec(memory_space=pltpu.HBM)] * len(pieces),
            out_specs=vmem,
            scratch_shapes=[
                pltpu.VMEM((rollouts, MAXP * PAGE, width), BF16),
                pltpu.VMEM((rollouts, MAXP * PAGE, width), BF16),
                pltpu.SemaphoreType.DMA((rollouts, 2, MAXP)),
            ],
        ),
        out_shape=jax.ShapeDtypeStruct((2, rows // 2, width), BF16),
        compiler_params=pltpu.CompilerParams(vmem_limit_bytes=VMEM_LIMIT),
        name="attend",
    )(first, counts, index, owner, qkv, *pieces)


def two_parts(value):
    high = value.astype(BF16)
    return high, (value - high.astype(F32)).astype(BF16)


def settle_kernel(place_ref, hidden_ref, up_ref, gain_ref, *refs):
    *parts, out_ref = refs
    model = hidden_ref.shape[1]
    rank = up_ref.shape[0]
    total = parts[0][...].astype(F32)
    for part in parts[1:]:
        total = total + part[...].astype(F32)
    reference = hidden_ref[...].astype(F32) + total[:, :model]
    delta = total[:, model:]
    high, low = two_parts(delta)
    policy = (
        reference
        + jnp.dot(high[:, :rank], up_ref[...], preferred_element_type=F32)
        + jnp.dot(low[:, :rank], up_ref[...], preferred_element_type=F32)
    )
    reference_scale = lax.rsqrt(jnp.mean(reference * reference, axis=1, keepdims=True) + EPSILON)
    policy_scale = lax.rsqrt(jnp.mean(policy * policy, axis=1, keepdims=True) + EPSILON)
    out_ref[:, :model] = (reference * reference_scale * gain_ref[...].astype(F32)).astype(BF16)
    lane = lax.broadcasted_iota(jnp.int32, delta.shape, 1)
    beside = high.astype(F32) + pltpu.roll(low.astype(F32), rank, 1)
    at = 2 * rank
    for scale in (policy_scale / reference_scale, policy_scale):
        for _ in range(3):
            part = scale.astype(BF16).astype(F32)
            beside = jnp.where(lane == at, part, beside)
            scale = scale - part
            at += 1
    out_ref[:, model:] = beside.astype(BF16)


def settle(place, hidden, up, gain, *parts):
    whole = lambda i, p: (0, 0)
    size, width = parts[0].shape
    return pl.pallas_call(
        settle_kernel,
        grid_spec=pltpu.PrefetchScalarGridSpec(
            num_scalar_prefetch=1,
            grid=(1,),
            in_specs=[
                pl.BlockSpec((size, hidden.shape[1]), lambda i, p: (p[0], 0)),
                pl.BlockSpec(up.shape, whole),
                pl.BlockSpec(gain.shape, whole),
            ]
            + [pl.BlockSpec(part.shape, whole) for part in parts],
            out_specs=pl.BlockSpec((size, width), whole),
        ),
        out_shape=jax.ShapeDtypeStruct((size, width), BF16),
        compiler_params=pltpu.CompilerParams(vmem_limit_bytes=VMEM_LIMIT),
        name="settle",
    )(place, hidden, up, gain, *parts)


def score_kernel(*refs):
    place_ref, up_ref, gain_ref = refs[:3]
    pieces = refs[3:11]
    out_ref, normed, deltas, scales, wanted, largest, total, picked, head, sems = refs[-10:]
    inputs = refs[11:-10]
    rank, model = up_ref.shape
    rows = deltas.shape[0]
    vocab = head.shape[1]
    part_rows = pieces[0].shape[0] // 8
    spans = sems.shape[0]
    span = vocab // spans
    my_y, my_x, my_core = place_ref[1], place_ref[2], place_ref[3]

    for which in range(spans):
        columns = slice(which * span, (which + 1) * span)
        for p, piece in enumerate(pieces):
            path = my_core if p < 4 else 1 - my_core

            def start_part(n, _, piece=piece, far=p % 4, path=path, which=which, columns=columns):
                near = n // 2
                y = (my_y + jnp.where(path == 0, far, near)) % 4
                x = (my_x + jnp.where(path == 0, near, far)) % 4
                core = jnp.where(n % 2 == 0, path, 1 - path)
                row = (y * 8 + x * 2 + core) * 2 * part_rows + path * part_rows
                pltpu.make_async_copy(
                    piece.at[pl.ds(pl.multiple_of(n * part_rows, 16), part_rows), columns],
                    head.at[pl.ds(pl.multiple_of(row, 16), part_rows), columns],
                    sems.at[which],
                ).start()
                return 0

            lax.fori_loop(0, 8, start_part, 0)

    start = 0
    for target_ref, block in zip(inputs[::2], inputs[1::2]):
        at = slice(start, start + block.shape[0])
        start += block.shape[0]
        normed[at, :] = block[:, :model]
        beside = block[:, model:]
        deltas[at, :] = beside[:, : 2 * rank]
        beside = beside.astype(F32)
        lane = lax.broadcasted_iota(jnp.int32, beside.shape, 1) - 2 * rank
        for which in range(2):
            parts = (lane >= 3 * which) & (lane < 3 * which + 3)
            scales[which, at, :] = jnp.sum(jnp.where(parts, beside, 0.0), axis=1, keepdims=True)
        wanted[at, :] = target_ref[...] - place_ref[0] * vocab
    high, low = two_parts(up_ref[...].astype(F32) * gain_ref[...].astype(F32))
    normed[rows : rows + rank, :] = high
    normed[rows + rank :, :] = low
    largest[...] = jnp.full_like(largest, NEGATIVE)
    total[...] = jnp.zeros_like(total)
    picked[...] = jnp.zeros_like(picked)
    tile = 512

    def score_tile(n, _):
        product = jnp.dot(
            normed[...],
            head[:, pl.ds(pl.multiple_of(n * tile, tile), tile)],
            preferred_element_type=F32,
        )
        reference_logits = product[:rows]
        adapted = jnp.zeros_like(reference_logits)
        for part in two_parts(product[rows : rows + rank] + product[rows + rank :]):
            adapted += jnp.dot(
                deltas[...], jnp.concatenate([part, part], axis=0), preferred_element_type=F32
            )
        policy_logits = scales[0] * reference_logits + scales[1] * adapted
        columns = lax.broadcasted_iota(jnp.int32, reference_logits.shape, 1)
        hit = columns == wanted[...] - n * tile
        for which, logits in enumerate((policy_logits, reference_logits)):
            picked[which] += jnp.sum(jnp.where(hit, logits, 0.0), axis=1, keepdims=True)
            before = largest[which]
            after = jnp.maximum(before, jnp.max(logits, axis=1, keepdims=True))
            total[which] = total[which] * jnp.exp(before - after) + jnp.sum(
                jnp.exp(logits - after), axis=1, keepdims=True
            )
            largest[which] = after
        return 0

    def score_span(which, _):
        columns = pl.ds(pl.multiple_of(which * span, span), span)
        pltpu.make_async_copy(head.at[:, columns], head.at[:, columns], sems.at[which]).wait()
        per_span = span // tile
        return lax.fori_loop(which * per_span, (which + 1) * per_span, score_tile, 0)

    lax.fori_loop(0, spans, score_span, 0)
    lane = lax.broadcasted_iota(jnp.int32, (2, rows, 128), 2)
    packed = jnp.where(lane == 0, largest[...], jnp.where(lane == 1, total[...], picked[...]))
    out_ref[...] = jnp.transpose(packed.reshape(2 * rows, 128))[:8, :]


def score(place, up, gain, targets, pieces, blocks):
    rank, model = up.shape
    vocab = pieces[0].shape[1]
    rows = sum(block.shape[0] for block in blocks)
    whole = lambda i, p: (0, 0)
    pieces = [pltpu.with_memory_space_constraint(piece, pltpu.HBM) for piece in pieces]
    per_block, operands = [], []
    for k, block in enumerate(blocks):
        per_block += [
            pl.BlockSpec((block.shape[0], 1), lambda i, p, k=k: (p[4 + k], 0)),
            pl.BlockSpec(block.shape, whole),
        ]
        operands += [targets, block]
    column = pltpu.VMEM((2, rows, 1), F32)
    return pl.pallas_call(
        score_kernel,
        grid_spec=pltpu.PrefetchScalarGridSpec(
            num_scalar_prefetch=1,
            grid=(1,),
            in_specs=[pl.BlockSpec(up.shape, whole), pl.BlockSpec(gain.shape, whole)]
            + [pl.BlockSpec(memory_space=pltpu.HBM)] * len(pieces)
            + per_block,
            out_specs=pl.BlockSpec((8, 2 * rows), whole),
            scratch_shapes=[
                pltpu.VMEM((rows + 2 * rank, model), BF16),
                pltpu.VMEM((rows, 2 * rank), BF16),
                column,
                pltpu.VMEM((rows, 1), jnp.int32),
                column,
                column,
                column,
                pltpu.VMEM((model, vocab), BF16),
                pltpu.SemaphoreType.DMA((2,)),
            ],
        ),
        out_shape=jax.ShapeDtypeStruct((8, 2 * rows), F32),
        compiler_params=pltpu.CompilerParams(vmem_limit_bytes=VMEM_LIMIT),
        cost_estimate=pl.CostEstimate(
            flops=4 * rows * model * vocab,
            transcendentals=2 * rows * vocab,
            bytes_accessed=2 * model * vocab,
        ),
        name="score",
    )(place, up, gain, *pieces, *operands)


def shifted(value, ranks, step):
    return lax.ppermute(value, "tensor", [(i, (i + step) % ranks) for i in range(ranks)])


def partnered(value, ranks):
    return lax.ppermute(value, "tensor", [(i, i ^ 1) for i in range(ranks)])


def reduce_rows(branch, ranks):
    me = lax.axis_index("tensor")
    size = branch.shape[0] // (ranks // 2)

    def block(step):
        at = (me + step) % ranks // 2 * size
        return lax.dynamic_slice_in_dim(branch, at, size, 0)

    arrived = [shifted(block(step), ranks, step) for step in (ranks // 2, 2, ranks - 2)]
    return [block(0)] + arrived


def crossed(value):
    return lax.ppermute(value, "seq", [(i, i ^ 1) for i in range(32)])


def turned(value, stage, step):
    def target(i):
        y, x, core = i // 8, i // 2 % 4, i % 2
        if core == stage:
            x = (x + step) % 4
        else:
            y = (y + step) % 4
        return y * 8 + x * 2 + core

    return lax.ppermute(value, "seq", [(i, target(i)) for i in range(32)])


def start_pair(first, second):
    first_core = lax.axis_index("seq") % 2 == 0
    kept = jnp.where(first_core, first, second)
    sent = jnp.where(first_core, second, first)
    return jnp.concatenate([kept, crossed(sent)])


def along_first(pair):
    return [pair] + [turned(pair, 0, step) for step in (3, 2, 1)]


def local(
    hidden,
    attention_norm_gain,
    query_key_value_weight,
    output_weight,
    adapter_down_weight,
    adapter_up_weight,
    final_norm_gain,
    head,
    prompt_key_slots,
    prompt_value_slots,
    counts,
    page_slot_index,
    owner,
    targets,
):
    tok_rows, model = hidden.shape
    rollouts_here = tok_rows // LEN
    width_here = output_weight.shape[0]
    heads_here = width_here // HEAD_WIDTH
    ranks = lax.axis_size("tensor")
    first = lax.axis_index("seq") * rollouts_here
    me = lax.axis_index("seq")
    rank = lax.axis_index("tensor")
    down = jnp.pad(adapter_down_weight, ((0, 0), (0, PAD - adapter_down_weight.shape[1])))
    groups_iota = jnp.arange(counts.shape[0], dtype=jnp.int32)
    my_groups = lax.dynamic_slice_in_dim(owner, first, rollouts_here, 0)
    my_pages = jnp.sum(
        jnp.where(my_groups[:, None] == groups_iota[None, :], counts[None, :], 0), axis=1
    )
    positions = jnp.repeat(my_pages, LEN) * PAGE + jnp.arange(tok_rows, dtype=jnp.int32) % LEN
    half = HEAD_WIDTH // 2
    place_in_head = jnp.arange(width_here, dtype=jnp.int32) % half
    frequency = 10000.0 ** (-place_in_head.astype(F32) * 2.0 / HEAD_WIDTH)
    angles = positions.astype(F32)[:, None] * frequency[None, :]
    pair = start_pair(prompt_key_slots, prompt_value_slots)
    partner_weights = partnered(output_weight, ranks)
    partner_down = partnered(down, ranks)
    line = lax.optimization_barrier(along_first(pair))
    line = lax.optimization_barrier(jnp.concatenate(line))
    ahead = [turned(line, 1, step) for step in (3, 2, 1)]
    near = crossed(line)
    qkv = project(
        hidden,
        attention_norm_gain[None, :],
        query_key_value_weight,
        jnp.cos(angles),
        jnp.sin(angles),
    )
    half = head.shape[1] // 2
    head_pair = start_pair(head.T[:half], head.T[half:])
    ahead, near, qkv, head_pair, partner_weights = lax.optimization_barrier(
        (ahead, near, qkv, head_pair, partner_weights)
    )
    pieces = [line] + ahead + [near] + [crossed(piece) for piece in ahead]
    head_line = along_first(head_pair)
    attended = attend(
        jnp.stack([first, me // 8, me // 2 % 4, me % 2]).astype(jnp.int32),
        counts,
        page_slot_index,
        owner,
        qkv,
        pieces,
    )
    theirs = partnered(lax.dynamic_index_in_dim(attended, 1 - rank % 2, 0, False), ranks)
    attended, head_line, partner_down = lax.optimization_barrier(
        (attended, head_line, partner_down)
    )
    own = lax.dynamic_index_in_dim(attended, rank % 2, 0, False)
    head_line = lax.optimization_barrier(jnp.concatenate(head_line))
    head_ahead = [turned(head_line, 1, 3), turned(head_line, 1, 1)]
    branch = [
        jnp.dot(own, factor, preferred_element_type=F32)
        + jnp.dot(theirs, partner_factor, preferred_element_type=F32)
        for factor, partner_factor in (
            (output_weight, partner_weights),
            (down, partner_down),
        )
    ]
    parts = reduce_rows(jnp.concatenate([part.astype(BF16) for part in branch], axis=1), ranks)
    parts, head_line, head_ahead = lax.optimization_barrier((parts, head_line, head_ahead))
    head_opposite = turned(head_line, 1, 2)
    mine = settle(
        rank[None].astype(jnp.int32),
        hidden,
        adapter_up_weight,
        final_norm_gain[None, :],
        *parts,
    )
    size = tok_rows // ranks
    half = size // 2

    def score_blocks(places, blocks):
        return score(
            jnp.stack([rank, me // 8, me // 2 % 4, me % 2] + places).astype(jnp.int32),
            adapter_up_weight,
            final_norm_gain[None, :],
            targets[:, None],
            head_pieces,
            blocks,
        )

    def by_offset(offsets, part):
        part = part.reshape(8, 2, len(offsets), size)
        return {offset: part[:, :, n] for n, offset in enumerate(offsets)}

    def place(offset):
        return (rank + offset) % ranks

    after_one, before_one, line_swapped, first_swapped, third = lax.optimization_barrier(
        (
            shifted(mine, ranks, -1),
            shifted(mine, ranks, 1),
            crossed(head_line),
            crossed(head_ahead[0]),
            head_ahead[1],
        )
    )
    after_two, before_two, head_opposite, third_swapped = lax.optimization_barrier(
        (
            shifted(after_one, ranks, -1),
            shifted(before_one, ranks, 1),
            head_opposite,
            crossed(third),
        )
    )
    head_pieces = [head_line, head_ahead[0], head_opposite, head_ahead[1]]
    head_pieces += [line_swapped, first_swapped, crossed(head_opposite), third_swapped]
    blocks = [
        mine,
        after_one,
        before_one,
        after_two,
        before_two,
        shifted(after_two, ranks, -1),
        shifted(before_two, ranks, 1),
        shifted(after_two[:half], ranks, -2),
        shifted(before_two[half:], ranks, 2),
    ]
    offsets = (0, 1, ranks - 1, 2, ranks - 2, 3, ranks - 3)
    opposite = 2 * place(ranks // 2)
    part = score_blocks([place(n) for n in offsets] + [opposite, opposite + 1], blocks)
    stats = by_offset(offsets + (ranks // 2,), part)
    line = jnp.stack([stats[k] for k in range(ranks)] * 2, axis=2)
    ordered = lax.dynamic_slice_in_dim(line, ranks - rank, ranks, 2).reshape(8, 2 * tok_rows)
    every = lax.all_to_all(
        jnp.broadcast_to(ordered[None], (ranks, 8, 2 * tok_rows)), "tensor", 0, 0, tiled=True
    )
    maxima, totals, picked = every[:, 0], every[:, 1], every[:, 2]
    largest = jnp.max(maxima, axis=0)
    total = jnp.sum(totals * jnp.exp(maxima - largest[None]), axis=0)
    log_probs = jnp.sum(picked, axis=0) - largest - jnp.log(total)
    return (log_probs[:tok_rows], log_probs[tok_rows:])


def solution(mesh):
    return jax.shard_map(
        local,
        mesh=mesh,
        in_specs=(
            P("seq", None),
            P(),
            P(None, None, "tensor"),
            P("tensor", None),
            P("tensor", None),
            P(),
            P(),
            P("tensor", "seq"),
            P("seq", None, "tensor"),
            P("seq", None, "tensor"),
            P(),
            P(),
            P(),
            P("seq"),
        ),
        out_specs=(P("seq"), P("seq")),
        check_vma=False,
    )
```
